32 devices in a mesh: dp: 32 (over z, y, x, core).
Axes of the slice: x: 2, y: 2, z: 4, core: 2. Of those that a mesh axis runs over, the one named last changes fastest.
Arguments:
- tokens: bfloat16 [32768, 1024], P('dp'), may hold values from -6 to 6
- cotangent: bfloat16 [32768, 1024], P('dp'), may hold values from -6 to 6
- lengths: int32 [256], replicated, may hold values from 0 to 512, as said below
- dealing: int32 [256], replicated, may hold values from 0 to 255, as said below
- query_weight: bfloat16 [1024, 1024], P('dp'), may hold values from -0.1875 to 0.1875
- key_weight: bfloat16 [1024, 1024], P('dp'), may hold values from -0.1875 to 0.1875
- value_weight: bfloat16 [1024, 1024], P('dp'), may hold values from -0.1875 to 0.1875
- out_weight: bfloat16 [1024, 1024], P('dp'), may hold values from -1.5 to 1.5
- up_weight: bfloat16 [1024, 4096], P('dp'), may hold values from -0.1875 to 0.1875
- down_weight: bfloat16 [4096, 1024], P('dp'), may hold values from -0.09375 to 0.09375
- query_bias: bfloat16 [1024], P('dp'), may hold values from -3 to 3
- value_bias: bfloat16 [1024], P('dp'), may hold values from -0.3125 to 0.3125
- out_bias: bfloat16 [1024], P('dp'), may hold values from -0.625 to 0.625
- up_bias: bfloat16 [4096], P('dp'), may hold values from -3 to 3
- down_bias: bfloat16 [1024], P('dp'), may hold values from -0.625 to 0.625
- first_gain: bfloat16 [1024], P('dp'), may hold values from 0.5 to 1.5
- first_shift: bfloat16 [1024], P('dp'), may hold values from -1.75 to 1.75
- second_gain: bfloat16 [1024], P('dp'), may hold values from 0.5 to 1.5
- second_shift: bfloat16 [1024], P('dp'), may hold values from -1.75 to 1.75
Outputs:
- layer_out: bfloat16 [32768, 1024], P('dp')
- token_gradient: bfloat16 [32768, 1024], P('dp')
- query_weight_gradient: float32 [1024, 1024], P('dp')
- key_weight_gradient: float32 [1024, 1024], P('dp')
- value_weight_gradient: float32 [1024, 1024], P('dp')
- out_weight_gradient: float32 [1024, 1024], P('dp')
- up_weight_gradient: float32 [1024, 4096], P('dp')
- down_weight_gradient: float32 [4096, 1024], P('dp')
- query_bias_gradient: float32 [1024], P('dp')
- value_bias_gradient: float32 [1024], P('dp')
- out_bias_gradient: float32 [1024], P('dp')
- up_bias_gradient: float32 [4096], P('dp')
- down_bias_gradient: float32 [1024], P('dp')
- first_gain_gradient: float32 [1024], P('dp')
- first_shift_gradient: float32 [1024], P('dp')
- second_gain_gradient: float32 [1024], P('dp')
- second_shift_gradient: float32 [1024], P('dp')
The draws below stay inside these ranges and needn't reach their ends.
Inputs may be any that keep to these rules, and one draw needn't show every extreme that they name: Every length is a multiple of 128; a length of 0 marks an empty place. The lengths sum to 32768. A permutation of the 256 places: sequence s goes to device dealing[s] // 8, to place dealing[s] % 8 of that device's ordered places. Taken in order, each device's places form 2 groups of 4 places whose lengths sum to 512.
All inputs are finite; a program needn't handle non-finite values.
Results may differ from the reference program's by a relative error of at most 0.014.
Values may be sent and summed in bfloat16 or wider, within the bound.
A program may use at most 256 MiB of HBM per device.

```python
import jax
import jax.numpy as jnp
from jax import lax

D = 1024
FF = 4096
H = 16
HD = 64
MB_TOK = 512
QUANT = 128
MAXLEN = 512
SEQ_DEV = 8
NSEQ = 256
TOKENS = 32768


def swap_into(order, position, wanted):
    found = jnp.argmax(order == wanted).astype(jnp.int32)
    current = order[position]
    order = order.at[found].set(current)
    return order.at[position].set(wanted)


def dealt_plan(key):
    quanta = MB_TOK // QUANT
    run_cap = max(MAXLEN // QUANT, 1)
    micro_total = NSEQ // quanta
    break_key = jax.random.fold_in(key, 101)
    pick_key = jax.random.fold_in(key, 202)
    permute_key = jax.random.fold_in(key, 303)
    gap_index = jnp.arange(quanta, dtype=jnp.int32)
    random_breaks = jax.random.randint(break_key, (micro_total, quanta), 0, 2).astype(jnp.int32)
    forced = ((gap_index + 1) % run_cap == 0).astype(jnp.int32)
    chosen = jax.random.randint(pick_key, (), 0, micro_total).astype(jnp.int32)
    micro_ids = jnp.arange(micro_total, dtype=jnp.int32)
    breaks = jnp.where(micro_ids[:, None] == chosen, forced[None, :], jnp.maximum(random_breaks, forced[None, :]))
    breaks = jnp.where(gap_index[None, :] < quanta - 1, breaks, 0).astype(jnp.int32)
    run_index = (jnp.cumsum(breaks, axis=1) - breaks).astype(jnp.int32)
    counts = jnp.sum((run_index[:, :, None] == gap_index[None, None, :]).astype(jnp.int32), axis=1)
    dealt_lengths = (counts * QUANT).astype(jnp.int32).reshape(NSEQ)
    permuted = jax.random.permutation(permute_key, NSEQ).astype(jnp.int32)
    last_device_place = jnp.asarray(NSEQ - SEQ_DEV, jnp.int32)
    permuted = swap_into(permuted, 0, last_device_place)
    permuted = swap_into(permuted, NSEQ - 1, jnp.asarray(0, jnp.int32))
    return (dealt_lengths, permuted)


def draw_lengths(key, part):
    dealt_lengths, permuted = dealt_plan(key)
    return dealt_lengths[permuted]


def draw_dealing(key, part):
    dealt_lengths, permuted = dealt_plan(key)
    return permuted


def strengthened(drawn, key, source, target, parts, factor):
    def block_of(dim):
        return (jnp.arange(drawn.shape[dim]) // (drawn.shape[dim] // parts)).reshape((-1,) + (1,) * (drawn.ndim - 1 - dim))

    first = jax.random.permutation(key, parts)[block_of(target)]
    far = (block_of(target) + parts // 2) % parts
    return jnp.where((block_of(source) == first) | (block_of(source) == far), factor * drawn, drawn)


def steps_of(stream_key, shape, split, smallest, high):
    gain = 1.0
    for dim, blocks in split:
        draws = jax.random.uniform(jax.random.fold_in(jax.random.fold_in(stream_key, 6), dim), (blocks,), jnp.float32, smallest / len(split), high / len(split))
        gain = gain * jnp.repeat(jnp.exp(draws), shape[dim] // blocks).reshape((-1,) + (1,) * (len(shape) - 1 - dim))
    return gain


def centred(key, shape, scale, reach, cuts=(), held_as=jnp.bfloat16):
    drawn = jax.random.normal(key, shape, jnp.float32) * scale
    if len(cuts) > 0:
        drawn = steps_of(key, shape, cuts, -0.22, 0.18) * drawn
    return jnp.clip(drawn, min=-reach, max=reach).astype(held_as)


def noise_with(key, dims, spread, most, split, heavy, kind=jnp.bfloat16):
    values = spread * jax.random.normal(key, dims, jnp.float32)
    if split:
        values = values * steps_of(key, dims, split, -0.22, 0.18)
    return jnp.clip(strengthened(values, jax.random.fold_in(key, 3), *heavy), -most, most).astype(kind)


def setup_inputs(seed: int = 0) -> dict:
    keys = jax.random.split(jax.random.key(seed), 20)
    return {
        "tokens": centred(keys[0], (TOKENS, D), 1.0, 6.0, ((0, 32),)),
        "cotangent": noise_with(keys[1], (TOKENS, D), 1.0, 6.0, ((0, 32),), (0, 1, 32, 2.75)),
        "lengths": draw_lengths(jax.random.fold_in(keys[19], 71), 0),
        "dealing": draw_dealing(jax.random.fold_in(keys[19], 71), 0),
        "query_weight": centred(keys[4], (D, D), D ** -0.5, 0.1875, ((0, 32),)),
        "key_weight": centred(keys[5], (D, D), D ** -0.5, 0.1875, ((0, 32),)),
        "value_weight": centred(keys[6], (D, D), D ** -0.5, 0.1875, ((0, 32),)),
        "out_weight": centred(keys[7], (D, D), (D // 64) ** -0.5, 1.5, ((0, 32),)),
        "up_weight": centred(keys[8], (D, FF), D ** -0.5, 0.1875, ((0, 32),)),
        "down_weight": centred(keys[9], (FF, D), FF ** -0.5, 0.09375, ((0, 32),)),
        "query_bias": centred(keys[10], (D,), 0.5, 3.0, ((0, 32),)),
        "value_bias": centred(keys[11], (D,), 0.05, 0.3125, ((0, 32),)),
        "out_bias": centred(keys[12], (D,), 0.1, 0.625, ((0, 32),)),
        "up_bias": centred(keys[13], (FF,), 0.5, 3.0, ((0, 32),)),
        "down_bias": centred(keys[14], (D,), 0.1, 0.625, ((0, 32),)),
        "first_gain": jnp.clip(1.0 + 0.1 * jax.random.normal(keys[15], (D,), jnp.float32), 0.5, 1.5).astype(jnp.bfloat16),
        "first_shift": centred(keys[16], (D,), 0.3, 1.75, ((0, 32),)),
        "second_gain": jnp.clip(1.0 + 0.1 * jax.random.normal(keys[17], (D,), jnp.float32), 0.5, 1.5).astype(jnp.bfloat16),
        "second_shift": centred(keys[18], (D,), 0.3, 1.75, ((0, 32),)),
    }


norm_epsilon = 1e-12
masked_score = -1000000000.0

@jax.custom_vjp
def low(v):
    return lax.optimization_barrier(v.astype(jnp.bfloat16)).astype(jnp.float32)

@jax.custom_vjp
def low_back(v):
    return v

def low_keep(v):
    return (low(v), None)

def low_pass(kept, grad):
    return (grad,)

def back_keep(v):
    return (v, None)

def back_low(kept, grad):
    return (low(grad),)
low.defvjp(low_keep, low_pass)
low_back.defvjp(back_keep, back_low)

def matmul(left_side, right_side):
    return jnp.dot(left_side, right_side, precision=lax.Precision.HIGHEST)

def layer_norm(values, norm_gain, norm_shift):
    centered = values - lax.optimization_barrier(jnp.mean(values, axis=-1, keepdims=True))
    variance = lax.optimization_barrier(jnp.mean(centered * centered, axis=-1, keepdims=True))
    return centered * lax.rsqrt(variance + norm_epsilon) * norm_gain + norm_shift

def block_layer(param_list, block_tokens, block_segments):
    query_weight, key_weight, value_weight, out_weight, up_weight, down_weight, query_bias, value_bias, out_bias, up_bias, down_bias, first_gain, first_shift, second_gain, second_shift = param_list
    queries = low(low_back(matmul(block_tokens, query_weight) + query_bias)).reshape(MB_TOK, H, HD)
    key_heads = low(low_back(matmul(block_tokens, key_weight))).reshape(MB_TOK, H, HD)
    value_heads = low(low_back(matmul(block_tokens, value_weight) + value_bias)).reshape(MB_TOK, H, HD)
    scores = low_back(jnp.einsum('qhd,khd->hqk', queries, key_heads, precision=lax.Precision.HIGHEST) * HD ** (-0.5))
    same_doc = block_segments[:, None] == block_segments[None, :]
    scores = jnp.where(same_doc[None], scores, masked_score)
    row_max = lax.optimization_barrier(jnp.max(scores, axis=-1, keepdims=True))
    expanded = jnp.exp(scores - row_max)
    attention = low(expanded / lax.optimization_barrier(jnp.sum(expanded, axis=-1, keepdims=True)))
    context = low(low_back(jnp.einsum('hqk,khd->qhd', attention, value_heads, precision=lax.Precision.HIGHEST).reshape(MB_TOK, D)))
    attended = low_back(matmul(context, out_weight) + out_bias)
    first_norm = layer_norm(block_tokens + attended, first_gain, first_shift)
    up_values = low_back(matmul(low(first_norm), up_weight) + up_bias)
    hidden = low(jax.nn.gelu(up_values, approximate=False))
    down_values = low_back(matmul(hidden, down_weight) + down_bias)
    return layer_norm(first_norm + down_values, second_gain, second_shift)

def reference(tokens, cotangent, lengths, dealing, query_weight, key_weight, value_weight, out_weight, up_weight, down_weight, query_bias, value_bias, out_bias, up_bias, down_bias, first_gain, first_shift, second_gain, second_shift):
    positions = jnp.arange(TOKENS, dtype=jnp.int32)
    starts = (jnp.cumsum(lengths) - lengths).astype(jnp.int32)
    dealt_lengths = jnp.zeros_like(lengths).at[dealing].set(lengths)
    dealt_starts = (jnp.cumsum(dealt_lengths) - dealt_lengths).astype(jnp.int32)
    owner_seq = (jnp.searchsorted(starts, positions, side='right') - 1).astype(jnp.int32)
    placement = (dealt_starts[dealing[owner_seq]] + positions - starts[owner_seq]).astype(jnp.int32)
    source = jnp.zeros_like(positions).at[placement].set(positions)
    dealt_owner = (jnp.searchsorted(dealt_starts, positions, side='right') - 1).astype(jnp.int32)
    block_count = TOKENS // MB_TOK
    dealt_tokens = tokens.astype(jnp.float32)[source].reshape(block_count, MB_TOK, D)
    dealt_cotangent = cotangent.astype(jnp.float32)[source].reshape(block_count, MB_TOK, D)
    segments = dealt_owner.reshape(block_count, MB_TOK)
    params = tuple((weight_item.astype(jnp.float32) for weight_item in (query_weight, key_weight, value_weight, out_weight, up_weight, down_weight, query_bias, value_bias, out_bias, up_bias, down_bias, first_gain, first_shift, second_gain, second_shift)))

    def forward(param_list, block_tokens):

        def block_step(carry_in, pieces):
            return (carry_in, jax.checkpoint(block_layer)(param_list, pieces[0], pieces[1]))
        carry_out, outputs = lax.scan(block_step, jnp.zeros((), jnp.float32), (block_tokens, segments))
        return outputs
    result, pullback = jax.vjp(forward, params, dealt_tokens)
    param_grads, token_grads = pullback(dealt_cotangent)
    query_weight_gradient, key_weight_gradient, value_weight_gradient, out_weight_gradient, up_weight_gradient, down_weight_gradient, query_bias_gradient, value_bias_gradient, out_bias_gradient, up_bias_gradient, down_bias_gradient, first_gain_gradient, first_shift_gradient, second_gain_gradient, second_shift_gradient = param_grads
    layer_out = result.reshape(TOKENS, D)[placement].astype(jnp.bfloat16)
    token_gradient = token_grads.reshape(TOKENS, D)[placement].astype(jnp.bfloat16)
    return (layer_out, token_gradient, query_weight_gradient, key_weight_gradient, value_weight_gradient, out_weight_gradient, up_weight_gradient, down_weight_gradient, query_bias_gradient, value_bias_gradient, out_bias_gradient, up_bias_gradient, down_bias_gradient, first_gain_gradient, first_shift_gradient, second_gain_gradient, second_shift_gradient)
```

```python
import functools

import jax
import jax.numpy as jnp
from jax import lax
from jax.experimental import pallas as pl
from jax.experimental.pallas import tpu as pltpu
from jax.sharding import PartitionSpec as P

HD = 64
GRAN = 128
HALO = 384
EPS = 1e-12
F32 = jnp.float32
BF16 = jnp.bfloat16
NT = (((1,), (1,)), ((), ()))
ANY = pl.BlockSpec(memory_space=pl.ANY)


def params(limit=56):
    return pltpu.CompilerParams(vmem_limit_bytes=limit << 20)


def whole(shape):
    return pl.BlockSpec(shape, lambda *_: (0,) * len(shape))


def dot(a, b):
    return jnp.dot(a, b, preferred_element_type=F32)


def dot_nt(a, b):
    return lax.dot_general(a, b, NT, preferred_element_type=F32)


def cost(flops, nbytes, trans=0):
    return pl.CostEstimate(flops=flops, bytes_accessed=nbytes, transcendentals=trans)


def qkv_kernel(xl, xo, xr, wq, wk, wv, vec, q, k, v):
    rows = xo.shape[0]
    for w, out, b in ((wq, q, vec[0:1, :]), (wk, k, None), (wv, v, vec[1:2, :])):
        def put(x, start, size):
            r = dot(x, w[...])
            if b is not None:
                r = r + b
            out[pl.ds(start, size), :] = r.astype(BF16)

        put(xl[...], 0, HALO)
        put(xr[...], HALO + rows, HALO)

        def step(i, c):
            s = pl.multiple_of(i * 256, 256)
            put(xo[pl.ds(s, 256), :], pl.multiple_of(HALO + s, 128), 256)
            return c

        lax.fori_loop(0, rows // 256, step, 0)


def qkv_call(xl, xo, xr, wq, wk, wv, vec):
    rows, d = xo.shape
    win = rows + 2 * HALO
    tn = 512
    wspec = pl.BlockSpec((d, tn), lambda j: (0, j))
    ospec = pl.BlockSpec((win, tn), lambda j: (0, j))
    out = jax.ShapeDtypeStruct((win, d), BF16)
    return pl.pallas_call(
        qkv_kernel,
        grid=(d // tn,),
        in_specs=[whole(xl.shape), whole(xo.shape), whole(xr.shape), wspec, wspec, wspec,
                  pl.BlockSpec((8, tn), lambda j: (0, j))],
        out_specs=[ospec] * 3,
        out_shape=[out] * 3,
        compiler_params=params(),
        cost_estimate=cost(6 * win * d * d, 2 * (4 * win * d + 3 * d * d)),
        name="qkv",
    )(xl, xo, xr, wq, wk, wv, vec)


def probs_t(k, qh):
    st = dot_nt(k, qh)
    e = jnp.exp(st - jnp.max(st, axis=0, keepdims=True))
    return e * (1.0 / jnp.sum(e, axis=0, keepdims=True))


def attn_fwd_kernel(tab, q_ref, k_ref, v_ref, o_ref, ctx):
    blocks = o_ref.shape[0] // GRAN

    def one(b, c):
        n = tab[1, b]
        s0 = tab[0, b]
        for nn in range(1, 5):
            @pl.when(n == nn)
            def _():
                size = nn * GRAN
                rows = pl.ds(pl.multiple_of(s0 * GRAN, GRAN), size)
                q = q_ref[rows, :] * jnp.asarray(0.125, BF16)
                k = k_ref[rows, :]
                vt = v_ref[rows, :].T
                low = lax.broadcasted_iota(jnp.int32, q.shape, 1) < HD
                parts = []
                for h in range(2):
                    qh = jnp.where(low if h == 0 else ~low, q, jnp.zeros_like(q))
                    p = probs_t(k, qh).astype(BF16)
                    parts.append(dot(vt[h * HD:(h + 1) * HD, :], p))
                ctx[rows, :] = jnp.concatenate(parts, axis=0).T.astype(BF16)
        return c

    lax.fori_loop(0, blocks, one, 0)
    o_ref[...] = ctx[pl.ds(HALO, o_ref.shape[0]), :]


def attn_fwd_call(tab, q, k, v, rows):
    win, d = q.shape
    spec = pl.BlockSpec((win, 2 * HD), lambda h, t: (0, h))
    return pl.pallas_call(
        attn_fwd_kernel,
        grid_spec=pltpu.PrefetchScalarGridSpec(
            num_scalar_prefetch=1,
            grid=(d // (2 * HD),),
            in_specs=[spec] * 3,
            out_specs=pl.BlockSpec((rows, 2 * HD), lambda h, t: (0, h)),
            scratch_shapes=[pltpu.VMEM((win, 2 * HD), BF16)],
        ),
        out_shape=jax.ShapeDtypeStruct((rows, d), BF16),
        compiler_params=params(),
        cost_estimate=cost(8 * rows * 512 * d, 8 * win * d, rows * 512 * 16),
        name="attn_fwd",
    )(tab, q, k, v)


def attn_bwd_kernel(tab, q_ref, k_ref, v_ref, gl, go, gr, dq_o, dk_o, dv_o, g_s, dq_s, dk_s, dv_s):
    rows_own = go.shape[0]
    blocks = rows_own // GRAN
    g_s[pl.ds(0, HALO), :] = gl[...]
    g_s[pl.ds(HALO, rows_own), :] = go[...]
    g_s[pl.ds(HALO + rows_own, HALO), :] = gr[...]

    def one(b, c):
        n = tab[1, b]
        s0 = tab[0, b]
        for nn in range(1, 5):
            @pl.when(n == nn)
            def _():
                size = nn * GRAN
                rows = pl.ds(pl.multiple_of(s0 * GRAN, GRAN), size)
                q = q_ref[rows, :] * jnp.asarray(0.125, BF16)
                k = k_ref[rows, :]
                v = v_ref[rows, :]
                g = g_s[rows, :]
                kt = (k * jnp.asarray(0.125, BF16)).T
                low = lax.broadcasted_iota(jnp.int32, q.shape, 1) < HD
                zero = jnp.zeros_like(q)
                dqs, dks, dvs = [], [], []
                for h in range(2):
                    mine = low if h == 0 else ~low
                    p = probs_t(k, jnp.where(mine, q, zero))
                    dp = dot_nt(v, jnp.where(mine, g, zero))
                    delta = jnp.sum(p * dp, axis=0, keepdims=True)
                    ds = (p * (dp - delta)).astype(BF16)
                    dvs.append(dot(p.astype(BF16), g))
                    dks.append(dot(ds, q))
                    dqs.append(dot(kt[h * HD:(h + 1) * HD, :], ds))
                dq_s[rows, :] = jnp.concatenate(dqs, axis=0).T.astype(BF16)
                dk_s[rows, :] = jnp.where(low, dks[0], dks[1]).astype(BF16)
                dv_s[rows, :] = jnp.where(low, dvs[0], dvs[1]).astype(BF16)
        return c

    lax.fori_loop(0, blocks, one, 0)
    own = pl.ds(HALO, rows_own)
    dq_o[...] = dq_s[own, :]
    dk_o[...] = dk_s[own, :]
    dv_o[...] = dv_s[own, :]


def attn_bwd_call(tab, q, k, v, gl, go, gr):
    win, d = q.shape
    rows = go.shape[0]
    spec = pl.BlockSpec((win, 2 * HD), lambda h, t: (0, h))
    own = pl.BlockSpec((rows, 2 * HD), lambda h, t: (0, h))
    halo = pl.BlockSpec((HALO, 2 * HD), lambda h, t: (0, h))
    out = jax.ShapeDtypeStruct((rows, d), BF16)
    return pl.pallas_call(
        attn_bwd_kernel,
        grid_spec=pltpu.PrefetchScalarGridSpec(
            num_scalar_prefetch=1,
            grid=(d // (2 * HD),),
            in_specs=[spec] * 3 + [halo, own, halo],
            out_specs=[own] * 3,
            scratch_shapes=[pltpu.VMEM((win, 2 * HD), BF16)] * 4,
        ),
        out_shape=[out] * 3,
        compiler_params=params(),
        cost_estimate=cost(20 * rows * 512 * d, 14 * win * d, rows * 512 * 16),
        name="attn_bwd",
    )(tab, q, k, v, gl, go, gr)


def norm_stats(z):
    cen = z - jnp.mean(z, axis=-1, keepdims=True)
    r = lax.rsqrt(jnp.mean(cen * cen, axis=-1, keepdims=True) + EPS)
    return cen * r, r


def norm_back(e, n, r):
    return r * (e - jnp.mean(e, axis=-1, keepdims=True) - n * jnp.mean(e * n, axis=-1, keepdims=True))


def out_proj_kernel(ctx, w, x, vec, xhat, low, r_o):
    z = x[...].astype(F32) + (dot(ctx[...], w[...]) + vec[2:3, :])
    n, r = norm_stats(z)
    xhat[...] = n
    r_o[...] = jnp.broadcast_to(r, r_o.shape)
    low[...] = (n * vec[4:5, :] + vec[5:6, :]).astype(BF16)


def out_proj_call(ctx, w, x, vec):
    rows, d = x.shape
    tm = 256
    t = pl.BlockSpec((tm, d), lambda i: (i, 0))
    return pl.pallas_call(
        out_proj_kernel,
        grid=(rows // tm,),
        in_specs=[t, whole(w.shape), t, whole(vec.shape)],
        out_specs=[t, t, pl.BlockSpec((tm, 128), lambda i: (i, 0))],
        out_shape=[jax.ShapeDtypeStruct((rows, d), F32), jax.ShapeDtypeStruct((rows, d), BF16),
                   jax.ShapeDtypeStruct((rows, 128), F32)],
        compiler_params=params(),
        cost_estimate=cost(2 * rows * d * d, rows * d * 10 + 2 * d * d),
        name="out_proj",
    )(ctx, w, x, vec)


RC = 256


def chunks(rows, fn):
    def step(i, c):
        fn(pl.ds(pl.multiple_of(i * RC, RC), RC))
        return c

    lax.fori_loop(0, rows // RC, step, 0)


def ffn_fwd_kernel(low, wu, bu, wd, xhat, g, vec, hid, dg, out, gs, sums, acc):
    rows = low.shape[0]
    t = pl.program_id(0)

    @pl.when(t == 0)
    def _():
        acc[...] = jnp.zeros_like(acc)

    def up(r):
        u = dot(low[r, :], wu[...]) + bu[...]
        phi = 0.5 * (1.0 + lax.erf(u * (0.5 ** 0.5)))
        h = (u * phi).astype(BF16)
        hid[r, :] = h
        dg[r, :] = (phi + u * (0.3989422804014327 * jnp.exp(-0.5 * u * u))).astype(BF16)
        acc[r, :] += dot(h, wd[...])

    chunks(rows, up)

    @pl.when(t == pl.num_programs(0) - 1)
    def _():
        sums[...] = jnp.zeros_like(sums)

        def fin(r):
            z = (xhat[r, :] * vec[4:5, :] + vec[5:6, :]) + (acc[r, :] + vec[3:4, :])
            n, rr = norm_stats(z)
            out[r, :] = (n * vec[6:7, :] + vec[7:8, :]).astype(BF16)
            gv = g[r, :].astype(F32)
            sums[0:1, :] += jnp.sum(gv * n, axis=0, keepdims=True)
            sums[1:2, :] += jnp.sum(gv, axis=0, keepdims=True)
            grad = norm_back(gv * vec[6:7, :], n, rr)
            gs[r, :] = grad
            sums[2:3, :] += jnp.sum(grad.astype(BF16).astype(F32), axis=0, keepdims=True)

        chunks(rows, fin)


def ffn_fwd_call(low, wu, bu, wd, xhat, g, vec):
    rows, d = low.shape
    ff = wu.shape[1]
    tf = 512
    col = pl.BlockSpec((rows, tf), lambda t: (0, t))
    return pl.pallas_call(
        ffn_fwd_kernel,
        grid=(ff // tf,),
        in_specs=[whole(low.shape), pl.BlockSpec((d, tf), lambda t: (0, t)), pl.BlockSpec((1, tf), lambda t: (0, t)),
                  pl.BlockSpec((tf, d), lambda t: (t, 0)), whole(xhat.shape), whole(g.shape), whole(vec.shape)],
        out_specs=[col, col, whole((rows, d)), whole((rows, d)), whole((8, d))],
        out_shape=[jax.ShapeDtypeStruct((rows, ff), BF16), jax.ShapeDtypeStruct((rows, ff), BF16),
                   jax.ShapeDtypeStruct((rows, d), BF16), jax.ShapeDtypeStruct((rows, d), F32),
                   jax.ShapeDtypeStruct((8, d), F32)],
        scratch_shapes=[pltpu.VMEM((rows, d), F32)],
        compiler_params=params(),
        cost_estimate=cost(4 * rows * d * ff, 4 * d * ff + 4 * rows * ff + rows * d * 14, 2 * rows * ff),
        name="ffn_fwd",
    )(low, wu, bu, wd, xhat, g, vec)


def ffn_bwd_kernel(low, gs, hid, dg, wu, wd, xhat, r1, vec, dwd, dwu, gsf, sums, sumu, acc, gd, lowt, gu):
    rows = low.shape[0]
    t = pl.program_id(0)
    tf = hid.shape[1]

    @pl.when(t == 0)
    def _():
        acc[...] = gs[...]
        gd[...] = gs[...].astype(BF16)
        lowt[...] = low[...].T

    sumu[...] = jnp.zeros_like(sumu)

    def back(r):
        gh = dot_nt(gd[r, :], wd[...])
        g = (gh * dg[r, :].astype(F32)).astype(BF16)
        gu[r, :] = g
        sumu[...] += jnp.sum(g.astype(F32), axis=0, keepdims=True)
        acc[r, :] += dot_nt(g, wu[...])

    chunks(rows, back)
    for j in range(tf // 256):
        c = slice(j * 256, (j + 1) * 256)
        dwd[c, :] = dot(hid[:, c].T, gd[...]).astype(BF16)

    def wgrad(r):
        dwu[r, :] = dot(lowt[r, :], gu[...]).astype(BF16)

    chunks(lowt.shape[0], wgrad)

    @pl.when(t == pl.num_programs(0) - 1)
    def _():
        sums[...] = jnp.zeros_like(sums)

        def fin(r):
            gf = acc[r, :]
            n = xhat[r, :]
            sums[0:1, :] += jnp.sum(gf * n, axis=0, keepdims=True)
            sums[1:2, :] += jnp.sum(gf, axis=0, keepdims=True)
            grad = norm_back(gf * vec[4:5, :], n, r1[r, 0:1])
            gsf[r, :] = grad
            sums[2:3, :] += jnp.sum(grad.astype(BF16).astype(F32), axis=0, keepdims=True)

        chunks(rows, fin)


def ffn_bwd_call(low, gs, hid, dg, wu, wd, xhat, r1, vec):
    rows, d = low.shape
    ff = wu.shape[1]
    tf = 512
    col = pl.BlockSpec((rows, tf), lambda t: (0, t))
    wus = pl.BlockSpec((d, tf), lambda t: (0, t))
    wds = pl.BlockSpec((tf, d), lambda t: (t, 0))
    once = dict(pipeline_mode=pl.Buffered(1))

    def one(shape):
        return pl.BlockSpec(shape, lambda *_: (0,) * len(shape), **once)

    return pl.pallas_call(
        ffn_bwd_kernel,
        grid=(ff // tf,),
        in_specs=[one(low.shape), one(gs.shape), col, col, wus, wds, one(xhat.shape), one(r1.shape), one(vec.shape)],
        out_specs=[wds, wus, whole((rows, d)), whole((8, d)), pl.BlockSpec((1, tf), lambda t: (0, t))],
        out_shape=[jax.ShapeDtypeStruct((ff, d), BF16), jax.ShapeDtypeStruct((d, ff), BF16),
                   jax.ShapeDtypeStruct((rows, d), F32), jax.ShapeDtypeStruct((8, d), F32),
                   jax.ShapeDtypeStruct((1, ff), F32)],
        scratch_shapes=[pltpu.VMEM((rows, d), F32), pltpu.VMEM((rows, d), BF16), pltpu.VMEM((d, rows), BF16),
                        pltpu.VMEM((rows, tf), BF16)],
        compiler_params=params(),
        cost_estimate=cost(8 * rows * d * ff, 8 * d * ff + 4 * rows * ff + rows * d * 18),
        name="ffn_bwd",
    )(low, gs, hid, dg, wu, wd, xhat, r1, vec)


def out_bwd_kernel(gsf, ctx, w, gc, dwo, ga, ctxt):
    rows = gsf.shape[0]

    def cast(r):
        ga[r, :] = gsf[r, :].astype(BF16)
        gc[r, :] = dot_nt(ga[r, :], w[...]).astype(BF16)

    chunks(rows, cast)
    ctxt[...] = ctx[...].T

    def wgrad(r):
        dwo[r, :] = dot(ctxt[r, :], ga[...]).astype(BF16)

    chunks(ctxt.shape[0], wgrad)


def out_bwd_call(gsf, ctx, w):
    rows, d = gsf.shape
    return pl.pallas_call(
        out_bwd_kernel,
        grid=(1,),
        in_specs=[whole(gsf.shape), whole(ctx.shape), whole(w.shape)],
        out_specs=[whole((rows, d)), whole((d, d))],
        out_shape=[jax.ShapeDtypeStruct((rows, d), BF16), jax.ShapeDtypeStruct((d, d), BF16)],
        scratch_shapes=[pltpu.VMEM((rows, d), BF16), pltpu.VMEM((d, rows), BF16)],
        compiler_params=params(),
        cost_estimate=cost(4 * rows * d * d, rows * d * 8 + 4 * d * d),
        name="out_bwd",
    )(gsf, ctx, w)


def in_bwd_kernel(x, gsf, dq, dk, dv, wq, wk, wv, tg, dwq, dwk, dwv, sums, xt):
    rows = x.shape[0]
    xt[...] = x[...].T
    sums[...] = jnp.zeros_like(sums)

    def tok(r):
        g = gsf[r, :] + dot_nt(dq[r, :], wq[...]) + dot_nt(dk[r, :], wk[...]) + dot_nt(dv[r, :], wv[...])
        tg[r, :] = g.astype(BF16)
        sums[0:1, :] += jnp.sum(dq[r, :].astype(F32), axis=0, keepdims=True)
        sums[1:2, :] += jnp.sum(dv[r, :].astype(F32), axis=0, keepdims=True)

    chunks(rows, tok)

    def wgrad(r):
        dwq[r, :] = dot(xt[r, :], dq[...]).astype(BF16)
        dwk[r, :] = dot(xt[r, :], dk[...]).astype(BF16)
        dwv[r, :] = dot(xt[r, :], dv[...]).astype(BF16)

    chunks(xt.shape[0], wgrad)


def in_bwd_call(x, gsf, dq, dk, dv, wq, wk, wv):
    rows, d = x.shape
    once = dict(pipeline_mode=pl.Buffered(1))

    def one(shape):
        return pl.BlockSpec(shape, lambda *_: (0,) * len(shape), **once)

    return pl.pallas_call(
        in_bwd_kernel,
        grid=(1,),
        in_specs=[one((rows, d))] * 5 + [one((d, d))] * 3,
        out_specs=[one((rows, d))] + [one((d, d))] * 3 + [one((8, d))],
        out_shape=[jax.ShapeDtypeStruct((rows, d), BF16)] + [jax.ShapeDtypeStruct((d, d), BF16)] * 3
        + [jax.ShapeDtypeStruct((8, d), F32)],
        scratch_shapes=[pltpu.VMEM((d, rows), BF16)],
        compiler_params=params(),
        cost_estimate=cost(12 * rows * d * d, rows * d * 14 + 12 * d * d),
        name="in_bwd",
    )(x, gsf, dq, dk, dv, wq, wk, wv)


def sequence_table(lengths, own, rows):
    ids = jnp.arange(lengths.shape[0], dtype=jnp.int32)
    starts = jnp.sum(jnp.where(ids[None, :] < ids[:, None], lengths[None, :], 0), axis=1)
    blocks = rows // GRAN
    at = own * rows + jnp.arange(blocks, dtype=jnp.int32) * GRAN
    inside = (starts[None, :] <= at[:, None]) & (at[:, None] < (starts + lengths)[None, :])
    first = jnp.sum(jnp.where(inside, starts[None, :], 0), axis=1)
    length = jnp.sum(jnp.where(inside, lengths[None, :], 0), axis=1)
    lead = (first == at) | (jnp.arange(blocks) == 0)
    return jnp.stack([(first - own * rows + HALO) // GRAN, jnp.where(lead, length // GRAN, 0)]).astype(jnp.int32)


def halo(x, n):
    right = [(i, i + 1) for i in range(n - 1)]
    left = [(i + 1, i) for i in range(n - 1)]
    return lax.ppermute(x[-HALO:], "dp", right), lax.ppermute(x[:HALO], "dp", left)


def local(tokens, cotangent, lengths, dealing, *shards):
    n = lax.axis_size("dp")
    own = lax.axis_index("dp")
    rows, d = tokens.shape
    part = d // n
    wq, wk, wv, wo, wu, wd = (lax.all_gather(s, "dp", axis=0, tiled=True) for s in shards[:6])
    qb, vb, ob, ub, db, fg, fs, sg, ss = shards[6:]
    packed = jnp.concatenate([qb, vb, ob, db, fg, fs, sg, ss, ub])
    gathered = lax.all_gather(packed, "dp", axis=0, tiled=False)
    vec = gathered[:, : 8 * part].reshape(n, 8, part).transpose(1, 0, 2).reshape(8, d).astype(F32)
    bu = gathered[:, 8 * part:].reshape(1, -1).astype(F32)
    tab = sequence_table(lengths, own, rows)
    xl, xr = halo(tokens, n)
    q, k, v = qkv_call(xl, tokens, xr, wq, wk, wv, vec)
    ctx = attn_fwd_call(tab, q, k, v, rows)
    xhat, low, r1 = out_proj_call(ctx, wo, tokens, vec)
    hid, dg, layer_out, gs, sums2 = ffn_fwd_call(low, wu, bu, wd, xhat, cotangent, vec)
    dwd, dwu, gsf, sums1, sumu = ffn_bwd_call(low, gs, hid, dg, wu, wd, xhat, r1, vec)
    gc, dwo = out_bwd_call(gsf, ctx, wo)
    gl, gr = halo(gc, n)
    dq, dk, dv = attn_bwd_call(tab, q, k, v, gl, gc, gr)
    tg, dwq, dwk, dwv, sums0 = in_bwd_call(tokens, gsf, dq, dk, dv, wq, wk, wv)
    big = jnp.concatenate([w.reshape(n, -1, d) for w in (dwq, dwk, dwv, dwo)]
                          + [dwu.reshape(n, part, -1, d).transpose(0, 2, 1, 3).reshape(n, -1, d), dwd.reshape(n, -1, d)], axis=1)
    share = lax.psum_scatter(big, "dp", scatter_dimension=0, tiled=False).astype(F32)
    small = jnp.stack([sums0[0], sums0[1], sums1[2], sums2[2], sums1[0], sums1[1], sums2[0], sums2[1]])
    small = jnp.concatenate([small.reshape(8, n, part).transpose(1, 0, 2).reshape(n, -1), sumu.reshape(n, -1)], axis=1)
    tiny = lax.psum_scatter(small, "dp", scatter_dimension=0, tiled=False)
    gq, gk, gv, go = (share[i * part:(i + 1) * part] for i in range(4))
    gu = share[4 * part:8 * part].reshape(-1, part, d).transpose(1, 0, 2).reshape(part, -1)
    gd = share[8 * part:]
    t = [tiny[i * part:(i + 1) * part] for i in range(8)] + [tiny[8 * part:]]
    return (layer_out, tg, gq, gk, gv, go, gu, gd, t[0], t[1], t[2], t[8], t[3], t[4], t[5], t[6], t[7])


def solution(mesh):
    mat = P("dp", None)
    vec = P("dp")
    return jax.shard_map(
        local,
        mesh=mesh,
        in_specs=(mat, mat, P(), P()) + (mat,) * 6 + (vec,) * 9,
        out_specs=(mat,) * 8 + (vec,) * 9,
        check_vma=False,
    )
```

```python
import functools

import jax
import jax.numpy as jnp
from jax import lax
from jax.experimental import pallas as pl
from jax.experimental.pallas import tpu as pltpu
from jax.sharding import PartitionSpec as P

HD = 64
GRAN = 128
HALO = 384
EPS = 1e-12
F32 = jnp.float32
BF16 = jnp.bfloat16
NT = (((1,), (1,)), ((), ()))
MESH = pl.DeviceIdType.MESH
ANY = pl.BlockSpec(memory_space=pl.ANY)


def params(limit=56):
    return pltpu.CompilerParams(vmem_limit_bytes=limit << 20)


def whole(shape):
    return pl.BlockSpec(shape, lambda *_: (0,) * len(shape))


def dot(a, b):
    return jnp.dot(a, b, preferred_element_type=F32)


def dot_nt(a, b):
    return lax.dot_general(a, b, NT, preferred_element_type=F32)


def cost(flops, nbytes, trans=0):
    return pl.CostEstimate(flops=flops, bytes_accessed=nbytes, transcendentals=trans)


def qkv_kernel(xl, xo, xr, wq, wk, wv, vec, q, k, v):
    rows = xo.shape[0]
    for w, out, b in ((wq, q, vec[0:1, :]), (wk, k, None), (wv, v, vec[1:2, :])):
        def put(x, start, size):
            r = dot(x, w[...])
            if b is not None:
                r = r + b
            out[pl.ds(start, size), :] = r.astype(BF16)

        put(xl[...], 0, HALO)
        put(xr[...], HALO + rows, HALO)

        def step(i, c):
            s = pl.multiple_of(i * 256, 256)
            put(xo[pl.ds(s, 256), :], pl.multiple_of(HALO + s, 128), 256)
            return c

        lax.fori_loop(0, rows // 256, step, 0)


def qkv_call(xl, xo, xr, wq, wk, wv, vec):
    rows, d = xo.shape
    win = rows + 2 * HALO
    tn = 512
    wspec = pl.BlockSpec((d, tn), lambda j: (0, j))
    ospec = pl.BlockSpec((win, tn), lambda j: (0, j))
    out = jax.ShapeDtypeStruct((win, d), BF16)
    return pl.pallas_call(
        qkv_kernel,
        grid=(d // tn,),
        in_specs=[whole(xl.shape), whole(xo.shape), whole(xr.shape), wspec, wspec, wspec,
                  pl.BlockSpec((8, tn), lambda j: (0, j))],
        out_specs=[ospec] * 3,
        out_shape=[out] * 3,
        compiler_params=params(),
        cost_estimate=cost(6 * win * d * d, 2 * (4 * win * d + 3 * d * d)),
        name="qkv",
    )(xl, xo, xr, wq, wk, wv, vec)


def probs_t(k, qh):
    st = dot_nt(k, qh)
    e = jnp.exp(st - jnp.max(st, axis=0, keepdims=True))
    return e * (1.0 / jnp.sum(e, axis=0, keepdims=True))


def attn_fwd_kernel(tab, q_ref, k_ref, v_ref, o_ref, ctx):
    blocks = o_ref.shape[0] // GRAN

    def one(b, c):
        n = tab[1, b]
        s0 = tab[0, b]
        for nn in range(1, 5):
            @pl.when(n == nn)
            def _():
                size = nn * GRAN
                rows = pl.ds(pl.multiple_of(s0 * GRAN, GRAN), size)
                q = q_ref[rows, :] * jnp.asarray(0.125, BF16)
                k = k_ref[rows, :]
                vt = v_ref[rows, :].T
                low = lax.broadcasted_iota(jnp.int32, q.shape, 1) < HD
                parts = []
                for h in range(2):
                    qh = jnp.where(low if h == 0 else ~low, q, jnp.zeros_like(q))
                    p = probs_t(k, qh).astype(BF16)
                    parts.append(dot(vt[h * HD:(h + 1) * HD, :], p))
                ctx[rows, :] = jnp.concatenate(parts, axis=0).T.astype(BF16)
        return c

    lax.fori_loop(0, blocks, one, 0)
    o_ref[...] = ctx[pl.ds(HALO, o_ref.shape[0]), :]


def attn_fwd_call(tab, q, k, v, rows):
    win, d = q.shape
    spec = pl.BlockSpec((win, 2 * HD), lambda h, t: (0, h))
    return pl.pallas_call(
        attn_fwd_kernel,
        grid_spec=pltpu.PrefetchScalarGridSpec(
            num_scalar_prefetch=1,
            grid=(d // (2 * HD),),
            in_specs=[spec] * 3,
            out_specs=pl.BlockSpec((rows, 2 * HD), lambda h, t: (0, h)),
            scratch_shapes=[pltpu.VMEM((win, 2 * HD), BF16)],
        ),
        out_shape=jax.ShapeDtypeStruct((rows, d), BF16),
        compiler_params=params(),
        cost_estimate=cost(8 * rows * 512 * d, 8 * win * d, rows * 512 * 16),
        name="attn_fwd",
    )(tab, q, k, v)


def attn_bwd_kernel(tab, q_ref, k_ref, v_ref, gl, go, gr, dq_o, dk_o, dv_o, g_s, dq_s, dk_s, dv_s):
    rows_own = go.shape[0]
    blocks = rows_own // GRAN
    g_s[pl.ds(0, HALO), :] = gl[...]
    g_s[pl.ds(HALO, rows_own), :] = go[...]
    g_s[pl.ds(HALO + rows_own, HALO), :] = gr[...]

    def one(b, c):
        n = tab[1, b]
        s0 = tab[0, b]
        for nn in range(1, 5):
            @pl.when(n == nn)
            def _():
                size = nn * GRAN
                rows = pl.ds(pl.multiple_of(s0 * GRAN, GRAN), size)
                q = q_ref[rows, :] * jnp.asarray(0.125, BF16)
                k = k_ref[rows, :]
                v = v_ref[rows, :]
                g = g_s[rows, :]
                kt = (k * jnp.asarray(0.125, BF16)).T
                low = lax.broadcasted_iota(jnp.int32, q.shape, 1) < HD
                zero = jnp.zeros_like(q)
                dqs, dks, dvs = [], [], []
                for h in range(2):
                    mine = low if h == 0 else ~low
                    p = probs_t(k, jnp.where(mine, q, zero))
                    dp = dot_nt(v, jnp.where(mine, g, zero))
                    delta = jnp.sum(p * dp, axis=0, keepdims=True)
                    ds = (p * (dp - delta)).astype(BF16)
                    dvs.append(dot(p.astype(BF16), g))
                    dks.append(dot(ds, q))
                    dqs.append(dot(kt[h * HD:(h + 1) * HD, :], ds))
                dq_s[rows, :] = jnp.concatenate(dqs, axis=0).T.astype(BF16)
                dk_s[rows, :] = jnp.where(low, dks[0], dks[1]).astype(BF16)
                dv_s[rows, :] = jnp.where(low, dvs[0], dvs[1]).astype(BF16)
        return c

    lax.fori_loop(0, blocks, one, 0)
    own = pl.ds(HALO, rows_own)
    dq_o[...] = dq_s[own, :]
    dk_o[...] = dk_s[own, :]
    dv_o[...] = dv_s[own, :]


def attn_bwd_call(tab, q, k, v, gl, go, gr):
    win, d = q.shape
    rows = go.shape[0]
    spec = pl.BlockSpec((win, 2 * HD), lambda h, t: (0, h))
    own = pl.BlockSpec((rows, 2 * HD), lambda h, t: (0, h))
    halo = pl.BlockSpec((HALO, 2 * HD), lambda h, t: (0, h))
    out = jax.ShapeDtypeStruct((rows, d), BF16)
    return pl.pallas_call(
        attn_bwd_kernel,
        grid_spec=pltpu.PrefetchScalarGridSpec(
            num_scalar_prefetch=1,
            grid=(d // (2 * HD),),
            in_specs=[spec] * 3 + [halo, own, halo],
            out_specs=[own] * 3,
            scratch_shapes=[pltpu.VMEM((win, 2 * HD), BF16)] * 4,
        ),
        out_shape=[out] * 3,
        compiler_params=params(),
        cost_estimate=cost(20 * rows * 512 * d, 14 * win * d, rows * 512 * 16),
        name="attn_bwd",
    )(tab, q, k, v, gl, go, gr)


def norm_stats(z):
    cen = z - jnp.mean(z, axis=-1, keepdims=True)
    r = lax.rsqrt(jnp.mean(cen * cen, axis=-1, keepdims=True) + EPS)
    return cen * r, r


def norm_back(e, n, r):
    return r * (e - jnp.mean(e, axis=-1, keepdims=True) - n * jnp.mean(e * n, axis=-1, keepdims=True))


def out_proj_kernel(ctx, w, x, vec, xhat, low, r_o):
    z = x[...].astype(F32) + (dot(ctx[...], w[...]) + vec[2:3, :])
    n, r = norm_stats(z)
    xhat[...] = n
    r_o[...] = jnp.broadcast_to(r, r_o.shape)
    low[...] = (n * vec[4:5, :] + vec[5:6, :]).astype(BF16)


def out_proj_call(ctx, w, x, vec):
    rows, d = x.shape
    tm = 256
    t = pl.BlockSpec((tm, d), lambda i: (i, 0))
    return pl.pallas_call(
        out_proj_kernel,
        grid=(rows // tm,),
        in_specs=[t, whole(w.shape), t, whole(vec.shape)],
        out_specs=[t, t, pl.BlockSpec((tm, 128), lambda i: (i, 0))],
        out_shape=[jax.ShapeDtypeStruct((rows, d), F32), jax.ShapeDtypeStruct((rows, d), BF16),
                   jax.ShapeDtypeStruct((rows, 128), F32)],
        compiler_params=params(),
        cost_estimate=cost(2 * rows * d * d, rows * d * 10 + 2 * d * d),
        name="out_proj",
    )(ctx, w, x, vec)


RC = 256


def chunks(rows, fn):
    def step(i, c):
        fn(pl.ds(pl.multiple_of(i * RC, RC), RC))
        return c

    lax.fori_loop(0, rows // RC, step, 0)


def ffn_fwd_kernel(low, wu, bu, wd, xhat, g, vec, hid, dg, out, gs, sums, acc):
    rows = low.shape[0]
    t = pl.program_id(0)

    @pl.when(t == 0)
    def _():
        acc[...] = jnp.zeros_like(acc)

    def up(r):
        u = dot(low[r, :], wu[...]) + bu[...]
        phi = 0.5 * (1.0 + lax.erf(u * (0.5 ** 0.5)))
        h = (u * phi).astype(BF16)
        hid[r, :] = h
        dg[r, :] = (phi + u * (0.3989422804014327 * jnp.exp(-0.5 * u * u))).astype(BF16)
        acc[r, :] += dot(h, wd[...])

    chunks(rows, up)

    @pl.when(t == pl.num_programs(0) - 1)
    def _():
        sums[...] = jnp.zeros_like(sums)

        def fin(r):
            z = (xhat[r, :] * vec[4:5, :] + vec[5:6, :]) + (acc[r, :] + vec[3:4, :])
            n, rr = norm_stats(z)
            out[r, :] = (n * vec[6:7, :] + vec[7:8, :]).astype(BF16)
            gv = g[r, :].astype(F32)
            sums[0:1, :] += jnp.sum(gv * n, axis=0, keepdims=True)
            sums[1:2, :] += jnp.sum(gv, axis=0, keepdims=True)
            grad = norm_back(gv * vec[6:7, :], n, rr)
            gs[r, :] = grad
            sums[2:3, :] += jnp.sum(grad.astype(BF16).astype(F32), axis=0, keepdims=True)

        chunks(rows, fin)


def ffn_fwd_call(low, wu, bu, wd, xhat, g, vec):
    rows, d = low.shape
    ff = wu.shape[1]
    tf = 512
    col = pl.BlockSpec((rows, tf), lambda t: (0, t))
    return pl.pallas_call(
        ffn_fwd_kernel,
        grid=(ff // tf,),
        in_specs=[whole(low.shape), pl.BlockSpec((d, tf), lambda t: (0, t)), pl.BlockSpec((1, tf), lambda t: (0, t)),
                  pl.BlockSpec((tf, d), lambda t: (t, 0)), whole(xhat.shape), whole(g.shape), whole(vec.shape)],
        out_specs=[col, col, whole((rows, d)), whole((rows, d)), whole((8, d))],
        out_shape=[jax.ShapeDtypeStruct((rows, ff), BF16), jax.ShapeDtypeStruct((rows, ff), BF16),
                   jax.ShapeDtypeStruct((rows, d), BF16), jax.ShapeDtypeStruct((rows, d), F32),
                   jax.ShapeDtypeStruct((8, d), F32)],
        scratch_shapes=[pltpu.VMEM((rows, d), F32)],
        compiler_params=params(),
        cost_estimate=cost(4 * rows * d * ff, 4 * d * ff + 4 * rows * ff + rows * d * 14, 2 * rows * ff),
        name="ffn_fwd",
    )(low, wu, bu, wd, xhat, g, vec)


def ffn_bwd_kernel(low, gs, hid, dg, wu, wd, xhat, r1, vec, dwd, dwu, gsf, sums, sumu, acc, gd, lowt, gu):
    rows = low.shape[0]
    t = pl.program_id(0)
    tf = hid.shape[1]

    @pl.when(t == 0)
    def _():
        acc[...] = gs[...]
        gd[...] = gs[...].astype(BF16)
        lowt[...] = low[...].T

    sumu[...] = jnp.zeros_like(sumu)

    def back(r):
        gh = dot_nt(gd[r, :], wd[...])
        g = (gh * dg[r, :].astype(F32)).astype(BF16)
        gu[r, :] = g
        sumu[...] += jnp.sum(g.astype(F32), axis=0, keepdims=True)
        acc[r, :] += dot_nt(g, wu[...])

    chunks(rows, back)
    for j in range(tf // 256):
        c = slice(j * 256, (j + 1) * 256)
        dwd[c, :] = dot(hid[:, c].T, gd[...]).astype(BF16)

    def wgrad(r):
        dwu[r, :] = dot(lowt[r, :], gu[...]).astype(BF16)

    chunks(lowt.shape[0], wgrad)

    @pl.when(t == pl.num_programs(0) - 1)
    def _():
        sums[...] = jnp.zeros_like(sums)

        def fin(r):
            gf = acc[r, :]
            n = xhat[r, :]
            sums[0:1, :] += jnp.sum(gf * n, axis=0, keepdims=True)
            sums[1:2, :] += jnp.sum(gf, axis=0, keepdims=True)
            grad = norm_back(gf * vec[4:5, :], n, r1[r, 0:1])
            gsf[r, :] = grad
            sums[2:3, :] += jnp.sum(grad.astype(BF16).astype(F32), axis=0, keepdims=True)

        chunks(rows, fin)


def ffn_bwd_call(low, gs, hid, dg, wu, wd, xhat, r1, vec):
    rows, d = low.shape
    ff = wu.shape[1]
    tf = 512
    col = pl.BlockSpec((rows, tf), lambda t: (0, t))
    wus = pl.BlockSpec((d, tf), lambda t: (0, t))
    wds = pl.BlockSpec((tf, d), lambda t: (t, 0))
    once = dict(pipeline_mode=pl.Buffered(1))

    def one(shape):
        return pl.BlockSpec(shape, lambda *_: (0,) * len(shape), **once)

    return pl.pallas_call(
        ffn_bwd_kernel,
        grid=(ff // tf,),
        in_specs=[one(low.shape), one(gs.shape), col, col, wus, wds, one(xhat.shape), one(r1.shape), one(vec.shape)],
        out_specs=[wds, wus, whole((rows, d)), whole((8, d)), pl.BlockSpec((1, tf), lambda t: (0, t))],
        out_shape=[jax.ShapeDtypeStruct((ff, d), BF16), jax.ShapeDtypeStruct((d, ff), BF16),
                   jax.ShapeDtypeStruct((rows, d), F32), jax.ShapeDtypeStruct((8, d), F32),
                   jax.ShapeDtypeStruct((1, ff), F32)],
        scratch_shapes=[pltpu.VMEM((rows, d), F32), pltpu.VMEM((rows, d), BF16), pltpu.VMEM((d, rows), BF16),
                        pltpu.VMEM((rows, tf), BF16)],
        compiler_params=params(),
        cost_estimate=cost(8 * rows * d * ff, 8 * d * ff + 4 * rows * ff + rows * d * 18),
        name="ffn_bwd",
    )(low, gs, hid, dg, wu, wd, xhat, r1, vec)


def out_bwd_kernel(gsf, ctx, w, gc, dwo, ga, ctxt):
    rows = gsf.shape[0]

    def cast(r):
        ga[r, :] = gsf[r, :].astype(BF16)
        gc[r, :] = dot_nt(ga[r, :], w[...]).astype(BF16)

    chunks(rows, cast)
    ctxt[...] = ctx[...].T

    def wgrad(r):
        dwo[r, :] = dot(ctxt[r, :], ga[...]).astype(BF16)

    chunks(ctxt.shape[0], wgrad)


def out_bwd_call(gsf, ctx, w):
    rows, d = gsf.shape
    return pl.pallas_call(
        out_bwd_kernel,
        grid=(1,),
        in_specs=[whole(gsf.shape), whole(ctx.shape), whole(w.shape)],
        out_specs=[whole((rows, d)), whole((d, d))],
        out_shape=[jax.ShapeDtypeStruct((rows, d), BF16), jax.ShapeDtypeStruct((d, d), BF16)],
        scratch_shapes=[pltpu.VMEM((rows, d), BF16), pltpu.VMEM((d, rows), BF16)],
        compiler_params=params(),
        cost_estimate=cost(4 * rows * d * d, rows * d * 8 + 4 * d * d),
        name="out_bwd",
    )(gsf, ctx, w)


def in_bwd_kernel(x, gsf, dq, dk, dv, wq, wk, wv, tg, dwq, dwk, dwv, sums, xt):
    rows = x.shape[0]
    xt[...] = x[...].T
    sums[...] = jnp.zeros_like(sums)

    def tok(r):
        g = gsf[r, :] + dot_nt(dq[r, :], wq[...]) + dot_nt(dk[r, :], wk[...]) + dot_nt(dv[r, :], wv[...])
        tg[r, :] = g.astype(BF16)
        sums[0:1, :] += jnp.sum(dq[r, :].astype(F32), axis=0, keepdims=True)
        sums[1:2, :] += jnp.sum(dv[r, :].astype(F32), axis=0, keepdims=True)

    chunks(rows, tok)

    def wgrad(r):
        dwq[r, :] = dot(xt[r, :], dq[...]).astype(BF16)
        dwk[r, :] = dot(xt[r, :], dk[...]).astype(BF16)
        dwv[r, :] = dot(xt[r, :], dv[...]).astype(BF16)

    chunks(xt.shape[0], wgrad)


def in_bwd_call(x, gsf, dq, dk, dv, wq, wk, wv):
    rows, d = x.shape
    once = dict(pipeline_mode=pl.Buffered(1))

    def one(shape):
        return pl.BlockSpec(shape, lambda *_: (0,) * len(shape), **once)

    return pl.pallas_call(
        in_bwd_kernel,
        grid=(1,),
        in_specs=[one((rows, d))] * 5 + [one((d, d))] * 3,
        out_specs=[one((rows, d))] + [one((d, d))] * 3 + [one((8, d))],
        out_shape=[jax.ShapeDtypeStruct((rows, d), BF16)] + [jax.ShapeDtypeStruct((d, d), BF16)] * 3
        + [jax.ShapeDtypeStruct((8, d), F32)],
        scratch_shapes=[pltpu.VMEM((d, rows), BF16)],
        compiler_params=params(),
        cost_estimate=cost(12 * rows * d * d, rows * d * 14 + 12 * d * d),
        name="in_bwd",
    )(x, gsf, dq, dk, dv, wq, wk, wv)


def grid_of(n):
    chips = n // 2
    return {16: (4, 2, 2), 64: (4, 4, 4)}.get(chips, (chips, 1, 1))


class Place:
    def __init__(self, n):
        self.n = n
        self.size = grid_of(n)
        me = lax.axis_index("dp")
        nz, ny, nx = self.size
        self.me = me
        self.c = lax.rem(me, 2)
        self.x = lax.rem(me // 2, nx)
        self.y = lax.rem(me // (2 * nx), ny)
        self.z = me // (2 * nx * ny)

    def at(self, axis, k):
        nz, ny, nx = self.size
        z, y, x, c = self.z, self.y, self.x, self.c
        if axis == "z":
            z = lax.rem(z + k, nz)
        elif axis == "y":
            y = lax.rem(y + k, ny)
        elif axis == "x":
            x = lax.rem(x + k, nx)
        else:
            c = lax.rem(c + k, 2)
        pos = {"z": z, "y": y, "x": x, "c": c}[axis]
        return ((z * ny + y) * nx + x) * 2 + c, pos

    def steps(self, axis):
        nz, ny, nx = self.size
        return range(1, {"z": nz, "y": ny, "x": nx, "c": 2}[axis])

    def peers(self):
        return [self.at(a, k)[0] for a in "zyxc" for k in self.steps(a)]


def enter(peers):
    sem = pltpu.get_barrier_semaphore()
    for p in peers:
        pl.semaphore_signal(sem, inc=1, device_id=(p,), device_id_type=MESH)
    pl.semaphore_wait(sem, len(peers))


def gather_slots(n):
    nz, ny, nx = grid_of(n)
    return (nz - 1) + 2 * (ny - 1) + 2 * (nx - 1) + 1


class Gather:
    def __init__(self, place, src, dst, rows, cols, ssem, rsem, lsem, index):
        self.p, self.index = place, index
        self.src, self.dst, self.rows, self.cols = src, dst, rows, cols
        self.ssem, self.rsem, self.lsem = ssem, rsem, lsem
        p = place
        r0, nr = rows
        c0, nc = cols
        rs = pl.ds(r0, nr)
        full = pl.ds(c0, nc)
        halves = (pl.ds(c0, nc // 2), pl.ds(c0 + nc // 2, nc // 2))
        al = pl.ds(0, p.size[0])
        self.local = pltpu.make_async_copy(src.at[rs, full], dst.at[p.z, p.y, p.x, p.c, rs, full], lsem.at[index])
        slot = 0

        def copy(s, d, dev):
            nonlocal slot
            cp = pltpu.make_async_remote_copy(src_ref=s, dst_ref=d, send_sem=ssem.at[index, slot], recv_sem=rsem.at[index, slot],
                                              device_id=(dev,), device_id_type=MESH)
            slot += 1
            return cp

        mine = dst.at[p.z, p.y, p.x, p.c, rs, full]
        self.ph = [[], [], [], []]
        for k in p.steps("z"):
            self.ph[0].append(copy(src.at[rs, full], mine, p.at("z", k)[0]))
        for h, axis in ((0, "y"), (1, "x")):
            s = dst.at[:, p.y, p.x, p.c, rs, halves[h]]
            for k in p.steps(axis):
                self.ph[1].append(copy(s, s, p.at(axis, k)[0]))
        for h, axis in ((0, "x"), (1, "y")):
            s = dst.at[:, :, p.x, p.c, rs, halves[0]] if h == 0 else dst.at[:, p.y, :, p.c, rs, halves[1]]
            for k in p.steps(axis):
                self.ph[2].append(copy(s, s, p.at(axis, k)[0]))
        s = dst.at[:, :, :, p.c, rs, full]
        self.ph[3].append(copy(s, s, p.at("c", 1)[0]))

    def start(self, i):
        if i == 0:
            self.local.start()
        for cp in self.ph[i]:
            cp.start()

    def wait(self, i):
        if i == 0:
            self.local.wait()
        for cp in self.ph[i]:
            cp.wait_recv()

    def sent(self):
        for ph in self.ph:
            for cp in ph:
                cp.wait_send()


def gather_kernel(n, plan, nsrc, *refs):
    srcs, xsrc, outs = refs[:nsrc], refs[nsrc], refs[nsrc + 1:2 * nsrc + 1]
    xl, xr = refs[2 * nsrc + 1:2 * nsrc + 3]
    ssem, rsem, lsem, hs, hr = refs[2 * nsrc+3:]
    p = Place(n)
    right, left = lax.rem(p.me + 1, n), lax.rem(p.me + n - 1, n)
    enter(p.peers() + [left, right])
    rows = xsrc.shape[0]
    halo = [pltpu.make_async_remote_copy(src_ref=xsrc.at[pl.ds(rows-HALO,HALO),:], dst_ref=xl, send_sem=hs.at[0], recv_sem=hr.at[0], device_id=(right,), device_id_type=MESH),
            pltpu.make_async_remote_copy(src_ref=xsrc.at[pl.ds(0,HALO),:], dst_ref=xr, send_sem=hs.at[1], recv_sem=hr.at[1], device_id=(left,), device_id_type=MESH)]
    for h in halo: h.start()
    g = [Gather(p, srcs[a], outs[a], r, c, ssem, rsem, lsem, i) for i, (a, r, c) in enumerate(plan)]
    for s in range(len(g) + 4):
        for ph in (0, 1, 2, 3, 4):
            i = s - ph
            if 0 <= i < len(g):
                if ph > 0:
                    g[i].wait(ph - 1)
                if ph < 4:
                    g[i].start(ph)
    for c in g:
        c.sent()
    for h in halo: h.wait()


def gather_plan(shards, d):
    least = min(s.shape[0] for s in shards if s.shape[-1] >= d)
    plan = []
    for a, s in enumerate(shards):
        if s.shape[1] < d:
            plan.append((a, (0, s.shape[0]), (0, s.shape[1])))
            continue
        for j in range(s.shape[1] // d):
            for i in range(s.shape[0] // least):
                plan.append((a, (i * least, least), (j * d, d)))
    return plan


def gather_call(n, shards, tokens, order=None):
    d = tokens.shape[1]
    plan = gather_plan(shards, d)
    k = gather_slots(n)
    outs = [jax.ShapeDtypeStruct(grid_of(n) + (2,) + s.shape, s.dtype) for s in shards]
    halo = jax.ShapeDtypeStruct((HALO, d), tokens.dtype)
    res = pl.pallas_call(
        functools.partial(gather_kernel, n, plan, len(shards)),
        in_specs=[ANY] * (len(shards)+1),
        out_specs=[ANY] * (len(shards)+2),
        out_shape=outs+[halo,halo],
        scratch_shapes=[pltpu.SemaphoreType.DMA((len(plan), k)), pltpu.SemaphoreType.DMA((len(plan), k)),
                        pltpu.SemaphoreType.DMA((len(plan),)),pltpu.SemaphoreType.DMA((2,)),pltpu.SemaphoreType.DMA((2,))],
        compiler_params=pltpu.CompilerParams(collective_id=1, has_side_effects=True),
        name="gather",
    )(*shards, tokens)
    return [r.reshape((n * s.shape[0],) + s.shape[1:]) for r, s in zip(res, shards)] + list(res[-2:])


def reduce_slots(n):
    nz, ny, nx = grid_of(n)
    return (nz - 1) + 2 * (ny - 1) + 2 * (nx - 1) + 1


def landing(n, r, cols, dtype):
    nz, ny, nx = grid_of(n)
    h = cols // 2
    return [pltpu.VMEM((nz, ny, nx, r, cols), dtype),
            pltpu.VMEM((max(nx - 1, 1), nz, ny, r, h), dtype), pltpu.VMEM((max(ny - 1, 1), nz, nx, r, h), dtype),
            pltpu.VMEM((max(ny - 1, 1), nz, r, h), dtype), pltpu.VMEM((max(nx - 1, 1), nz, r, h), dtype),
            pltpu.VMEM((max(nz - 1, 1), r, cols), dtype)]


def partial(n, r, cols, dtype):
    nz, ny, nx = grid_of(n)
    h = cols // 2
    return [pltpu.VMEM((nz, ny, nx, r, cols), dtype), pltpu.VMEM((nz, ny, r, h), dtype), pltpu.VMEM((nz, nx, r, h), dtype),
            pltpu.VMEM((nz, r, cols), dtype), pltpu.VMEM((r, cols), F32)]


class Reduce:
    def __init__(self, place, src, land, part, out, ssem, rsem, lsem, index):
        self.p, self.src, self.land, self.part, self.out = place, src, land, part, out
        p = place
        self.h = part[3].shape[-1] // 2
        self.ca, self.cb = pl.ds(0, self.h), pl.ds(self.h, self.h)
        self.get = pltpu.make_async_copy(src.at[:, :, :, p.c], part[0], lsem.at[index, 0])
        self.put = pltpu.make_async_copy(part[4], out, lsem.at[index, 1])
        slot = 0

        def copy(s, d, dev):
            nonlocal slot
            cp = pltpu.make_async_remote_copy(src_ref=s, dst_ref=d, send_sem=ssem.at[index, slot], recv_sem=rsem.at[index, slot],
                                              device_id=(dev,), device_id_type=MESH)
            slot += 1
            return cp

        self.ph = [[], [], [], []]
        dev, oc = p.at("c", 1)
        self.ph[0].append(copy(src.at[:, :, :, oc], land[0], dev))
        for k in p.steps("x"):
            dev, o = p.at("x", k)
            self.ph[1].append(copy(part[0].at[:, :, o, :, self.ca], land[1].at[k - 1], dev))
        for k in p.steps("y"):
            dev, o = p.at("y", k)
            self.ph[1].append(copy(part[0].at[:, o, :, :, self.cb], land[2].at[k - 1], dev))
        for k in p.steps("y"):
            dev, o = p.at("y", k)
            self.ph[2].append(copy(part[1].at[:, o], land[3].at[k - 1], dev))
        for k in p.steps("x"):
            dev, o = p.at("x", k)
            self.ph[2].append(copy(part[2].at[:, o], land[4].at[k - 1], dev))
        for k in p.steps("z"):
            dev, o = p.at("z", k)
            self.ph[3].append(copy(part[3].at[o], land[5].at[k - 1], dev))

    def begin(self):
        self.get.start()
        self.ph[0][0].start()

    def go(self, i):
        p, land, part = self.p, self.land, self.part
        nz, ny, nx = p.size
        dt = part[0].dtype
        for cp in self.ph[i - 1]:
            cp.wait_recv()
        if i == 1:
            self.get.wait()

            def add(z, c):
                part[0][z] = (part[0][z].astype(F32) + land[0][z].astype(F32)).astype(dt)
                return c

            lax.fori_loop(0, nz, add, 0)
        elif i == 2:
            def add(z, c):
                a = part[0][z, :, pl.ds(p.x, 1), :, self.ca].astype(F32)[:, 0]
                for k in range(nx - 1):
                    a += land[1][k, z].astype(F32)
                part[1][z] = a.astype(dt)
                b = part[0][z, pl.ds(p.y, 1), :, :, self.cb].astype(F32)[0]
                for k in range(ny - 1):
                    b += land[2][k, z].astype(F32)
                part[2][z] = b.astype(dt)
                return c

            lax.fori_loop(0, nz, add, 0)
        elif i == 3:
            a = part[1][:, pl.ds(p.y, 1)].astype(F32)[:, 0]
            for k in range(ny - 1):
                a += land[3][k].astype(F32)
            part[3][:, :, self.ca] = a.astype(dt)
            b = part[2][:, pl.ds(p.x, 1)].astype(F32)[:, 0]
            for k in range(nx - 1):
                b += land[4][k].astype(F32)
            part[3][:, :, self.cb] = b.astype(dt)
        else:
            a = part[3][pl.ds(p.z, 1)].astype(F32)[0]
            for k in range(nz - 1):
                a += land[5][k].astype(F32)
            part[4][...] = a
            self.put.start()
            return
        for cp in self.ph[i]:
            cp.start()

    def finish(self):
        self.put.wait()
        for ph in self.ph:
            for cp in ph:
                cp.wait_send()


def reduce_kernel(n, plan, nsrc, *refs):
    srcs, outs = refs[:nsrc], refs[nsrc:2 * nsrc]
    scratch = refs[2 * nsrc:]
    ssem, rsem, lsem = scratch[-3:]
    p = Place(n)
    enter(p.peers())
    red = []
    for i, (a, (r0, nr), (c0, nc)) in enumerate(plan):
        land, part = scratch[11 * i:11 * i + 6], scratch[11 * i + 6:11 * i + 11]
        rs, cs = pl.ds(r0, nr), pl.ds(c0, nc)
        red.append(Reduce(p, srcs[a].at[:, :, :, :, rs, cs], land, part, outs[a].at[rs, cs], ssem, rsem, lsem, i))
    for s in range(len(red) + 5):
        for ph in (0, 1, 2, 3, 4, 5):
            i = s - ph
            if 0 <= i < len(red):
                if ph == 0:
                    red[i].begin()
                elif ph < 5:
                    red[i].go(ph)
                else:
                    red[i].finish()


def reduce_call(n, grads, d):
    views = [g.reshape(grid_of(n) + (2, g.shape[0] // n) + g.shape[1:]) for g in grads]
    plan = gather_plan([jax.ShapeDtypeStruct(v.shape[4:], v.dtype) for v in views], d)
    k = reduce_slots(n)
    scratch = []
    for a, r, c in plan:
        scratch += landing(n, r[1], c[1], grads[a].dtype) + partial(n, r[1], c[1], grads[a].dtype)
    return pl.pallas_call(
        functools.partial(reduce_kernel, n, plan, len(grads)),
        in_specs=[ANY] * len(grads),
        out_specs=[ANY] * len(grads),
        out_shape=[jax.ShapeDtypeStruct(v.shape[4:], F32) for v in views],
        scratch_shapes=scratch + [pltpu.SemaphoreType.DMA((len(plan), k)), pltpu.SemaphoreType.DMA((len(plan), k)),
                                  pltpu.SemaphoreType.DMA((len(plan), 2))],
        compiler_params=pltpu.CompilerParams(collective_id=2, has_side_effects=True, vmem_limit_bytes=60 << 20),
        name="reduce",
    )(*views)


def sequence_table(lengths, own, rows):
    ids = jnp.arange(lengths.shape[0], dtype=jnp.int32)
    starts = jnp.sum(jnp.where(ids[None, :] < ids[:, None], lengths[None, :], 0), axis=1)
    blocks = rows // GRAN
    at = own * rows + jnp.arange(blocks, dtype=jnp.int32) * GRAN
    inside = (starts[None, :] <= at[:, None]) & (at[:, None] < (starts + lengths)[None, :])
    first = jnp.sum(jnp.where(inside, starts[None, :], 0), axis=1)
    length = jnp.sum(jnp.where(inside, lengths[None, :], 0), axis=1)
    lead = (first == at) | (jnp.arange(blocks) == 0)
    return jnp.stack([(first - own * rows + HALO) // GRAN, jnp.where(lead, length // GRAN, 0)]).astype(jnp.int32)


def halo(x, n):
    right = [(i, i + 1) for i in range(n - 1)]
    left = [(i + 1, i) for i in range(n - 1)]
    return lax.ppermute(x[-HALO:], "dp", right), lax.ppermute(x[:HALO], "dp", left)


def pack(values, n, rows, dtype):
    cols = [v.reshape(n, -1) for v in values]
    flat = jnp.concatenate(cols, axis=1)
    return jnp.pad(flat, ((0, 0), (0, rows * 256 - flat.shape[1]))).astype(dtype).reshape(n * rows, 256)


def unpack(packed, n, part):
    flat = packed.reshape(n, -1)
    vec = flat[:, : 8 * part].reshape(n, 8, part).transpose(1, 0, 2).reshape(8, n * part)
    return vec, flat[:, 8 * part:12 * part].reshape(1, -1)


def local(tokens, cotangent, lengths, dealing, *shards):
    n = lax.axis_size("dp")
    own = lax.axis_index("dp")
    rows, d = tokens.shape
    part = d // n
    qb, vb, ob, ub, db, fg, fs, sg, ss = shards[6:]
    packed = pack([qb, vb, ob, db, fg, fs, sg, ss, ub], 1, 16, BF16)
    packed, wq, wk, wv, wo, wu, wd, xl, xr = gather_call(n, [packed] + list(shards[:6]), tokens)
    vec, bu = unpack(packed.astype(F32), n, part)
    tab = sequence_table(lengths, own, rows)
    q, k, v = qkv_call(xl, tokens, xr, wq, wk, wv, vec)
    ctx = attn_fwd_call(tab, q, k, v, rows)
    xhat, low, r1 = out_proj_call(ctx, wo, tokens, vec)
    hid, dg, layer_out, gs, sums2 = ffn_fwd_call(low, wu, bu, wd, xhat, cotangent, vec)
    dwd, dwu, gsf, sums1, sumu = ffn_bwd_call(low, gs, hid, dg, wu, wd, xhat, r1, vec)
    gc, dwo = out_bwd_call(gsf, ctx, wo)
    gl, gr = halo(gc, n)
    dq, dk, dv = attn_bwd_call(tab, q, k, v, gl, gc, gr)
    tg, dwq, dwk, dwv, sums0 = in_bwd_call(tokens, gsf, dq, dk, dv, wq, wk, wv)
    small = pack([sums0[0], sums0[1], sums1[2], sums2[2], sums1[0], sums1[1], sums2[0], sums2[1], sumu], n, 8, F32)
    tiny, gd, gu, go, gq, gk, gv = reduce_call(n, [small, dwd, dwu, dwo, dwq, dwk, dwv], d)
    vecs, ubg = unpack(tiny, 1, part)
    t = [vecs[i] for i in range(8)]
    return (layer_out, tg, gq, gk, gv, go, gu, gd, t[0], t[1], t[2], ubg[0], t[3], t[4], t[5], t[6], t[7])


def solution(mesh):
    mat = P("dp", None)
    vec = P("dp")
    return jax.shard_map(
        local,
        mesh=mesh,
        in_specs=(mat, mat, P(), P()) + (mat,) * 6 + (vec,) * 9,
        out_specs=(mat,) * 8 + (vec,) * 9,
        check_vma=False,
    )
```

```python
import functools

import jax
import jax.numpy as jnp
from jax import lax
from jax.experimental import pallas as pl
from jax.experimental.pallas import tpu as pltpu
from jax.sharding import PartitionSpec as P

HD = 64
GRAN = 128
HALO = 384
EPS = 1e-12
F32 = jnp.float32
BF16 = jnp.bfloat16
NT = (((1,), (1,)), ((), ()))
MESH = pl.DeviceIdType.MESH
ANY = pl.BlockSpec(memory_space=pl.ANY)


def params(limit=56):
    return pltpu.CompilerParams(vmem_limit_bytes=limit << 20)


def whole(shape):
    return pl.BlockSpec(shape, lambda *_: (0,) * len(shape))


def dot(a, b):
    return jnp.dot(a, b, preferred_element_type=F32)


def dot_nt(a, b):
    return lax.dot_general(a, b, NT, preferred_element_type=F32)


def cost(flops, nbytes, trans=0):
    return pl.CostEstimate(flops=flops, bytes_accessed=nbytes, transcendentals=trans)


def qkv_kernel(xl, xo, xr, wq, wk, wv, vec, q, k, v, x):
    rows = xo.shape[0]

    @pl.when(pl.program_id(0) == 0)
    def _():
        x[pl.ds(0, HALO), :] = xl[...]
        x[pl.ds(HALO, rows), :] = xo[...]
        x[pl.ds(HALO + rows, HALO), :] = xr[...]

    q[...] = (dot(x[...], wq[...]) + vec[0:1, :]).astype(BF16)
    k[...] = dot(x[...], wk[...]).astype(BF16)
    v[...] = (dot(x[...], wv[...]) + vec[1:2, :]).astype(BF16)


def qkv_call(xl, xo, xr, wq, wk, wv, vec):
    rows, d = xo.shape
    win = rows + 2 * HALO
    tn = 256
    wspec = pl.BlockSpec((d, tn), lambda j: (0, j))
    ospec = pl.BlockSpec((win, tn), lambda j: (0, j))
    out = jax.ShapeDtypeStruct((win, d), BF16)
    return pl.pallas_call(
        qkv_kernel,
        grid=(d // tn,),
        in_specs=[whole(xl.shape), whole(xo.shape), whole(xr.shape), wspec, wspec, wspec,
                  pl.BlockSpec((8, tn), lambda j: (0, j))],
        out_specs=[ospec] * 3,
        out_shape=[out] * 3,
        scratch_shapes=[pltpu.VMEM((win, d), BF16)],
        compiler_params=params(),
        cost_estimate=cost(6 * win * d * d, 2 * (4 * win * d + 3 * d * d)),
        name="qkv",
    )(xl, xo, xr, wq, wk, wv, vec)


LANES = 512
TOGETHER = {1: 4, 2: 2, 3: 1, 4: 1}


def sequences(tab, blocks, fn):
    def one(b, c):
        n = tab[1, b]
        s0 = tab[0, b]
        for nn in range(1, 5):
            @pl.when(n == nn)
            def _():
                rows = pl.ds(pl.multiple_of(s0 * GRAN, GRAN), nn * GRAN)
                per = TOGETHER[nn]

                def group(i, c):
                    pairs = [i * per + j for j in range(per)]
                    fn(rows, [(pl.ds(pl.multiple_of(p * 2 * HD, 2 * HD), 2 * HD), 2 * p) for p in pairs])
                    return c

                lax.fori_loop(0, LANES // (2 * HD) // per, group, 0)
        return c

    lax.fori_loop(0, blocks, one, 0)


def masks(shape):
    low = lax.broadcasted_iota(jnp.int32, shape, 1) < HD
    return low, ~low


def eighth(x):
    return x * jnp.asarray(0.125, BF16)


def attn_fwd_kernel(tab, q_ref, k_ref, v_ref, o_ref, lse_ref, ctx):
    def work(rows, pairs):
        mine = masks((rows.size, 2 * HD))
        st = []
        for c, h in pairs:
            q, k = eighth(q_ref[rows, c]), k_ref[rows, c]
            st += [dot_nt(k, jnp.where(m, q, jnp.zeros_like(q))) for m in mine]
        top = [jnp.max(s, axis=0, keepdims=True) for s in st]
        e = [jnp.exp(s - m) for s, m in zip(st, top)]
        total = [jnp.sum(x, axis=0, keepdims=True) for x in e]
        for i, (c, h) in enumerate(pairs):
            vt = v_ref[rows, c].T
            parts = []
            for j in range(2):
                x = 2 * i + j
                parts.append(dot(vt[j * HD:(j + 1) * HD, :], e[x].astype(BF16)) * (1.0 / total[x]))
                lse_ref[pl.ds(h + j, 1), rows] = top[x] + jnp.log(total[x])
            ctx[rows, c] = jnp.concatenate(parts, axis=0).T.astype(BF16)

    sequences(tab, o_ref.shape[0] // GRAN, work)
    o_ref[...] = ctx[pl.ds(HALO, o_ref.shape[0]), :]


def attn_fwd_call(tab, q, k, v, rows):
    win, d = q.shape
    spec = pl.BlockSpec((win, LANES), lambda h, t: (0, h))
    return pl.pallas_call(
        attn_fwd_kernel,
        grid_spec=pltpu.PrefetchScalarGridSpec(
            num_scalar_prefetch=1,
            grid=(d // LANES,),
            in_specs=[spec] * 3,
            out_specs=[pl.BlockSpec((rows, LANES), lambda h, t: (0, h)), pl.BlockSpec((LANES // HD, win), lambda h, t: (h, 0))],
            scratch_shapes=[pltpu.VMEM((win, LANES), BF16)],
        ),
        out_shape=[jax.ShapeDtypeStruct((rows, d), BF16), jax.ShapeDtypeStruct((d // HD, win), F32)],
        compiler_params=params(),
        cost_estimate=cost(8 * rows * 512 * d, 8 * win * d, rows * 512 * 16),
        name="attn_fwd",
    )(tab, q, k, v)


def attn_bwd_kernel(tab, q_ref, k_ref, v_ref, lse_ref, gl, go, gr, dq_o, dk_o, dv_o, g_s, dq_s, dk_s, dv_s):
    rows_own = go.shape[0]
    g_s[pl.ds(0, HALO), :] = gl[...]
    g_s[pl.ds(HALO, rows_own), :] = go[...]
    g_s[pl.ds(HALO + rows_own, HALO), :] = gr[...]

    def work(rows, pairs):
        mine = masks((rows.size, 2 * HD))
        qs, gs, p, dp = [], [], [], []
        for c, h in pairs:
            q, k, v, g = eighth(q_ref[rows, c]), k_ref[rows, c], v_ref[rows, c], g_s[rows, c]
            zero = jnp.zeros_like(q)
            for j, m in enumerate(mine):
                st = dot_nt(k, jnp.where(m, q, zero))
                p.append(jnp.exp(st - lse_ref[pl.ds(h + j, 1), rows]))
                dp.append(dot_nt(v, jnp.where(m, g, zero)))
            qs.append(q)
            gs.append(g)
        delta = [jnp.sum(a * b, axis=0, keepdims=True) for a, b in zip(p, dp)]
        ds = [(a * (b - d)).astype(BF16) for a, b, d in zip(p, dp, delta)]
        for i, (c, h) in enumerate(pairs):
            kt = eighth(k_ref[rows, c]).T
            dq = [dot(kt[j * HD:(j + 1) * HD, :], ds[2 * i + j]) for j in range(2)]
            dk = [dot(ds[2 * i + j], qs[i]) for j in range(2)]
            dv = [dot(p[2 * i + j].astype(BF16), gs[i]) for j in range(2)]
            dq_s[rows, c] = jnp.concatenate(dq, axis=0).T.astype(BF16)
            dk_s[rows, c] = jnp.where(mine[0], dk[0], dk[1]).astype(BF16)
            dv_s[rows, c] = jnp.where(mine[0], dv[0], dv[1]).astype(BF16)

    sequences(tab, rows_own // GRAN, work)
    own = pl.ds(HALO, rows_own)
    dq_o[...] = dq_s[own, :]
    dk_o[...] = dk_s[own, :]
    dv_o[...] = dv_s[own, :]


def attn_bwd_call(tab, q, k, v, lse, gl, go, gr):
    win, d = q.shape
    rows = go.shape[0]
    spec = pl.BlockSpec((win, LANES), lambda h, t: (0, h))
    own = pl.BlockSpec((rows, LANES), lambda h, t: (0, h))
    halo = pl.BlockSpec((HALO, LANES), lambda h, t: (0, h))
    out = jax.ShapeDtypeStruct((rows, d), BF16)
    return pl.pallas_call(
        attn_bwd_kernel,
        grid_spec=pltpu.PrefetchScalarGridSpec(
            num_scalar_prefetch=1,
            grid=(d // LANES,),
            in_specs=[spec] * 3 + [pl.BlockSpec((LANES // HD, win), lambda h, t: (h, 0)), halo, own, halo],
            out_specs=[own] * 3,
            scratch_shapes=[pltpu.VMEM((win, LANES), BF16)] * 4,
        ),
        out_shape=[out] * 3,
        compiler_params=params(),
        cost_estimate=cost(20 * rows * 512 * d, 14 * win * d, rows * 512 * 16),
        name="attn_bwd",
    )(tab, q, k, v, lse, gl, go, gr)


def norm_stats(z):
    cen = z - jnp.mean(z, axis=-1, keepdims=True)
    r = lax.rsqrt(jnp.mean(cen * cen, axis=-1, keepdims=True) + EPS)
    return cen * r, r


def norm_back(e, n, r):
    return r * (e - jnp.mean(e, axis=-1, keepdims=True) - n * jnp.mean(e * n, axis=-1, keepdims=True))


RC = 256
TF = 512
TC = 256


def chunks(rows, fn):
    def step(i, c):
        fn(pl.ds(pl.multiple_of(i * RC, RC), RC))
        return c

    lax.fori_loop(0, rows // RC, step, 0)


def clip(t, first, count):
    return jnp.clip(t - first, 0, count - 1)


def lanes(t, size):
    return pl.ds(pl.multiple_of(t * size, size), size)


def colsum(v):
    return jnp.sum(v, axis=0, keepdims=True)


def gelu_parts(u):
    phi = 0.5 * (1.0 + lax.erf(u * (0.5 ** 0.5)))
    return u * phi, phi + u * (0.3989422804014327 * jnp.exp(-0.5 * u * u))


def fwd_kernel(nu, nc, ctx, wo, x, wu, bu, wd, g, vec, xhat, low, r1, hidt, dg, out, gs, sums, z, hid):
    t = pl.program_id(0)
    rows = x.shape[0]

    @pl.when(t < nc)
    def _():
        c = lanes(t, TC)
        z[:, c] = dot(ctx[...], wo[...]) + x[:, c].astype(F32)

    @pl.when(t == nc - 1)
    def _():
        def fin(r):
            n, rr = norm_stats(z[r, :] + vec[2:3, :])
            xhat[r, :] = n
            r1[r, :] = jnp.broadcast_to(rr, (RC, r1.shape[1]))
            low[r, :] = (n * vec[4:5, :] + vec[5:6, :]).astype(BF16)

        chunks(rows, fin)

    @pl.when((t >= nc) & (t < nc + nu))
    def _():
        for j in range(TF // TC):
            c = slice(j * TC, (j + 1) * TC)
            h, s = gelu_parts(dot(low[...], wu[:, c]) + bu[:, c])
            h = h.astype(BF16)
            dg[:, c] = s.astype(BF16)
            hid[:, lanes((t - nc) * (TF // TC) + j, TC)] = h
            hidt[c, :] = h.T

    @pl.when(t >= nc + nu)
    def _():
        c = lanes(t - nc - nu, TC)
        z[:, c] = dot(hid[...], wd[...])

    @pl.when(t == 2 * nc + nu - 1)
    def _():
        sums[...] = jnp.zeros_like(sums)

        def fin(r):
            v = (xhat[r, :] * vec[4:5, :] + vec[5:6, :]) + (z[r, :] + vec[3:4, :])
            n, rr = norm_stats(v)
            out[r, :] = (n * vec[6:7, :] + vec[7:8, :]).astype(BF16)
            gv = g[r, :].astype(F32)
            sums[0:1, :] += colsum(gv * n)
            sums[1:2, :] += colsum(gv)
            grad = norm_back(gv * vec[6:7, :], n, rr)
            gs[r, :] = grad
            sums[2:3, :] += colsum(grad.astype(BF16).astype(F32))

        chunks(rows, fin)


def single(shape):
    return pl.BlockSpec(shape, lambda *_: (0,) * len(shape), pipeline_mode=pl.Buffered(1))


def fwd_call(ctx, wo, x, wu, bu, wd, g, vec):
    rows, d = x.shape
    ff = wu.shape[1]
    nu, nc = ff // TF, d // TC
    return pl.pallas_call(
        functools.partial(fwd_kernel, nu, nc),
        grid=(2 * nc + nu,),
        in_specs=[single(ctx.shape), pl.BlockSpec((d, TC), lambda t: (0, clip(t, 0, nc))), single(x.shape),
                  pl.BlockSpec((d, TF), lambda t: (0, clip(t, nc, nu))), pl.BlockSpec((1, TF), lambda t: (0, clip(t, nc, nu))),
                  pl.BlockSpec((ff, TC), lambda t: (0, clip(t, nc + nu, nc))), single(g.shape), single(vec.shape)],
        out_specs=[single((rows, d)), single((rows, d)), single((rows, 128)),
                   pl.BlockSpec((TF, rows), lambda t: (clip(t, nc, nu), 0)), pl.BlockSpec((rows, TF), lambda t: (0, clip(t, nc, nu))),
                   single((rows, d)), single((rows, d)), single((8, d))],
        out_shape=[jax.ShapeDtypeStruct((rows, d), F32), jax.ShapeDtypeStruct((rows, d), BF16),
                   jax.ShapeDtypeStruct((rows, 128), F32), jax.ShapeDtypeStruct((ff, rows), BF16),
                   jax.ShapeDtypeStruct((rows, ff), BF16), jax.ShapeDtypeStruct((rows, d), BF16),
                   jax.ShapeDtypeStruct((rows, d), F32), jax.ShapeDtypeStruct((8, d), F32)],
        scratch_shapes=[pltpu.VMEM((rows, d), F32), pltpu.VMEM((rows, ff), BF16)],
        compiler_params=params(60),
        cost_estimate=cost(4 * rows * d * ff, 4 * d * ff + 4 * rows * ff + rows * d * 14, 2 * rows * ff),
        name="fwd",
    )(ctx, wo, x, wu, bu, wd, g, vec)


def bwd_kernel(nu, nc, low, gs, hidt, dg, wu, wd, xhat, r1, ctx, wo, vec, dwd, dwu, gsf, sums, sumu, gc, dwo, gd, lowt, gu, z, ctxt, ga):
    t = pl.program_id(0)
    rows = low.shape[0]

    @pl.when(t == 0)
    def _():
        gd[...] = gs[...].astype(BF16)
        lowt[...] = low[...].T
        ctxt[...] = ctx[...].T

    @pl.when(t < nu)
    def _():
        for j in range(TF // TC):
            c = slice(j * TC, (j + 1) * TC)
            g = (dot_nt(gd[...], wd[c, :]) * dg[:, c].astype(F32)).astype(BF16)
            gu[:, lanes(t * (TF // TC) + j, TC)] = g
            sumu[:, c] = colsum(g.astype(F32))
            dwu[:, c] = dot(lowt[...], g).astype(BF16)
        dwd[...] = dot(hidt[...], gd[...]).astype(BF16)

    @pl.when((t >= nu) & (t < nu + nc))
    def _():
        c = lanes(t - nu, TC)
        z[:, c] = gs[:, c] + dot_nt(gu[...], wu[...])

    @pl.when(t == nu + nc - 1)
    def _():
        sums[...] = jnp.zeros_like(sums)

        def fin(r):
            gf = z[r, :]
            n = xhat[r, :]
            sums[0:1, :] += colsum(gf * n)
            sums[1:2, :] += colsum(gf)
            grad = norm_back(gf * vec[4:5, :], n, r1[r, 0:1])
            gsf[r, :] = grad
            low_g = grad.astype(BF16)
            ga[r, :] = low_g
            sums[2:3, :] += colsum(low_g.astype(F32))

        chunks(rows, fin)

    @pl.when(t >= nu + nc)
    def _():
        c = lanes(t - nu - nc, TC)
        gc[...] = dot_nt(ga[...], wo[...]).astype(BF16)
        dwo[...] = dot(ctxt[...], ga[:, c]).astype(BF16)


def bwd_call(low, gs, hidt, dg, wu, wd, xhat, r1, ctx, wo, vec):
    rows, d = low.shape
    ff = wu.shape[1]
    nu, nc = ff // TF, d // TC

    def up(t):
        return clip(t, 0, nu)

    def last(t):
        return clip(t, nu + nc, nc)

    return pl.pallas_call(
        functools.partial(bwd_kernel, nu, nc),
        grid=(nu + 2 * nc,),
        in_specs=[single(low.shape), single(gs.shape), pl.BlockSpec((TF, rows), lambda t: (up(t), 0)),
                  pl.BlockSpec((rows, TF), lambda t: (0, up(t))), pl.BlockSpec((TC, ff), lambda t: (clip(t, nu, nc), 0)),
                  pl.BlockSpec((TF, d), lambda t: (up(t), 0)), single(xhat.shape), single(r1.shape), single(ctx.shape),
                  pl.BlockSpec((TC, d), lambda t: (last(t), 0)), single(vec.shape)],
        out_specs=[pl.BlockSpec((TF, d), lambda t: (up(t), 0)), pl.BlockSpec((d, TF), lambda t: (0, up(t))), single((rows, d)),
                   single((8, d)), pl.BlockSpec((1, TF), lambda t: (0, up(t))), pl.BlockSpec((rows, TC), lambda t: (0, last(t))),
                   pl.BlockSpec((d, TC), lambda t: (0, last(t)))],
        out_shape=[jax.ShapeDtypeStruct((ff, d), BF16), jax.ShapeDtypeStruct((d, ff), BF16),
                   jax.ShapeDtypeStruct((rows, d), F32), jax.ShapeDtypeStruct((8, d), F32),
                   jax.ShapeDtypeStruct((1, ff), F32), jax.ShapeDtypeStruct((rows, d), BF16), jax.ShapeDtypeStruct((d, d), BF16)],
        scratch_shapes=[pltpu.VMEM((rows, d), BF16), pltpu.VMEM((d, rows), BF16), pltpu.VMEM((rows, ff), BF16),
                        pltpu.VMEM((rows, d), F32), pltpu.VMEM((d, rows), BF16), pltpu.VMEM((rows, d), BF16)],
        compiler_params=params(60),
        cost_estimate=cost(8 * rows * d * ff, 8 * d * ff + 4 * rows * ff + rows * d * 18),
        name="bwd",
    )(low, gs, hidt, dg, wu, wd, xhat, r1, ctx, wo, vec)


def in_bwd_kernel(x, gsf, dq, dk, dv, wq, wk, wv, tg, dwq, dwk, dwv, sums, xt):
    t = pl.program_id(0)

    @pl.when(t == 0)
    def _():
        xt[...] = x[...].T

    c = lanes(t, TC)
    g = gsf[...] + dot_nt(dq[...], wq[...]) + dot_nt(dk[...], wk[...]) + dot_nt(dv[...], wv[...])
    tg[...] = g.astype(BF16)
    sums[0:1, :] = colsum(dq[:, c].astype(F32))
    sums[1:2, :] = colsum(dv[:, c].astype(F32))
    for a, o in ((dq, dwq), (dk, dwk), (dv, dwv)):
        o[...] = dot(xt[...], a[:, c]).astype(BF16)


def in_bwd_call(x, gsf, dq, dk, dv, wq, wk, wv):
    rows, d = x.shape
    col = pl.BlockSpec((rows, TC), lambda t: (0, t))
    wcol = pl.BlockSpec((d, TC), lambda t: (0, t))
    return pl.pallas_call(
        in_bwd_kernel,
        grid=(d // TC,),
        in_specs=[single((rows, d)), col] + [single((rows, d))] * 3 + [pl.BlockSpec((TC, d), lambda t: (t, 0))] * 3,
        out_specs=[col] + [wcol] * 3 + [pl.BlockSpec((8, TC), lambda t: (0, t))],
        out_shape=[jax.ShapeDtypeStruct((rows, d), BF16)] + [jax.ShapeDtypeStruct((d, d), BF16)] * 3
        + [jax.ShapeDtypeStruct((8, d), F32)],
        scratch_shapes=[pltpu.VMEM((d, rows), BF16)],
        compiler_params=params(),
        cost_estimate=cost(12 * rows * d * d, rows * d * 14 + 12 * d * d),
        name="in_bwd",
    )(x, gsf, dq, dk, dv, wq, wk, wv)


def grid_of(n):
    chips = n // 2
    return {16: (4, 2, 2), 64: (4, 4, 4)}.get(chips, (chips, 1, 1))


class Place:
    def __init__(self, n):
        self.n = n
        self.size = grid_of(n)
        me = lax.axis_index("dp")
        nz, ny, nx = self.size
        self.me = me
        self.c = lax.rem(me, 2)
        self.x = lax.rem(me // 2, nx)
        self.y = lax.rem(me // (2 * nx), ny)
        self.z = me // (2 * nx * ny)

    def at(self, axis, k):
        nz, ny, nx = self.size
        z, y, x, c = self.z, self.y, self.x, self.c
        if axis == "z":
            z = lax.rem(z + k, nz)
        elif axis == "y":
            y = lax.rem(y + k, ny)
        elif axis == "x":
            x = lax.rem(x + k, nx)
        else:
            c = lax.rem(c + k, 2)
        pos = {"z": z, "y": y, "x": x, "c": c}[axis]
        return ((z * ny + y) * nx + x) * 2 + c, pos

    def steps(self, axis):
        nz, ny, nx = self.size
        return range(1, {"z": nz, "y": ny, "x": nx, "c": 2}[axis])

    def peers(self):
        return [self.at(a, k)[0] for a in "zyxc" for k in self.steps(a)]


def enter(peers):
    sem = pltpu.get_barrier_semaphore()
    for p in peers:
        pl.semaphore_signal(sem, inc=1, device_id=(p,), device_id_type=MESH)
    pl.semaphore_wait(sem, len(peers))


def gather_slots(n):
    nz, ny, nx = grid_of(n)
    return (nz - 1) + 2 * (ny - 1) + 2 * (nx - 1) + 1


class Gather:
    def __init__(self, place, src, dst, rows, cols, ssem, rsem, lsem, index):
        self.p, self.index = place, index
        self.src, self.dst, self.rows, self.cols = src, dst, rows, cols
        self.ssem, self.rsem, self.lsem = ssem, rsem, lsem
        p = place
        r0, nr = rows
        c0, nc = cols
        rs = pl.ds(r0, nr)
        full = pl.ds(c0, nc)
        halves = (pl.ds(c0, nc // 2), pl.ds(c0 + nc // 2, nc // 2))
        al = pl.ds(0, p.size[0])
        self.local = pltpu.make_async_copy(src.at[rs, full], dst.at[p.z, p.y, p.x, p.c, rs, full], lsem.at[index])
        slot = 0

        def copy(s, d, dev):
            nonlocal slot
            cp = pltpu.make_async_remote_copy(src_ref=s, dst_ref=d, send_sem=ssem.at[index, slot], recv_sem=rsem.at[index, slot],
                                              device_id=(dev,), device_id_type=MESH)
            slot += 1
            return cp

        mine = dst.at[p.z, p.y, p.x, p.c, rs, full]
        self.ph = [[], [], [], []]
        for k in p.steps("z"):
            self.ph[0].append(copy(src.at[rs, full], mine, p.at("z", k)[0]))
        for h, axis in ((0, "y"), (1, "x")):
            s = dst.at[:, p.y, p.x, p.c, rs, halves[h]]
            for k in p.steps(axis):
                self.ph[1].append(copy(s, s, p.at(axis, k)[0]))
        for h, axis in ((0, "x"), (1, "y")):
            s = dst.at[:, :, p.x, p.c, rs, halves[0]] if h == 0 else dst.at[:, p.y, :, p.c, rs, halves[1]]
            for k in p.steps(axis):
                self.ph[2].append(copy(s, s, p.at(axis, k)[0]))
        s = dst.at[:, :, :, p.c, rs, full]
        self.ph[3].append(copy(s, s, p.at("c", 1)[0]))

    def start(self, i):
        if i == 0:
            self.local.start()
        for cp in self.ph[i]:
            cp.start()

    def wait(self, i):
        if i == 0:
            self.local.wait()
        for cp in self.ph[i]:
            cp.wait_recv()

    def sent(self):
        for ph in self.ph:
            for cp in ph:
                cp.wait_send()


def gather_kernel(n, plan, nsrc, *refs):
    srcs, xsrc, outs = refs[:nsrc], refs[nsrc], refs[nsrc + 1:2 * nsrc + 1]
    xl, xr = refs[2 * nsrc + 1:2 * nsrc + 3]
    ssem, rsem, lsem, hs, hr = refs[2 * nsrc+3:]
    p = Place(n)
    right, left = lax.rem(p.me + 1, n), lax.rem(p.me + n - 1, n)
    enter(p.peers() + [left, right])
    rows = xsrc.shape[0]
    halo = [pltpu.make_async_remote_copy(src_ref=xsrc.at[pl.ds(rows-HALO,HALO),:], dst_ref=xl, send_sem=hs.at[0], recv_sem=hr.at[0], device_id=(right,), device_id_type=MESH),
            pltpu.make_async_remote_copy(src_ref=xsrc.at[pl.ds(0,HALO),:], dst_ref=xr, send_sem=hs.at[1], recv_sem=hr.at[1], device_id=(left,), device_id_type=MESH)]
    for h in halo: h.start()
    g = [Gather(p, srcs[a], outs[a], r, c, ssem, rsem, lsem, i) for i, (a, r, c) in enumerate(plan)]
    for s in range(len(g) + 4):
        for ph in (0, 1, 2, 3, 4):
            i = s - ph
            if 0 <= i < len(g):
                if ph > 0:
                    g[i].wait(ph - 1)
                if ph < 4:
                    g[i].start(ph)
    for c in g:
        c.sent()
    for h in halo: h.wait()


def gather_plan(shards, d):
    least = min(s.shape[0] for s in shards if s.shape[-1] >= d)
    plan = []
    for a, s in enumerate(shards):
        if s.shape[1] < d:
            plan.append((a, (0, s.shape[0]), (0, s.shape[1])))
            continue
        for j in range(s.shape[1] // d):
            for i in range(s.shape[0] // least):
                plan.append((a, (i * least, least), (j * d, d)))
    return plan


def gather_call(n, shards, tokens, order=None):
    d = tokens.shape[1]
    plan = gather_plan(shards, d)
    k = gather_slots(n)
    outs = [jax.ShapeDtypeStruct(grid_of(n) + (2,) + s.shape, s.dtype) for s in shards]
    halo = jax.ShapeDtypeStruct((HALO, d), tokens.dtype)
    res = pl.pallas_call(
        functools.partial(gather_kernel, n, plan, len(shards)),
        in_specs=[ANY] * (len(shards)+1),
        out_specs=[ANY] * (len(shards)+2),
        out_shape=outs+[halo,halo],
        scratch_shapes=[pltpu.SemaphoreType.DMA((len(plan), k)), pltpu.SemaphoreType.DMA((len(plan), k)),
                        pltpu.SemaphoreType.DMA((len(plan),)),pltpu.SemaphoreType.DMA((2,)),pltpu.SemaphoreType.DMA((2,))],
        compiler_params=pltpu.CompilerParams(collective_id=1, has_side_effects=True),
        name="gather",
    )(*shards, tokens)
    return [r.reshape((n * s.shape[0],) + s.shape[1:]) for r, s in zip(res, shards)] + list(res[-2:])


def reduce_slots(n):
    nz, ny, nx = grid_of(n)
    return (nz - 1) + 2 * (ny - 1) + 2 * (nx - 1) + 1


def landing(n, r, cols, dtype):
    nz, ny, nx = grid_of(n)
    h = cols // 2
    return [pltpu.VMEM((nz, ny, nx, r, cols), dtype),
            pltpu.VMEM((max(nx - 1, 1), nz, ny, r, h), dtype), pltpu.VMEM((max(ny - 1, 1), nz, nx, r, h), dtype),
            pltpu.VMEM((max(ny - 1, 1), nz, r, h), dtype), pltpu.VMEM((max(nx - 1, 1), nz, r, h), dtype),
            pltpu.VMEM((max(nz - 1, 1), r, cols), dtype)]


def partial(n, r, cols, dtype):
    nz, ny, nx = grid_of(n)
    h = cols // 2
    return [pltpu.VMEM((nz, ny, nx, r, cols), dtype), pltpu.VMEM((nz, ny, r, h), dtype), pltpu.VMEM((nz, nx, r, h), dtype),
            pltpu.VMEM((nz, r, cols), dtype), pltpu.VMEM((r, cols), F32)]


class Reduce:
    def __init__(self, place, src, land, part, out, ssem, rsem, lsem, index):
        self.p, self.src, self.land, self.part, self.out = place, src, land, part, out
        p = place
        self.h = part[3].shape[-1] // 2
        self.ca, self.cb = pl.ds(0, self.h), pl.ds(self.h, self.h)
        self.get = pltpu.make_async_copy(src.at[:, :, :, p.c], part[0], lsem.at[index, 0])
        self.put = pltpu.make_async_copy(part[4], out, lsem.at[index, 1])
        slot = 0

        def copy(s, d, dev):
            nonlocal slot
            cp = pltpu.make_async_remote_copy(src_ref=s, dst_ref=d, send_sem=ssem.at[index, slot], recv_sem=rsem.at[index, slot],
                                              device_id=(dev,), device_id_type=MESH)
            slot += 1
            return cp

        self.ph = [[], [], [], []]
        dev, oc = p.at("c", 1)
        self.ph[0].append(copy(src.at[:, :, :, oc], land[0], dev))
        for k in p.steps("x"):
            dev, o = p.at("x", k)
            self.ph[1].append(copy(part[0].at[:, :, o, :, self.ca], land[1].at[k - 1], dev))
        for k in p.steps("y"):
            dev, o = p.at("y", k)
            self.ph[1].append(copy(part[0].at[:, o, :, :, self.cb], land[2].at[k - 1], dev))
        for k in p.steps("y"):
            dev, o = p.at("y", k)
            self.ph[2].append(copy(part[1].at[:, o], land[3].at[k - 1], dev))
        for k in p.steps("x"):
            dev, o = p.at("x", k)
            self.ph[2].append(copy(part[2].at[:, o], land[4].at[k - 1], dev))
        for k in p.steps("z"):
            dev, o = p.at("z", k)
            self.ph[3].append(copy(part[3].at[o], land[5].at[k - 1], dev))

    def begin(self):
        self.get.start()
        self.ph[0][0].start()

    def go(self, i):
        p, land, part = self.p, self.land, self.part
        nz, ny, nx = p.size
        dt = part[0].dtype
        for cp in self.ph[i - 1]:
            cp.wait_recv()
        if i == 1:
            self.get.wait()

            def add(z, c):
                part[0][z] = (part[0][z].astype(F32) + land[0][z].astype(F32)).astype(dt)
                return c

            lax.fori_loop(0, nz, add, 0)
        elif i == 2:
            def add(z, c):
                a = part[0][z, :, pl.ds(p.x, 1), :, self.ca].astype(F32)[:, 0]
                for k in range(nx - 1):
                    a += land[1][k, z].astype(F32)
                part[1][z] = a.astype(dt)
                b = part[0][z, pl.ds(p.y, 1), :, :, self.cb].astype(F32)[0]
                for k in range(ny - 1):
                    b += land[2][k, z].astype(F32)
                part[2][z] = b.astype(dt)
                return c

            lax.fori_loop(0, nz, add, 0)
        elif i == 3:
            a = part[1][:, pl.ds(p.y, 1)].astype(F32)[:, 0]
            for k in range(ny - 1):
                a += land[3][k].astype(F32)
            part[3][:, :, self.ca] = a.astype(dt)
            b = part[2][:, pl.ds(p.x, 1)].astype(F32)[:, 0]
            for k in range(nx - 1):
                b += land[4][k].astype(F32)
            part[3][:, :, self.cb] = b.astype(dt)
        else:
            a = part[3][pl.ds(p.z, 1)].astype(F32)[0]
            for k in range(nz - 1):
                a += land[5][k].astype(F32)
            part[4][...] = a
            self.put.start()
            return
        for cp in self.ph[i]:
            cp.start()

    def finish(self):
        self.put.wait()
        for ph in self.ph:
            for cp in ph:
                cp.wait_send()


def reduce_kernel(n, plan, nsrc, *refs):
    srcs, outs = refs[:nsrc], refs[nsrc:2 * nsrc]
    scratch = refs[2 * nsrc:]
    ssem, rsem, lsem = scratch[-3:]
    p = Place(n)
    enter(p.peers())
    red = []
    for i, (a, (r0, nr), (c0, nc)) in enumerate(plan):
        land, part = scratch[11 * i:11 * i + 6], scratch[11 * i + 6:11 * i + 11]
        rs, cs = pl.ds(r0, nr), pl.ds(c0, nc)
        red.append(Reduce(p, srcs[a].at[:, :, :, :, rs, cs], land, part, outs[a].at[rs, cs], ssem, rsem, lsem, i))
    for s in range(len(red) + 5):
        for ph in (0, 1, 2, 3, 4, 5):
            i = s - ph
            if 0 <= i < len(red):
                if ph == 0:
                    red[i].begin()
                elif ph < 5:
                    red[i].go(ph)
                else:
                    red[i].finish()


def reduce_call(n, grads, d):
    views = [g.reshape(grid_of(n) + (2, g.shape[0] // n) + g.shape[1:]) for g in grads]
    plan = gather_plan([jax.ShapeDtypeStruct(v.shape[4:], v.dtype) for v in views], d)
    k = reduce_slots(n)
    scratch = []
    for a, r, c in plan:
        scratch += landing(n, r[1], c[1], grads[a].dtype) + partial(n, r[1], c[1], grads[a].dtype)
    return pl.pallas_call(
        functools.partial(reduce_kernel, n, plan, len(grads)),
        in_specs=[ANY] * len(grads),
        out_specs=[ANY] * len(grads),
        out_shape=[jax.ShapeDtypeStruct(v.shape[4:], F32) for v in views],
        scratch_shapes=scratch + [pltpu.SemaphoreType.DMA((len(plan), k)), pltpu.SemaphoreType.DMA((len(plan), k)),
                                  pltpu.SemaphoreType.DMA((len(plan), 2))],
        compiler_params=pltpu.CompilerParams(collective_id=2, has_side_effects=True, vmem_limit_bytes=60 << 20),
        name="reduce",
    )(*views)


def hand_on_kernel(*refs):
    half = len(refs) // 2
    for a, b in zip(refs[:half], refs[half:]):
        b[...] = a[...]


def hand_on(arrays):
    return pl.pallas_call(
        hand_on_kernel,
        out_shape=[jax.ShapeDtypeStruct(a.shape, a.dtype) for a in arrays],
        name="hand_on",
    )(*arrays)


def sequence_table(lengths, own, rows):
    ids = jnp.arange(lengths.shape[0], dtype=jnp.int32)
    starts = jnp.sum(jnp.where(ids[None, :] < ids[:, None], lengths[None, :], 0), axis=1)
    blocks = rows // GRAN
    at = own * rows + jnp.arange(blocks, dtype=jnp.int32) * GRAN
    inside = (starts[None, :] <= at[:, None]) & (at[:, None] < (starts + lengths)[None, :])
    first = jnp.sum(jnp.where(inside, starts[None, :], 0), axis=1)
    length = jnp.sum(jnp.where(inside, lengths[None, :], 0), axis=1)
    lead = (first == at) | (jnp.arange(blocks) == 0)
    return jnp.stack([(first - own * rows + HALO) // GRAN, jnp.where(lead, length // GRAN, 0)]).astype(jnp.int32)


def halo(x, n):
    right = [(i, i + 1) for i in range(n - 1)]
    left = [(i + 1, i) for i in range(n - 1)]
    return lax.ppermute(x[-HALO:], "dp", right), lax.ppermute(x[:HALO], "dp", left)


def pack(values, n, rows, dtype):
    cols = [v.reshape(n, -1) for v in values]
    flat = jnp.concatenate(cols, axis=1)
    return jnp.pad(flat, ((0, 0), (0, rows * 256 - flat.shape[1]))).astype(dtype).reshape(n * rows, 256)


def unpack(packed, n, part):
    flat = packed.reshape(n, -1)
    vec = flat[:, : 8 * part].reshape(n, 8, part).transpose(1, 0, 2).reshape(8, n * part)
    return vec, flat[:, 8 * part:12 * part].reshape(1, -1)


def local(tokens, cotangent, lengths, dealing, *shards):
    n = lax.axis_size("dp")
    own = lax.axis_index("dp")
    rows, d = tokens.shape
    part = d // n
    qb, vb, ob, ub, db, fg, fs, sg, ss = shards[6:]
    packed = pack([qb, vb, ob, db, fg, fs, sg, ss, ub], 1, 16, BF16)
    packed, wq, wk, wv, wo, wu, wd, xl, xr = gather_call(n, [packed] + list(shards[:6]), tokens)
    vec, bu = unpack(packed.astype(F32), n, part)
    tab = sequence_table(lengths, own, rows)
    q, k, v = qkv_call(xl, tokens, xr, wq, wk, wv, vec)
    ctx, lse = attn_fwd_call(tab, q, k, v, rows)
    xhat, low, r1, hidt, dg, layer_out, gs, sums2 = fwd_call(ctx, wo, tokens, wu, bu, wd, cotangent, vec)
    dwd, dwu, gsf, sums1, sumu, gc, dwo = bwd_call(low, gs, hidt, dg, wu, wd, xhat, r1, ctx, wo, vec)
    gl, gr = halo(gc, n)
    dq, dk, dv = attn_bwd_call(tab, q, k, v, lse, gl, gc, gr)
    tg, dwq, dwk, dwv, sums0 = in_bwd_call(tokens, gsf, dq, dk, dv, wq, wk, wv)
    small = pack([sums0[0], sums0[1], sums1[2], sums2[2], sums1[0], sums1[1], sums2[0], sums2[1], sumu], n, 8, F32)
    tiny, gd, gu, go, gq, gk, gv = reduce_call(n, [small, dwd, dwu, dwo, dwq, dwk, dwv], d)
    gq, gk, gv, go, gu, gd = hand_on([gq, gk, gv, go, gu, gd])
    vecs, ubg = unpack(tiny, 1, part)
    t = [vecs[i] for i in range(8)]
    return (layer_out, tg, gq, gk, gv, go, gu, gd, t[0], t[1], t[2], ubg[0], t[3], t[4], t[5], t[6], t[7])


def solution(mesh):
    mat = P("dp", None)
    vec = P("dp")
    return jax.shard_map(
        local,
        mesh=mesh,
        in_specs=(mat, mat, P(), P()) + (mat,) * 6 + (vec,) * 9,
        out_specs=(mat,) * 8 + (vec,) * 9,
        check_vma=False,
    )
```

```python
import functools

import jax
import jax.numpy as jnp
from jax import lax
from jax.experimental import pallas as pl
from jax.experimental.pallas import tpu as pltpu
from jax.sharding import PartitionSpec as P

HD = 64
GRAN = 128
HALO = 384
EPS = 1e-12
F32 = jnp.float32
BF16 = jnp.bfloat16
NT = (((1,), (1,)), ((), ()))
MESH = pl.DeviceIdType.MESH
ANY = pl.BlockSpec(memory_space=pl.ANY)


def params(limit=56):
    return pltpu.CompilerParams(vmem_limit_bytes=limit << 20)


def whole(shape):
    return pl.BlockSpec(shape, lambda *_: (0,) * len(shape))


def dot(a, b):
    return jnp.dot(a, b, preferred_element_type=F32)


def dot_nt(a, b):
    return lax.dot_general(a, b, NT, preferred_element_type=F32)


def cost(flops, nbytes, trans=0):
    return pl.CostEstimate(flops=flops, bytes_accessed=nbytes, transcendentals=trans)


def qkv_kernel(xl, xo, xr, wq, wk, wv, vec, q, k, v, x):
    rows = xo.shape[0]

    @pl.when(pl.program_id(0) == 0)
    def _():
        x[pl.ds(0, HALO), :] = xl[...]
        x[pl.ds(HALO, rows), :] = xo[...]
        x[pl.ds(HALO + rows, HALO), :] = xr[...]

    q[...] = (dot(x[...], wq[...]) + vec[0:1, :]).astype(BF16)
    k[...] = dot(x[...], wk[...]).astype(BF16)
    v[...] = (dot(x[...], wv[...]) + vec[1:2, :]).astype(BF16)


def qkv_call(xl, xo, xr, wq, wk, wv, vec):
    rows, d = xo.shape
    win = rows + 2 * HALO
    tn = 256
    wspec = pl.BlockSpec((d, tn), lambda j: (0, j))
    ospec = pl.BlockSpec((win, tn), lambda j: (0, j))
    out = jax.ShapeDtypeStruct((win, d), BF16)
    return pl.pallas_call(
        qkv_kernel,
        grid=(d // tn,),
        in_specs=[whole(xl.shape), whole(xo.shape), whole(xr.shape), wspec, wspec, wspec,
                  pl.BlockSpec((8, tn), lambda j: (0, j))],
        out_specs=[ospec] * 3,
        out_shape=[out] * 3,
        scratch_shapes=[pltpu.VMEM((win, d), BF16)],
        compiler_params=params(),
        cost_estimate=cost(6 * win * d * d, 2 * (4 * win * d + 3 * d * d)),
        name="qkv",
    )(xl, xo, xr, wq, wk, wv, vec)


LANES = 512
TOGETHER = {1: 4, 2: 2, 3: 1, 4: 1}


def sequences(tab, blocks, fn):
    def one(b, c):
        n = tab[1, b]
        s0 = tab[0, b]
        for nn in range(1, 5):
            @pl.when(n == nn)
            def _():
                rows = pl.ds(pl.multiple_of(s0 * GRAN, GRAN), nn * GRAN)
                per = TOGETHER[nn]

                def group(i, c):
                    pairs = [i * per + j for j in range(per)]
                    fn(rows, [(pl.ds(pl.multiple_of(p * 2 * HD, 2 * HD), 2 * HD), 2 * p) for p in pairs])
                    return c

                lax.fori_loop(0, LANES // (2 * HD) // per, group, 0)
        return c

    lax.fori_loop(0, blocks, one, 0)


def masks(shape):
    low = lax.broadcasted_iota(jnp.int32, shape, 1) < HD
    return low, ~low


def eighth(x):
    return x * jnp.asarray(0.125, BF16)


def attn_fwd_kernel(tab, q_ref, k_ref, v_ref, o_ref, lse_ref, ctx):
    def work(rows, pairs):
        mine = masks((rows.size, 2 * HD))
        st = []
        for c, h in pairs:
            q, k = eighth(q_ref[rows, c]), k_ref[rows, c]
            st += [dot_nt(k, jnp.where(m, q, jnp.zeros_like(q))) for m in mine]
        top = [jnp.max(s, axis=0, keepdims=True) for s in st]
        e = [jnp.exp(s - m) for s, m in zip(st, top)]
        total = [jnp.sum(x, axis=0, keepdims=True) for x in e]
        for i, (c, h) in enumerate(pairs):
            vt = v_ref[rows, c].T
            parts = []
            for j in range(2):
                x = 2 * i + j
                parts.append(dot(vt[j * HD:(j + 1) * HD, :], e[x].astype(BF16)) * (1.0 / total[x]))
                lse_ref[pl.ds(h + j, 1), rows] = top[x] + jnp.log(total[x])
            ctx[rows, c] = jnp.concatenate(parts, axis=0).T.astype(BF16)

    sequences(tab, o_ref.shape[0] // GRAN, work)
    o_ref[...] = ctx[pl.ds(HALO, o_ref.shape[0]), :]


def attn_fwd_call(tab, q, k, v, rows):
    win, d = q.shape
    spec = pl.BlockSpec((win, LANES), lambda h, t: (0, h))
    return pl.pallas_call(
        attn_fwd_kernel,
        grid_spec=pltpu.PrefetchScalarGridSpec(
            num_scalar_prefetch=1,
            grid=(d // LANES,),
            in_specs=[spec] * 3,
            out_specs=[pl.BlockSpec((rows, LANES), lambda h, t: (0, h)), pl.BlockSpec((LANES // HD, win), lambda h, t: (h, 0))],
            scratch_shapes=[pltpu.VMEM((win, LANES), BF16)],
        ),
        out_shape=[jax.ShapeDtypeStruct((rows, d), BF16), jax.ShapeDtypeStruct((d // HD, win), F32)],
        compiler_params=params(),
        cost_estimate=cost(8 * rows * 512 * d, 8 * win * d, rows * 512 * 16),
        name="attn_fwd",
    )(tab, q, k, v)


def attn_bwd_kernel(tab, q_ref, k_ref, v_ref, lse_ref, gl, go, gr, dq_o, dk_o, dv_o, sums, g_s, dq_s, dk_s, dv_s):
    rows_own = go.shape[0]
    g_s[pl.ds(0, HALO), :] = gl[...]
    g_s[pl.ds(HALO, rows_own), :] = go[...]
    g_s[pl.ds(HALO + rows_own, HALO), :] = gr[...]

    def work(rows, pairs):
        mine = masks((rows.size, 2 * HD))
        qs, gs, p, dp = [], [], [], []
        for c, h in pairs:
            q, k, v, g = eighth(q_ref[rows, c]), k_ref[rows, c], v_ref[rows, c], g_s[rows, c]
            zero = jnp.zeros_like(q)
            for j, m in enumerate(mine):
                st = dot_nt(k, jnp.where(m, q, zero))
                p.append(jnp.exp(st - lse_ref[pl.ds(h + j, 1), rows]))
                dp.append(dot_nt(v, jnp.where(m, g, zero)))
            qs.append(q)
            gs.append(g)
        delta = [jnp.sum(a * b, axis=0, keepdims=True) for a, b in zip(p, dp)]
        ds = [(a * (b - d)).astype(BF16) for a, b, d in zip(p, dp, delta)]
        for i, (c, h) in enumerate(pairs):
            kt = eighth(k_ref[rows, c]).T
            dq = [dot(kt[j * HD:(j + 1) * HD, :], ds[2 * i + j]) for j in range(2)]
            dk = [dot(ds[2 * i + j], qs[i]) for j in range(2)]
            dv = [dot(p[2 * i + j].astype(BF16), gs[i]) for j in range(2)]
            dq_s[rows, c] = jnp.concatenate(dq, axis=0).T.astype(BF16)
            dk_s[rows, c] = jnp.where(mine[0], dk[0], dk[1]).astype(BF16)
            dv_s[rows, c] = jnp.where(mine[0], dv[0], dv[1]).astype(BF16)

    sequences(tab, rows_own // GRAN, work)
    own = pl.ds(HALO, rows_own)
    dq_o[...] = dq_s[own, :]
    dk_o[...] = dk_s[own, :]
    dv_o[...] = dv_s[own, :]
    sums[0:1, :] = jnp.sum(dq_o[...].astype(F32), axis=0, keepdims=True)
    sums[1:2, :] = jnp.sum(dv_o[...].astype(F32), axis=0, keepdims=True)


def attn_bwd_call(tab, q, k, v, lse, gl, go, gr):
    win, d = q.shape
    rows = go.shape[0]
    spec = pl.BlockSpec((win, LANES), lambda h, t: (0, h))
    own = pl.BlockSpec((rows, LANES), lambda h, t: (0, h))
    halo = pl.BlockSpec((HALO, LANES), lambda h, t: (0, h))
    out = jax.ShapeDtypeStruct((rows, d), BF16)
    return pl.pallas_call(
        attn_bwd_kernel,
        grid_spec=pltpu.PrefetchScalarGridSpec(
            num_scalar_prefetch=1,
            grid=(d // LANES,),
            in_specs=[spec] * 3 + [pl.BlockSpec((LANES // HD, win), lambda h, t: (h, 0)), halo, own, halo],
            out_specs=[own] * 3 + [pl.BlockSpec((8, LANES), lambda h, t: (0, h))],
            scratch_shapes=[pltpu.VMEM((win, LANES), BF16)] * 4,
        ),
        out_shape=[out] * 3 + [jax.ShapeDtypeStruct((8, d), F32)],
        compiler_params=params(),
        cost_estimate=cost(20 * rows * 512 * d, 14 * win * d, rows * 512 * 16),
        name="attn_bwd",
    )(tab, q, k, v, lse, gl, go, gr)


def norm_stats(z):
    cen = z - jnp.mean(z, axis=-1, keepdims=True)
    r = lax.rsqrt(jnp.mean(cen * cen, axis=-1, keepdims=True) + EPS)
    return cen * r, r


def norm_back(e, n, r):
    return r * (e - jnp.mean(e, axis=-1, keepdims=True) - n * jnp.mean(e * n, axis=-1, keepdims=True))


RC = 256
TF = 512
TC = 256


def chunks(rows, fn):
    def step(i, c):
        fn(pl.ds(pl.multiple_of(i * RC, RC), RC))
        return c

    lax.fori_loop(0, rows // RC, step, 0)


def clip(t, first, count):
    return jnp.clip(t - first, 0, count - 1)


def lanes(t, size):
    return pl.ds(pl.multiple_of(t * size, size), size)


def colsum(v):
    return jnp.sum(v, axis=0, keepdims=True)


def gelu_parts(u):
    phi = 0.5 * (1.0 + lax.erf(u * (0.5 ** 0.5)))
    return u * phi, phi + u * (0.3989422804014327 * jnp.exp(-0.5 * u * u))


def fwd_kernel(nu, nc, ctx, wo, x, wu, bu, wd, g, vec, xhat, lowt, ctxt, r1, hidt, dg, out, gs, gd, sums, z, hid, low):
    t = pl.program_id(0)
    rows = x.shape[0]

    @pl.when(t < nc)
    def _():
        c = lanes(t, TC)
        z[:, c] = dot(ctx[...], wo[...]) + x[:, c].astype(F32)

    @pl.when(t == nc - 1)
    def _():
        def fin(r):
            n, rr = norm_stats(z[r, :] + vec[2:3, :])
            xhat[r, :] = n
            r1[r, :] = jnp.broadcast_to(rr, (RC, r1.shape[1]))
            v = (n * vec[4:5, :] + vec[5:6, :]).astype(BF16)
            low[r, :] = v
            lowt[:, r] = v.T
            ctxt[:, r] = ctx[r, :].T

        chunks(rows, fin)

    @pl.when((t >= nc) & (t < nc + nu))
    def _():
        for j in range(TF // TC):
            c = slice(j * TC, (j + 1) * TC)
            h, s = gelu_parts(dot(low[...], wu[:, c]) + bu[:, c])
            h = h.astype(BF16)
            dg[:, c] = s.astype(BF16)
            hid[:, lanes((t - nc) * (TF // TC) + j, TC)] = h
            hidt[c, :] = h.T

    @pl.when(t >= nc + nu)
    def _():
        c = lanes(t - nc - nu, TC)
        z[:, c] = dot(hid[...], wd[...])

    @pl.when(t == 2 * nc + nu - 1)
    def _():
        sums[...] = jnp.zeros_like(sums)

        def fin(r):
            v = (xhat[r, :] * vec[4:5, :] + vec[5:6, :]) + (z[r, :] + vec[3:4, :])
            n, rr = norm_stats(v)
            out[r, :] = (n * vec[6:7, :] + vec[7:8, :]).astype(BF16)
            gv = g[r, :].astype(F32)
            sums[0:1, :] += colsum(gv * n)
            sums[1:2, :] += colsum(gv)
            grad = norm_back(gv * vec[6:7, :], n, rr)
            gs[r, :] = grad
            low_g = grad.astype(BF16)
            gd[r, :] = low_g
            sums[2:3, :] += colsum(low_g.astype(F32))

        chunks(rows, fin)


def single(shape):
    return pl.BlockSpec(shape, lambda *_: (0,) * len(shape), pipeline_mode=pl.Buffered(1))


def fwd_call(ctx, wo, x, wu, bu, wd, g, vec):
    rows, d = x.shape
    ff = wu.shape[1]
    nu, nc = ff // TF, d // TC
    return pl.pallas_call(
        functools.partial(fwd_kernel, nu, nc),
        grid=(2 * nc + nu,),
        in_specs=[single(ctx.shape), pl.BlockSpec((d, TC), lambda t: (0, clip(t, 0, nc))), single(x.shape),
                  pl.BlockSpec((d, TF), lambda t: (0, clip(t, nc, nu))), pl.BlockSpec((1, TF), lambda t: (0, clip(t, nc, nu))),
                  pl.BlockSpec((ff, TC), lambda t: (0, clip(t, nc + nu, nc))), single(g.shape), single(vec.shape)],
        out_specs=[single((rows, d)), single((d, rows)), single((d, rows)), single((rows, 128)),
                   pl.BlockSpec((TF, rows), lambda t: (clip(t, nc, nu), 0)), pl.BlockSpec((rows, TF), lambda t: (0, clip(t, nc, nu))),
                   single((rows, d)), single((rows, d)), single((rows, d)), single((8, d))],
        out_shape=[jax.ShapeDtypeStruct((rows, d), F32), jax.ShapeDtypeStruct((d, rows), BF16), jax.ShapeDtypeStruct((d, rows), BF16),
                   jax.ShapeDtypeStruct((rows, 128), F32), jax.ShapeDtypeStruct((ff, rows), BF16),
                   jax.ShapeDtypeStruct((rows, ff), BF16), jax.ShapeDtypeStruct((rows, d), BF16),
                   jax.ShapeDtypeStruct((rows, d), F32), jax.ShapeDtypeStruct((rows, d), BF16), jax.ShapeDtypeStruct((8, d), F32)],
        scratch_shapes=[pltpu.VMEM((rows, d), F32), pltpu.VMEM((rows, ff), BF16), pltpu.VMEM((rows, d), BF16)],
        compiler_params=params(60),
        cost_estimate=cost(4 * rows * d * ff, 4 * d * ff + 4 * rows * ff + rows * d * 14, 2 * rows * ff),
        name="fwd",
    )(ctx, wo, x, wu, bu, wd, g, vec)


def grid_of(n):
    chips = n // 2
    return {16: (4, 2, 2), 64: (4, 4, 4)}.get(chips, (chips, 1, 1))


class Place:
    def __init__(self, n):
        self.n = n
        self.size = grid_of(n)
        me = lax.axis_index("dp")
        nz, ny, nx = self.size
        self.me = me
        self.c = lax.rem(me, 2)
        self.x = lax.rem(me // 2, nx)
        self.y = lax.rem(me // (2 * nx), ny)
        self.z = me // (2 * nx * ny)

    def at(self, axis, k):
        nz, ny, nx = self.size
        z, y, x, c = self.z, self.y, self.x, self.c
        if axis == "z":
            z = lax.rem(z + k, nz)
        elif axis == "y":
            y = lax.rem(y + k, ny)
        elif axis == "x":
            x = lax.rem(x + k, nx)
        else:
            c = lax.rem(c + k, 2)
        pos = {"z": z, "y": y, "x": x, "c": c}[axis]
        return ((z * ny + y) * nx + x) * 2 + c, pos

    def steps(self, axis):
        nz, ny, nx = self.size
        return range(1, {"z": nz, "y": ny, "x": nx, "c": 2}[axis])

    def peers(self):
        return [self.at(a, k)[0] for a in "zyxc" for k in self.steps(a)]


def enter(peers):
    sem = pltpu.get_barrier_semaphore()
    for p in peers:
        pl.semaphore_signal(sem, inc=1, device_id=(p,), device_id_type=MESH)
    pl.semaphore_wait(sem, len(peers))


def gather_slots(n):
    nz, ny, nx = grid_of(n)
    return (nz - 1) + 2 * (ny - 1) + 2 * (nx - 1) + 1


class Gather:
    def __init__(self, place, src, dst, rows, cols, ssem, rsem, lsem, index):
        self.p, self.index = place, index
        self.src, self.dst, self.rows, self.cols = src, dst, rows, cols
        self.ssem, self.rsem, self.lsem = ssem, rsem, lsem
        p = place
        r0, nr = rows
        c0, nc = cols
        rs = pl.ds(r0, nr)
        full = pl.ds(c0, nc)
        halves = (pl.ds(c0, nc // 2), pl.ds(c0 + nc // 2, nc // 2))
        al = pl.ds(0, p.size[0])
        self.local = pltpu.make_async_copy(src.at[rs, full], dst.at[p.z, p.y, p.x, p.c, rs, full], lsem.at[index])
        slot = 0

        def copy(s, d, dev):
            nonlocal slot
            cp = pltpu.make_async_remote_copy(src_ref=s, dst_ref=d, send_sem=ssem.at[index, slot], recv_sem=rsem.at[index, slot],
                                              device_id=(dev,), device_id_type=MESH)
            slot += 1
            return cp

        mine = dst.at[p.z, p.y, p.x, p.c, rs, full]
        self.ph = [[], [], [], []]
        for k in p.steps("z"):
            self.ph[0].append(copy(src.at[rs, full], mine, p.at("z", k)[0]))
        for h, axis in ((0, "y"), (1, "x")):
            s = dst.at[:, p.y, p.x, p.c, rs, halves[h]]
            for k in p.steps(axis):
                self.ph[1].append(copy(s, s, p.at(axis, k)[0]))
        for h, axis in ((0, "x"), (1, "y")):
            s = dst.at[:, :, p.x, p.c, rs, halves[0]] if h == 0 else dst.at[:, p.y, :, p.c, rs, halves[1]]
            for k in p.steps(axis):
                self.ph[2].append(copy(s, s, p.at(axis, k)[0]))
        s = dst.at[:, :, :, p.c, rs, full]
        self.ph[3].append(copy(s, s, p.at("c", 1)[0]))

    def start(self, i):
        if i == 0:
            self.local.start()
        for cp in self.ph[i]:
            cp.start()

    def wait(self, i):
        if i == 0:
            self.local.wait()
        for cp in self.ph[i]:
            cp.wait_recv()

    def sent(self):
        for ph in self.ph:
            for cp in ph:
                cp.wait_send()


def gather_kernel(n, plan, nsrc, *refs):
    srcs, xsrc, outs = refs[:nsrc], refs[nsrc], refs[nsrc + 1:2 * nsrc + 1]
    xl, xr = refs[2 * nsrc + 1:2 * nsrc + 3]
    ssem, rsem, lsem, hs, hr = refs[2 * nsrc+3:]
    p = Place(n)
    right, left = lax.rem(p.me + 1, n), lax.rem(p.me + n - 1, n)
    enter(p.peers() + [left, right])
    rows = xsrc.shape[0]
    halo = [pltpu.make_async_remote_copy(src_ref=xsrc.at[pl.ds(rows-HALO,HALO),:], dst_ref=xl, send_sem=hs.at[0], recv_sem=hr.at[0], device_id=(right,), device_id_type=MESH),
            pltpu.make_async_remote_copy(src_ref=xsrc.at[pl.ds(0,HALO),:], dst_ref=xr, send_sem=hs.at[1], recv_sem=hr.at[1], device_id=(left,), device_id_type=MESH)]
    for h in halo: h.start()
    g = [Gather(p, srcs[a], outs[a], r, c, ssem, rsem, lsem, i) for i, (a, r, c) in enumerate(plan)]
    for s in range(len(g) + 4):
        for ph in (0, 1, 2, 3, 4):
            i = s - ph
            if 0 <= i < len(g):
                if ph > 0:
                    g[i].wait(ph - 1)
                if ph < 4:
                    g[i].start(ph)
    for c in g:
        c.sent()
    for h in halo: h.wait()


def gather_plan(shards, d):
    least = min(s.shape[0] for s in shards if s.shape[-1] >= d)
    plan = []
    for a, s in enumerate(shards):
        if s.shape[1] < d:
            plan.append((a, (0, s.shape[0]), (0, s.shape[1])))
            continue
        for j in range(s.shape[1] // d):
            for i in range(s.shape[0] // least):
                plan.append((a, (i * least, least), (j * d, d)))
    return plan


def gather_call(n, shards, tokens, order=None):
    d = tokens.shape[1]
    plan = gather_plan(shards, d)
    k = gather_slots(n)
    outs = [jax.ShapeDtypeStruct(grid_of(n) + (2,) + s.shape, s.dtype) for s in shards]
    halo = jax.ShapeDtypeStruct((HALO, d), tokens.dtype)
    res = pl.pallas_call(
        functools.partial(gather_kernel, n, plan, len(shards)),
        in_specs=[ANY] * (len(shards)+1),
        out_specs=[ANY] * (len(shards)+2),
        out_shape=outs+[halo,halo],
        scratch_shapes=[pltpu.SemaphoreType.DMA((len(plan), k)), pltpu.SemaphoreType.DMA((len(plan), k)),
                        pltpu.SemaphoreType.DMA((len(plan),)),pltpu.SemaphoreType.DMA((2,)),pltpu.SemaphoreType.DMA((2,))],
        compiler_params=pltpu.CompilerParams(collective_id=1, has_side_effects=True),
        name="gather",
    )(*shards, tokens)
    return [r.reshape((n * s.shape[0],) + s.shape[1:]) for r, s in zip(res, shards)] + list(res[-2:])


def reduce_slots(n):
    nz, ny, nx = grid_of(n)
    return (nz - 1) + 2 * (ny - 1) + 2 * (nx - 1) + 1


def reduce_buffers(n, r, cols, dtype):
    nz, ny, nx = grid_of(n)
    h = cols // 2
    return [pltpu.VMEM((nz, ny, nx, r, cols), dtype),
            pltpu.VMEM((max(nx - 1, 1), nz, ny, r, h), dtype), pltpu.VMEM((max(ny - 1, 1), nz, nx, r, h), dtype),
            pltpu.VMEM((max(ny - 1, 1), nz, r, h), dtype), pltpu.VMEM((max(nx - 1, 1), nz, r, h), dtype),
            pltpu.VMEM((max(nz - 1, 1), r, cols), dtype), pltpu.VMEM((nz, r, cols), dtype), pltpu.VMEM((r, cols), F32)]


class Reduce:
    def __init__(self, place, src, own, bufs, out, ssem, rsem, lsem, index):
        self.p, self.src, self.own, self.bufs = place, src, own, bufs
        p = place
        self.h = bufs[1].shape[-1]
        self.ca, self.cb = pl.ds(0, self.h), pl.ds(self.h, self.h)
        if own is not None:
            self.get = pltpu.make_async_copy(src.at[:, :, :, p.c], own, lsem.at[index, 0])
        self.put = pltpu.make_async_copy(bufs[7], out, lsem.at[index, 1])
        slot = 0

        def copy(s, d, dev):
            nonlocal slot
            cp = pltpu.make_async_remote_copy(src_ref=s, dst_ref=d, send_sem=ssem.at[index, slot], recv_sem=rsem.at[index, slot],
                                              device_id=(dev,), device_id_type=MESH)
            slot += 1
            return cp

        self.ph = [[], [], [], []]
        dev, oc = p.at("c", 1)
        self.ph[0].append(copy(src.at[:, :, :, oc], bufs[0], dev))
        for k in p.steps("x"):
            dev, o = p.at("x", k)
            self.ph[1].append(copy(bufs[0].at[:, :, o, :, self.ca], bufs[1].at[k - 1], dev))
        for k in p.steps("y"):
            dev, o = p.at("y", k)
            self.ph[1].append(copy(bufs[0].at[:, o, :, :, self.cb], bufs[2].at[k - 1], dev))
        for k in p.steps("y"):
            dev, o = p.at("y", k)
            self.ph[2].append(copy(bufs[1].at[0, :, o], bufs[3].at[k - 1], dev))
        for k in p.steps("x"):
            dev, o = p.at("x", k)
            self.ph[2].append(copy(bufs[2].at[0, :, o], bufs[4].at[k - 1], dev))
        for k in p.steps("z"):
            dev, o = p.at("z", k)
            self.ph[3].append(copy(bufs[6].at[o], bufs[5].at[k - 1], dev))

    def begin(self):
        self.ph[0][0].start()
        if self.own is not None:
            self.get.start()

    def go(self, i):
        p, bufs = self.p, self.bufs
        nz, ny, nx = p.size
        dt = bufs[0].dtype
        for cp in self.ph[i - 1]:
            cp.wait_recv()
        if i == 1:
            self.ph[0][0].wait_send()
            if self.own is not None:
                self.get.wait()

            def add(z, c):
                mine = self.own[z] if self.own is not None else self.src[z, :, :, pl.ds(p.c, 1)][:, :, 0]
                bufs[0][z] = (mine.astype(F32) + bufs[0][z].astype(F32)).astype(dt)
                return c

            lax.fori_loop(0, nz, add, 0)
        elif i == 2:
            def add(z, c):
                a = bufs[0][z, :, pl.ds(p.x, 1), :, self.ca].astype(F32)[:, 0]
                for k in range(nx - 1):
                    a += bufs[1][k, z].astype(F32)
                bufs[1][0, z] = a.astype(dt)
                b = bufs[0][z, pl.ds(p.y, 1), :, :, self.cb].astype(F32)[0]
                for k in range(ny - 1):
                    b += bufs[2][k, z].astype(F32)
                bufs[2][0, z] = b.astype(dt)
                return c

            lax.fori_loop(0, nz, add, 0)
        elif i == 3:
            a = bufs[1][0, :, pl.ds(p.y, 1)].astype(F32)[:, 0]
            for k in range(ny - 1):
                a += bufs[3][k].astype(F32)
            bufs[6][:, :, self.ca] = a.astype(dt)
            b = bufs[2][0, :, pl.ds(p.x, 1)].astype(F32)[:, 0]
            for k in range(nx - 1):
                b += bufs[4][k].astype(F32)
            bufs[6][:, :, self.cb] = b.astype(dt)
        else:
            a = bufs[6][pl.ds(p.z, 1)].astype(F32)[0]
            for k in range(nz - 1):
                a += bufs[5][k].astype(F32)
            bufs[7][...] = a
            self.put.start()
            return
        for cp in self.ph[i]:
            cp.start()

    def finish(self):
        self.put.wait()
        for ph in self.ph[1:]:
            for cp in ph:
                cp.wait_send()


def run_at(t, events):
    for step in sorted({e[0] for e in events}):
        @pl.when(t == step)
        def _():
            for e in events:
                if e[0] == step:
                    e[1](*e[2:])


EARLY = 3


def bwd_kernel(n, nu, nc, nr, gd, lowt, hidt, dg, wd, wu, gs, xhat, r1, vec, gsf, ga, sums, sumu, dwd3, dwu3, rd, ru, gu, bufd, bufu, *rest):
    t = pl.program_id(0)
    d, rows = lowt.shape
    ssem, rsem, lsem, wsem = rest[-4:]
    p = Place(n)
    r = d // n
    red = []
    for i in range(2 * EARLY):
        j = i // 2
        out = rd.at[pl.ds(j * r, r), :] if i % 2 == 0 else ru.at[:, pl.ds(j * d, d)]
        red.append(Reduce(p, (bufd, bufu)[i % 2], None, rest[8 * i:8 * i + 8], out, ssem, rsem, lsem, i))
    late = [pltpu.make_async_copy(bufd, dwd3, wsem.at[0]), pltpu.make_async_copy(bufu, dwu3, wsem.at[1])]

    @pl.when(t == 0)
    def _():
        enter(p.peers())

    @pl.when(t < nu)
    def _():
        for j in range(TF // TC):
            c = slice(j * TC, (j + 1) * TC)
            g = (dot_nt(gd[...], wd[c, :]) * dg[:, c].astype(F32)).astype(BF16)
            gu[:, lanes(t * (TF // TC) + j, TC)] = g
            sumu[:, c] = colsum(g.astype(F32))

    mid = []
    for j in range(EARLY):
        mid += [(2 * j + 2, red[2 * j].go, 1), (2 * j + 2, red[2 * j + 1].go, 1)]
        if j > 0:
            mid += [(2 * j + 2, red[2 * j - 1].go, 2)]
        if j > 1:
            mid += [(2 * j + 2, red[2 * j - 3].go, 4)]
    run_at(t, mid)

    @pl.when(t < nu)
    def _():
        half = lax.rem(t, d // TF)
        for j in range(TF // TC):
            c = lanes(half * (TF // TC) + j, TC)
            bufu[..., c] = dot(lowt[...], gu[:, lanes(t * (TF // TC) + j, TC)]).astype(BF16).reshape(bufu.shape[:-1] + (TC,))
            bufd[..., c] = dot(hidt[...].reshape(d, rows), gd[:, c]).astype(BF16).reshape(bufd.shape[:-1] + (TC,))

    @pl.when((t >= nu) & (t < nu + nc))
    def _():
        gsf[:, lanes(t - nu, TC)] = gs[...] + dot_nt(gu[...], wu[...])

    @pl.when(t == nu + nc)
    def _():
        sums[...] = jnp.zeros_like(sums)

    @pl.when(t >= nu + nc)
    def _():
        at = lanes(t - nu - nc, RC)
        gf = gsf[at, :]
        nn = xhat[...]
        sums[0:1, :] += colsum(gf * nn)
        sums[1:2, :] += colsum(gf)
        grad = norm_back(gf * vec[4:5, :], nn, r1[:, 0:1])
        gsf[at, :] = grad
        low_g = grad.astype(BF16)
        ga[...] = low_g
        sums[2:3, :] += colsum(low_g.astype(F32))

    end = []
    for j in range(EARLY):
        s = 2 * j + 1
        end += [(s, red[2 * j].begin), (s, red[2 * j + 1].begin)]
    end += [(3, red[0].go, 2), (4, red[0].go, 3), (5, red[1].go, 3), (5, red[2].go, 2), (5, red[0].go, 4)]
    end += [(6, red[2].go, 3), (7, late[0].start), (7, late[1].start), (7, red[3].go, 3), (7, red[4].go, 2), (8, red[2].go, 4),
            (8, red[5].go, 2), (9, red[4].go, 3), (9, red[3].go, 4), (10, red[5].go, 3), (12, red[4].go, 4)]
    last = nu + nc + nr - 1
    end += [(last, red[5].go, 4)] + [(last, c.wait) for c in late] + [(last, c.finish) for c in red]
    run_at(t, end)


def bwd_call(n, gd, lowt, hidt, dg, wd, wu, gs, xhat, r1, vec):
    d, rows = lowt.shape
    ff = wu.shape[1]
    nu, nc, nr = ff // TF, d // TC, rows // RC
    r = d // n
    parts = ff // d
    z = grid_of(n) + (2, r)
    per = d // TF
    chunk = jax.ShapeDtypeStruct(z + (d,), BF16)
    k = reduce_slots(n)
    scratch = [pltpu.VMEM((rows, ff), BF16), pltpu.VMEM(z + (d,), BF16), pltpu.VMEM(z + (d,), BF16)]
    for i in range(2 * EARLY):
        scratch += reduce_buffers(n, r, d, BF16)
    scratch += [pltpu.SemaphoreType.DMA((2 * EARLY, k)), pltpu.SemaphoreType.DMA((2 * EARLY, k)), pltpu.SemaphoreType.DMA((2 * EARLY, 2)),
                pltpu.SemaphoreType.DMA((2,))]
    return pl.pallas_call(
        functools.partial(bwd_kernel, n, nu, nc, nr),
        grid=(nu + nc + nr,),
        in_specs=[single(gd.shape), single(lowt.shape),
                  pl.BlockSpec((n, 1, r, rows), lambda t: (0, clip(t, 0, nu) // per, 0, 0)),
                  pl.BlockSpec((rows, TF), lambda t: (0, clip(t, 0, nu))), pl.BlockSpec((TF, d), lambda t: (clip(t, 0, nu), 0)),
                  pl.BlockSpec((TC, ff), lambda t: (clip(t, nu, nc), 0)), pl.BlockSpec((rows, TC), lambda t: (0, clip(t, nu, nc))),
                  pl.BlockSpec((RC, d), lambda t: (clip(t, nu + nc, nr), 0)), pl.BlockSpec((RC, 128), lambda t: (clip(t, nu + nc, nr), 0)),
                  single(vec.shape)],
        out_specs=[single((rows, d)), pl.BlockSpec((RC, d), lambda t: (clip(t, nu + nc, nr), 0)), single((8, d)),
                   pl.BlockSpec((1, TF), lambda t: (0, clip(t, 0, nu))), ANY, ANY, ANY, ANY],
        out_shape=[jax.ShapeDtypeStruct((rows, d), F32), jax.ShapeDtypeStruct((rows, d), BF16), jax.ShapeDtypeStruct((8, d), F32),
                   jax.ShapeDtypeStruct((1, ff), F32), chunk, chunk,
                   jax.ShapeDtypeStruct((EARLY * r, d), F32), jax.ShapeDtypeStruct((r, EARLY * d), F32)],
        scratch_shapes=scratch,
        compiler_params=pltpu.CompilerParams(collective_id=3, has_side_effects=True, vmem_limit_bytes=60 << 20),
        cost_estimate=cost(8 * rows * d * ff, 8 * d * ff + 4 * rows * ff + rows * d * 18),
        name="bwd",
    )(gd, lowt, hidt.reshape(n, parts, r, rows), dg, wd, wu, gs, xhat, r1, vec)


def ctx_bwd_kernel(n, nc, ga, wo, ctxt, gc, dwo, gl, gr, ssem, rsem):
    t = pl.program_id(0)
    rows = ga.shape[0]
    me = lax.axis_index("dp")
    right, left = lax.rem(me + 1, n), lax.rem(me + n - 1, n)
    copies = [pltpu.make_async_remote_copy(src_ref=gc.at[pl.ds(rows - HALO, HALO), :], dst_ref=gl, send_sem=ssem.at[0], recv_sem=rsem.at[0],
                                           device_id=(right,), device_id_type=MESH),
              pltpu.make_async_remote_copy(src_ref=gc.at[pl.ds(0, HALO), :], dst_ref=gr, send_sem=ssem.at[1], recv_sem=rsem.at[1],
                                           device_id=(left,), device_id_type=MESH)]

    @pl.when(t == 0)
    def _():
        enter([left, right])

    @pl.when(t < nc)
    def _():
        gc[:, lanes(t, TC)] = dot_nt(ga[...], wo[...]).astype(BF16)

    @pl.when(t == nc - 1)
    def _():
        for c in copies:
            c.start()

    @pl.when(t >= nc)
    def _():
        dwo[...] = dot(ctxt[...], ga[:, lanes(t - nc, TC)]).astype(BF16)

    @pl.when(t == 2 * nc - 1)
    def _():
        for c in copies:
            c.wait()


def ctx_bwd_call(n, ga, wo, ctxt):
    rows, d = ga.shape
    nc = d // TC
    edge = jax.ShapeDtypeStruct((HALO, d), BF16)
    return pl.pallas_call(
        functools.partial(ctx_bwd_kernel, n, nc),
        grid=(2 * nc,),
        in_specs=[single(ga.shape), pl.BlockSpec((TC, d), lambda t: (clip(t, 0, nc), 0)), single(ctxt.shape)],
        out_specs=[single((rows, d)), pl.BlockSpec((d, TC), lambda t: (0, clip(t, nc, nc))), ANY, ANY],
        out_shape=[jax.ShapeDtypeStruct((rows, d), BF16), jax.ShapeDtypeStruct((d, d), BF16), edge, edge],
        scratch_shapes=[pltpu.SemaphoreType.DMA((2,)), pltpu.SemaphoreType.DMA((2,))],
        compiler_params=pltpu.CompilerParams(collective_id=4, has_side_effects=True, vmem_limit_bytes=40 << 20),
        cost_estimate=cost(4 * rows * d * d, rows * d * 8 + 4 * d * d),
        name="ctx_bwd",
    )(ga, wo, ctxt)


def in_bwd_kernel(n, nc, x, gsf, dq, dk, dv, wq, wk, wv, sd, su, so, sv, tg, rd, ru, ro, rv, rq, rk, rw, xt, bq, bk, bv, od, ou, oo, ov, *rest):
    t = pl.program_id(0)
    ssem, rsem, lsem = rest[-3:]
    p = Place(n)
    plan = [(sd, od, rd), (su, ou, ru), (so, oo, ro), (bq, None, rq), (bk, None, rk), (bv, None, rw), (sv, ov, rv)]
    red = [Reduce(p, s, o, rest[8 * i:8 * i + 8], out, ssem, rsem, lsem, i) for i, (s, o, out) in enumerate(plan)]

    @pl.when(t == 0)
    def _():
        enter(p.peers())

    start = [(0, red[i].begin) for i in (0, 1, 2, 6)]
    run_at(t, start)

    @pl.when(t == 0)
    def _():
        xt[...] = x[...].T

    for i, (a, b) in enumerate(((dq, bq), (dk, bk), (dv, bv))):
        @pl.when((t >= i * nc) & (t < (i + 1) * nc))
        def _():
            c = lanes(t - i * nc, TC)
            b[..., c] = dot(xt[...], a[:, c]).astype(BF16).reshape(b.shape[:-1] + (TC,))

    @pl.when(t >= 3 * nc)
    def _():
        g = gsf[...] + dot_nt(dq[...], wq[...]) + dot_nt(dk[...], wk[...]) + dot_nt(dv[...], wv[...])
        tg[...] = g.astype(BF16)

    a, b, o, q, k, v, s = red
    end = [(0, a.go, 1), (1, b.go, 1), (2, o.go, 1), (3, q.begin), (5, q.go, 1), (6, a.go, 2), (7, k.begin), (8, s.go, 1), (9, k.go, 1), (10, b.go, 2),
           (11, v.begin), (12, a.go, 3), (13, v.go, 1), (14, o.go, 2)]
    last = 4 * nc - 1
    end += [(last, s.go, 2), (last, b.go, 3), (last, a.go, 4), (last, q.go, 2), (last, o.go, 3), (last, k.go, 2), (last, b.go, 4), (last, q.go, 3),
            (last, s.go, 3), (last, v.go, 2), (last, o.go, 4), (last, k.go, 3), (last, q.go, 4), (last, v.go, 3), (last, s.go, 4), (last, k.go, 4),
            (last, v.go, 4)]
    end += [(last, c.finish) for c in red]
    run_at(t, end)


def in_bwd_call(n, x, gsf, dq, dk, dv, wq, wk, wv, dwd3, dwu3, dwo, small):
    rows, d = x.shape
    nc = d // TC
    r = d // n
    z = grid_of(n)
    col = pl.BlockSpec((rows, TC), lambda t: (0, clip(t, 3 * nc, nc)))
    wrow = pl.BlockSpec((TC, d), lambda t: (clip(t, 3 * nc, nc), 0))
    chunk = pltpu.VMEM(z + (2, r, d), BF16)
    own = pltpu.VMEM(z + (r, d), BF16)
    share = jax.ShapeDtypeStruct((r, d), F32)
    sr, sc = small.shape[0] // n, small.shape[1]
    k = reduce_slots(n)
    scratch = [pltpu.VMEM((d, rows), BF16)] + [chunk] * 3 + [own] * 3 + [pltpu.VMEM(z + (sr, sc), F32)]
    for i in range(6):
        scratch += reduce_buffers(n, r, d, BF16)
    scratch += reduce_buffers(n, sr, sc, F32)
    scratch += [pltpu.SemaphoreType.DMA((7, k)), pltpu.SemaphoreType.DMA((7, k)), pltpu.SemaphoreType.DMA((7, 2))]
    return pl.pallas_call(
        functools.partial(in_bwd_kernel, n, nc),
        grid=(4 * nc,),
        in_specs=[single((rows, d)), col] + [single((rows, d))] * 3 + [wrow] * 3 + [ANY] * 4,
        out_specs=[col] + [ANY] * 7,
        out_shape=[jax.ShapeDtypeStruct((rows, d), BF16), share, share, share, jax.ShapeDtypeStruct((sr, sc), F32), share, share, share],
        scratch_shapes=scratch,
        compiler_params=pltpu.CompilerParams(collective_id=5, has_side_effects=True, vmem_limit_bytes=60 << 20),
        cost_estimate=cost(12 * rows * d * d, rows * d * 14 + 12 * d * d),
        name="in_bwd",
    )(x, gsf, dq, dk, dv, wq, wk, wv, dwd3, dwu3, dwo.reshape(z + (2, r, d)), small.reshape(z + (2, sr, sc)))


def hand_on_kernel(q, k, v, o, ua, ub, da, db, qo, ko, vo, oo, u, d):
    for a, b in ((q, qo), (k, ko), (v, vo), (o, oo)):
        b[...] = a[...]
    u[:, : ua.shape[1]] = ua[...]
    u[:, ua.shape[1]:] = ub[...]
    d[: da.shape[0], :] = da[...]
    d[da.shape[0]:, :] = db[...]


def hand_on(q, k, v, o, ua, ub, da, db):
    r, d = q.shape
    return pl.pallas_call(
        hand_on_kernel,
        out_shape=[jax.ShapeDtypeStruct((r, d), F32)] * 4
        + [jax.ShapeDtypeStruct((r, ua.shape[1] + ub.shape[1]), F32), jax.ShapeDtypeStruct((da.shape[0] + db.shape[0], d), F32)],
        name="hand_on",
    )(q, k, v, o, ua, ub, da, db)


def sequence_table(lengths, own, rows):
    ids = jnp.arange(lengths.shape[0], dtype=jnp.int32)
    starts = jnp.sum(jnp.where(ids[None, :] < ids[:, None], lengths[None, :], 0), axis=1)
    blocks = rows // GRAN
    at = own * rows + jnp.arange(blocks, dtype=jnp.int32) * GRAN
    inside = (starts[None, :] <= at[:, None]) & (at[:, None] < (starts + lengths)[None, :])
    first = jnp.sum(jnp.where(inside, starts[None, :], 0), axis=1)
    length = jnp.sum(jnp.where(inside, lengths[None, :], 0), axis=1)
    lead = (first == at) | (jnp.arange(blocks) == 0)
    return jnp.stack([(first - own * rows + HALO) // GRAN, jnp.where(lead, length // GRAN, 0)]).astype(jnp.int32)


def pack(values, n, rows, dtype):
    cols = [v.reshape(n, -1) for v in values]
    flat = jnp.concatenate(cols, axis=1)
    return jnp.pad(flat, ((0, 0), (0, rows * 256 - flat.shape[1]))).astype(dtype).reshape(n * rows, 256)


def unpack(packed, n, part):
    flat = packed.reshape(n, -1)
    vec = flat[:, : 8 * part].reshape(n, 8, part).transpose(1, 0, 2).reshape(8, n * part)
    return vec, flat[:, 8 * part:12 * part].reshape(1, -1)


def local(tokens, cotangent, lengths, dealing, *shards):
    n = lax.axis_size("dp")
    own = lax.axis_index("dp")
    rows, d = tokens.shape
    part = d // n
    qb, vb, ob, ub, db, fg, fs, sg, ss = shards[6:]
    packed = pack([qb, vb, ob, db, fg, fs, sg, ss, ub], 1, 16, BF16)
    packed, wq, wk, wv, wo, wu, wd, xl, xr = gather_call(n, [packed] + list(shards[:6]), tokens)
    vec, bu = unpack(packed.astype(F32), n, part)
    tab = sequence_table(lengths, own, rows)
    q, k, v = qkv_call(xl, tokens, xr, wq, wk, wv, vec)
    ctx, lse = attn_fwd_call(tab, q, k, v, rows)
    xhat, lowt, ctxt, r1, hidt, dg, layer_out, gs, gd, sums2 = fwd_call(ctx, wo, tokens, wu, bu, wd, cotangent, vec)
    gsf, ga, sums1, sumu, dwd3, dwu3, rd, ru = bwd_call(n, gd, lowt, hidt, dg, wd, wu, gs, xhat, r1, vec)
    gc, dwo, gl, gr = ctx_bwd_call(n, ga, wo, ctxt)
    dq, dk, dv, sums0 = attn_bwd_call(tab, q, k, v, lse, gl, gc, gr)
    small = pack([sums0[0], sums0[1], sums1[2], sums2[2], sums1[0], sums1[1], sums2[0], sums2[1], sumu], n, 8, F32)
    tg, rd3, ru3, go, tiny, gq, gk, gv = in_bwd_call(n, tokens, gsf, dq, dk, dv, wq, wk, wv, dwd3, dwu3, dwo, small)
    gq, gk, gv, go, gu, gd = hand_on(gq, gk, gv, go, ru, ru3, rd, rd3)
    vecs, ubg = unpack(tiny, 1, part)
    t = [vecs[i] for i in range(8)]
    return (layer_out, tg, gq, gk, gv, go, gu, gd, t[0], t[1], t[2], ubg[0], t[3], t[4], t[5], t[6], t[7])


def solution(mesh):
    mat = P("dp", None)
    vec = P("dp")
    return jax.shard_map(
        local,
        mesh=mesh,
        in_specs=(mat, mat, P(), P()) + (mat,) * 6 + (vec,) * 9,
        out_specs=(mat,) * 8 + (vec,) * 9,
        check_vma=False,
    )
```

```python
import functools

import jax
import jax.numpy as jnp
from jax import lax
from jax.experimental import pallas as pl
from jax.experimental.pallas import tpu as pltpu
from jax.sharding import PartitionSpec as P

HD = 64
GRAN = 128
HALO = 384
EPS = 1e-12
F32 = jnp.float32
BF16 = jnp.bfloat16
NT = (((1,), (1,)), ((), ()))
MESH = pl.DeviceIdType.MESH
ANY = pl.BlockSpec(memory_space=pl.ANY)


def params(limit=56):
    return pltpu.CompilerParams(vmem_limit_bytes=limit << 20)


def whole(shape):
    return pl.BlockSpec(shape, lambda *_: (0,) * len(shape))


def dot(a, b):
    return jnp.dot(a, b, preferred_element_type=F32)


def dot_nt(a, b):
    return lax.dot_general(a, b, NT, preferred_element_type=F32)


def cost(flops, nbytes, trans=0):
    return pl.CostEstimate(flops=flops, bytes_accessed=nbytes, transcendentals=trans)


LANES = 512
TOGETHER = {1: 4, 2: 2, 3: 1, 4: 1}


def sequences(tab, blocks, fn):
    def one(b, c):
        n = tab[1, b]
        s0 = tab[0, b]
        for nn in range(1, 5):
            @pl.when(n == nn)
            def _():
                rows = pl.ds(pl.multiple_of(s0 * GRAN, GRAN), nn * GRAN)
                per = TOGETHER[nn]

                def group(i, c):
                    pairs = [i * per + j for j in range(per)]
                    fn(rows, [(pl.ds(pl.multiple_of(p * 2 * HD, 2 * HD), 2 * HD), 2 * p) for p in pairs])
                    return c

                lax.fori_loop(0, LANES // (2 * HD) // per, group, 0)
        return c

    lax.fori_loop(0, blocks, one, 0)


def masks(shape):
    low = lax.broadcasted_iota(jnp.int32, shape, 1) < HD
    return low, ~low


def eighth(x):
    return x * jnp.asarray(0.125, BF16)


def attn_fwd_kernel(tab, q_ref, k_ref, v_ref, o_ref, lse_ref, ctx):
    def work(rows, pairs):
        mine = masks((rows.size, 2 * HD))
        st = []
        for c, h in pairs:
            q, k = eighth(q_ref[rows, c]), k_ref[rows, c]
            st += [dot_nt(k, jnp.where(m, q, jnp.zeros_like(q))) for m in mine]
        top = [jnp.max(s, axis=0, keepdims=True) for s in st]
        e = [jnp.exp(s - m) for s, m in zip(st, top)]
        total = [jnp.sum(x, axis=0, keepdims=True) for x in e]
        for i, (c, h) in enumerate(pairs):
            vt = v_ref[rows, c].T
            parts = []
            for j in range(2):
                x = 2 * i + j
                parts.append(dot(vt[j * HD:(j + 1) * HD, :], e[x].astype(BF16)) * (1.0 / total[x]))
                lse_ref[pl.ds(h + j, 1), rows] = top[x] + jnp.log(total[x])
            ctx[rows, c] = jnp.concatenate(parts, axis=0).T.astype(BF16)

    sequences(tab, o_ref.shape[0] // GRAN, work)
    o_ref[...] = ctx[pl.ds(HALO, o_ref.shape[0]), :]


def attn_fwd_call(tab, q, k, v, rows):
    win, d = q.shape
    spec = pl.BlockSpec((win, LANES), lambda h, t: (0, h))
    return pl.pallas_call(
        attn_fwd_kernel,
        grid_spec=pltpu.PrefetchScalarGridSpec(
            num_scalar_prefetch=1,
            grid=(d // LANES,),
            in_specs=[spec] * 3,
            out_specs=[pl.BlockSpec((rows, LANES), lambda h, t: (0, h)), pl.BlockSpec((LANES // HD, win), lambda h, t: (h, 0))],
            scratch_shapes=[pltpu.VMEM((win, LANES), BF16)],
        ),
        out_shape=[jax.ShapeDtypeStruct((rows, d), BF16), jax.ShapeDtypeStruct((d // HD, win), F32)],
        compiler_params=params(),
        cost_estimate=cost(8 * rows * 512 * d, 8 * win * d, rows * 512 * 16),
        name="attn_fwd",
    )(tab, q, k, v)


def attn_bwd_kernel(tab, q_ref, k_ref, v_ref, lse_ref, gl, go, gr, dq_o, dk_o, dv_o, sums, g_s, dq_s, dk_s, dv_s):
    rows_own = go.shape[0]
    g_s[pl.ds(0, HALO), :] = gl[...]
    g_s[pl.ds(HALO, rows_own), :] = go[...]
    g_s[pl.ds(HALO + rows_own, HALO), :] = gr[...]

    def work(rows, pairs):
        mine = masks((rows.size, 2 * HD))
        qs, gs, p, dp = [], [], [], []
        for c, h in pairs:
            q, k, v, g = eighth(q_ref[rows, c]), k_ref[rows, c], v_ref[rows, c], g_s[rows, c]
            zero = jnp.zeros_like(q)
            for j, m in enumerate(mine):
                st = dot_nt(k, jnp.where(m, q, zero))
                p.append(jnp.exp(st - lse_ref[pl.ds(h + j, 1), rows]))
                dp.append(dot_nt(v, jnp.where(m, g, zero)))
            qs.append(q)
            gs.append(g)
        delta = [jnp.sum(a * b, axis=0, keepdims=True) for a, b in zip(p, dp)]
        ds = [(a * (b - d)).astype(BF16) for a, b, d in zip(p, dp, delta)]
        for i, (c, h) in enumerate(pairs):
            kt = eighth(k_ref[rows, c]).T
            dq = [dot(kt[j * HD:(j + 1) * HD, :], ds[2 * i + j]) for j in range(2)]
            dk = [dot(ds[2 * i + j], qs[i]) for j in range(2)]
            dv = [dot(p[2 * i + j].astype(BF16), gs[i]) for j in range(2)]
            dq_s[rows, c] = jnp.concatenate(dq, axis=0).T.astype(BF16)
            dk_s[rows, c] = jnp.where(mine[0], dk[0], dk[1]).astype(BF16)
            dv_s[rows, c] = jnp.where(mine[0], dv[0], dv[1]).astype(BF16)

    sequences(tab, rows_own // GRAN, work)
    own = pl.ds(HALO, rows_own)
    dq_o[...] = dq_s[own, :]
    dk_o[...] = dk_s[own, :]
    dv_o[...] = dv_s[own, :]
    sums[0:1, :] = jnp.sum(dq_o[...].astype(F32), axis=0, keepdims=True)
    sums[1:2, :] = jnp.sum(dv_o[...].astype(F32), axis=0, keepdims=True)


def attn_bwd_call(tab, q, k, v, lse, gl, go, gr):
    win, d = q.shape
    rows = go.shape[0]
    spec = pl.BlockSpec((win, LANES), lambda h, t: (0, h))
    own = pl.BlockSpec((rows, LANES), lambda h, t: (0, h))
    halo = pl.BlockSpec((HALO, LANES), lambda h, t: (0, h))
    out = jax.ShapeDtypeStruct((rows, d), BF16)
    return pl.pallas_call(
        attn_bwd_kernel,
        grid_spec=pltpu.PrefetchScalarGridSpec(
            num_scalar_prefetch=1,
            grid=(d // LANES,),
            in_specs=[spec] * 3 + [pl.BlockSpec((LANES // HD, win), lambda h, t: (h, 0)), halo, own, halo],
            out_specs=[own] * 3 + [pl.BlockSpec((8, LANES), lambda h, t: (0, h))],
            scratch_shapes=[pltpu.VMEM((win, LANES), BF16)] * 4,
        ),
        out_shape=[out] * 3 + [jax.ShapeDtypeStruct((8, d), F32)],
        compiler_params=params(),
        cost_estimate=cost(20 * rows * 512 * d, 14 * win * d, rows * 512 * 16),
        name="attn_bwd",
    )(tab, q, k, v, lse, gl, go, gr)


def norm_stats(z):
    cen = z - jnp.mean(z, axis=-1, keepdims=True)
    r = lax.rsqrt(jnp.mean(cen * cen, axis=-1, keepdims=True) + EPS)
    return cen * r, r


def norm_back(e, n, r):
    return r * (e - jnp.mean(e, axis=-1, keepdims=True) - n * jnp.mean(e * n, axis=-1, keepdims=True))


RC = 256
TF = 512
TC = 256


def chunks(rows, fn):
    def step(i, c):
        fn(pl.ds(pl.multiple_of(i * RC, RC), RC))
        return c

    lax.fori_loop(0, rows // RC, step, 0)


def clip(t, first, count):
    return jnp.clip(t - first, 0, count - 1)


def lanes(t, size):
    return pl.ds(pl.multiple_of(t * size, size), size)


def colsum(v):
    return jnp.sum(v, axis=0, keepdims=True)


def gelu_parts(u):
    phi = 0.5 * (1.0 + lax.erf(u * (0.5 ** 0.5)))
    return u * phi, phi + u * (0.3989422804014327 * jnp.exp(-0.5 * u * u))


def single(shape):
    return pl.BlockSpec(shape, lambda *_: (0,) * len(shape), pipeline_mode=pl.Buffered(1))


def grid_of(n):
    chips = n // 2
    return {16: (4, 2, 2), 64: (4, 4, 4)}.get(chips, (chips, 1, 1))


class Place:
    def __init__(self, n):
        self.n = n
        self.size = grid_of(n)
        me = lax.axis_index("dp")
        nz, ny, nx = self.size
        self.me = me
        self.c = lax.rem(me, 2)
        self.x = lax.rem(me // 2, nx)
        self.y = lax.rem(me // (2 * nx), ny)
        self.z = me // (2 * nx * ny)

    def at(self, axis, k):
        nz, ny, nx = self.size
        z, y, x, c = self.z, self.y, self.x, self.c
        if axis == "z":
            z = lax.rem(z + k, nz)
        elif axis == "y":
            y = lax.rem(y + k, ny)
        elif axis == "x":
            x = lax.rem(x + k, nx)
        else:
            c = lax.rem(c + k, 2)
        pos = {"z": z, "y": y, "x": x, "c": c}[axis]
        return ((z * ny + y) * nx + x) * 2 + c, pos

    def steps(self, axis):
        nz, ny, nx = self.size
        return range(1, {"z": nz, "y": ny, "x": nx, "c": 2}[axis])

    def peers(self):
        return [self.at(a, k)[0] for a in "zyxc" for k in self.steps(a)]


def enter(peers):
    sem = pltpu.get_barrier_semaphore()
    for p in peers:
        pl.semaphore_signal(sem, inc=1, device_id=(p,), device_id_type=MESH)
    pl.semaphore_wait(sem, len(peers))


def gather_slots(n):
    nz, ny, nx = grid_of(n)
    return (nz - 1) + 2 * (ny - 1) + 2 * (nx - 1) + 1


class Gather:
    def __init__(self, place, src, dst, rows, cols, ssem, rsem, lsem, index):
        self.p, self.index = place, index
        self.src, self.dst, self.rows, self.cols = src, dst, rows, cols
        self.ssem, self.rsem, self.lsem = ssem, rsem, lsem
        p = place
        r0, nr = rows
        c0, nc = cols
        rs = pl.ds(r0, nr)
        full = pl.ds(c0, nc)
        halves = (pl.ds(c0, nc // 2), pl.ds(c0 + nc // 2, nc // 2))
        al = pl.ds(0, p.size[0])
        self.local = pltpu.make_async_copy(src.at[rs, full], dst.at[p.z, p.y, p.x, p.c, rs, full], lsem.at[index])
        slot = 0

        def copy(s, d, dev):
            nonlocal slot
            cp = pltpu.make_async_remote_copy(src_ref=s, dst_ref=d, send_sem=ssem.at[index, slot], recv_sem=rsem.at[index, slot],
                                              device_id=(dev,), device_id_type=MESH)
            slot += 1
            return cp

        mine = dst.at[p.z, p.y, p.x, p.c, rs, full]
        self.ph = [[], [], [], []]
        for k in p.steps("z"):
            self.ph[0].append(copy(src.at[rs, full], mine, p.at("z", k)[0]))
        for h, axis in ((0, "y"), (1, "x")):
            s = dst.at[:, p.y, p.x, p.c, rs, halves[h]]
            for k in p.steps(axis):
                self.ph[1].append(copy(s, s, p.at(axis, k)[0]))
        for h, axis in ((0, "x"), (1, "y")):
            s = dst.at[:, :, p.x, p.c, rs, halves[0]] if h == 0 else dst.at[:, p.y, :, p.c, rs, halves[1]]
            for k in p.steps(axis):
                self.ph[2].append(copy(s, s, p.at(axis, k)[0]))
        s = dst.at[:, :, :, p.c, rs, full]
        self.ph[3].append(copy(s, s, p.at("c", 1)[0]))

    def start(self, i):
        if i == 0:
            self.local.start()
        for cp in self.ph[i]:
            cp.start()

    def wait(self, i):
        if i == 0:
            self.local.wait()
        for cp in self.ph[i]:
            cp.wait_recv()

    def sent(self):
        for ph in self.ph:
            for cp in ph:
                cp.wait_send()


def gather_go(g, ph):
    if ph > 0:
        g.wait(ph - 1)
    if ph < 4:
        g.start(ph)


def reduce_slots(n):
    nz, ny, nx = grid_of(n)
    return (nz - 1) + 2 * (ny - 1) + 2 * (nx - 1) + 1


def reduce_buffers(n, r, cols, dtype):
    nz, ny, nx = grid_of(n)
    h = cols // 2
    return [pltpu.VMEM((nz, ny, nx, r, cols), dtype),
            pltpu.VMEM((max(nx - 1, 1), nz, ny, r, h), dtype), pltpu.VMEM((max(ny - 1, 1), nz, nx, r, h), dtype),
            pltpu.VMEM((max(ny - 1, 1), nz, r, h), dtype), pltpu.VMEM((max(nx - 1, 1), nz, r, h), dtype),
            pltpu.VMEM((max(nz - 1, 1), r, cols), dtype), pltpu.VMEM((nz, r, cols), dtype), pltpu.VMEM((r, cols), F32)]


class Reduce:
    def __init__(self, place, src, own, bufs, out, ssem, rsem, lsem, index):
        self.p, self.src, self.own, self.bufs = place, src, own, bufs
        p = place
        self.h = bufs[1].shape[-1]
        self.ca, self.cb = pl.ds(0, self.h), pl.ds(self.h, self.h)
        if own is not None:
            self.get = pltpu.make_async_copy(src.at[:, :, :, p.c], own, lsem.at[index, 0])
        self.put = pltpu.make_async_copy(bufs[7], out, lsem.at[index, 1])
        slot = 0

        def copy(s, d, dev):
            nonlocal slot
            cp = pltpu.make_async_remote_copy(src_ref=s, dst_ref=d, send_sem=ssem.at[index, slot], recv_sem=rsem.at[index, slot],
                                              device_id=(dev,), device_id_type=MESH)
            slot += 1
            return cp

        self.ph = [[], [], [], []]
        dev, oc = p.at("c", 1)
        self.ph[0].append(copy(src.at[:, :, :, oc], bufs[0], dev))
        for k in p.steps("x"):
            dev, o = p.at("x", k)
            self.ph[1].append(copy(bufs[0].at[:, :, o, :, self.ca], bufs[1].at[k - 1], dev))
        for k in p.steps("y"):
            dev, o = p.at("y", k)
            self.ph[1].append(copy(bufs[0].at[:, o, :, :, self.cb], bufs[2].at[k - 1], dev))
        for k in p.steps("y"):
            dev, o = p.at("y", k)
            self.ph[2].append(copy(bufs[1].at[0, :, o], bufs[3].at[k - 1], dev))
        for k in p.steps("x"):
            dev, o = p.at("x", k)
            self.ph[2].append(copy(bufs[2].at[0, :, o], bufs[4].at[k - 1], dev))
        for k in p.steps("z"):
            dev, o = p.at("z", k)
            self.ph[3].append(copy(bufs[6].at[o], bufs[5].at[k - 1], dev))

    def go(self, i):
        if i == 0:
            self.ph[0][0].start()
            if self.own is not None:
                self.get.start()
            return
        p, bufs = self.p, self.bufs
        nz, ny, nx = p.size
        dt = bufs[0].dtype
        if i == 5:
            for cp in self.ph[1]:
                cp.start()
            return
        for cp in self.ph[i - 1]:
            cp.wait_recv()
        if i == 1:
            self.ph[0][0].wait_send()
            if self.own is not None:
                self.get.wait()

            def add(z, c):
                mine = self.own[z] if self.own is not None else self.src[z, :, :, pl.ds(p.c, 1)][:, :, 0]
                bufs[0][z] = (mine.astype(F32) + bufs[0][z].astype(F32)).astype(dt)
                return c

            lax.fori_loop(0, nz, add, 0)
            return
        elif i == 2:
            def add(z, c):
                a = bufs[0][z, :, pl.ds(p.x, 1), :, self.ca].astype(F32)[:, 0]
                for k in range(nx - 1):
                    a += bufs[1][k, z].astype(F32)
                bufs[1][0, z] = a.astype(dt)
                b = bufs[0][z, pl.ds(p.y, 1), :, :, self.cb].astype(F32)[0]
                for k in range(ny - 1):
                    b += bufs[2][k, z].astype(F32)
                bufs[2][0, z] = b.astype(dt)
                return c

            lax.fori_loop(0, nz, add, 0)
        elif i == 3:
            a = bufs[1][0, :, pl.ds(p.y, 1)].astype(F32)[:, 0]
            for k in range(ny - 1):
                a += bufs[3][k].astype(F32)
            bufs[6][:, :, self.ca] = a.astype(dt)
            b = bufs[2][0, :, pl.ds(p.x, 1)].astype(F32)[:, 0]
            for k in range(nx - 1):
                b += bufs[4][k].astype(F32)
            bufs[6][:, :, self.cb] = b.astype(dt)
        else:
            a = bufs[6][pl.ds(p.z, 1)].astype(F32)[0]
            for k in range(nz - 1):
                a += bufs[5][k].astype(F32)
            bufs[7][...] = a
            self.put.start()
            return
        for cp in self.ph[i]:
            cp.start()

    def finish(self):
        self.put.wait()
        for ph in self.ph[1:]:
            for cp in ph:
                cp.wait_send()


def run_at(t, events):
    for step in sorted({e[0] for e in events}):
        @pl.when(t == step)
        def _():
            for e in events:
                if e[0] == step:
                    e[1](*e[2:])


FIRST_PLAN = (
    (0, 1, 0), (0, 1, 1), (0, 0, 0), (0, 2, 0), (0, 1, 2), (0, 0, 1), (0, 7, 0), (0, 0, 2),
    (0, 6, 0), (0, 1, 3), (0, 2, 1), (0, 0, 3), (0, 7, 1), (0, 3, 0), (0, 2, 2), (0, 0, 4),
    (0, 1, 4), (1, 8, 0), (1, 5, 0), (2, 6, 1), (3, 7, 2), (3, 3, 1), (3, 6, 2), (3, 3, 2),
    (3, 4, 0), (4, 2, 3), (4, 5, 1), (4, 2, 4), (5, 4, 1), (5, 5, 2), (5, 7, 3), (7, 4, 2),
    (7, 8, 1), (8, 3, 3), (8, 3, 4), (9, 6, 3), (9, 7, 4), (10, 8, 2), (11, 5, 3), (11, 4, 3),
    (11, 8, 3), (12, 4, 4), (12, 6, 4), (12, 5, 4), (12, 8, 4),
)
ZERO_ROW, OB, DB, FG, FS, SG, SS, UB = 1, 3, 4, 5, 6, 7, 8, 9


def first_kernel(n, nc, ps, qs, ks, vs, os, us, xs, wq, wk, wv, wo, wu, vec, q, k, v,
                 x, pk, w3, y3, ssem, rsem, lsem, hs, hr, xsem, osem):
    t = pl.program_id(0)
    p = Place(n)
    rows, d = xs.shape
    r = qs.shape[0]
    right, left = lax.rem(p.me + 1, n), lax.rem(p.me + n - 1, n)
    edges = [pltpu.make_async_remote_copy(src_ref=xs.at[pl.ds(rows - HALO, HALO), :], dst_ref=x.at[pl.ds(0, HALO), :], send_sem=hs.at[0],
                                          recv_sem=hr.at[0], device_id=(right,), device_id_type=MESH),
             pltpu.make_async_remote_copy(src_ref=xs.at[pl.ds(0, HALO), :], dst_ref=x.at[pl.ds(HALO + rows, HALO), :], send_sem=hs.at[1],
                                          recv_sem=hr.at[1], device_id=(left,), device_id_type=MESH)]
    mine = pltpu.make_async_copy(xs, x.at[pl.ds(HALO, rows), :], xsem)
    plan = [(ps, pk, 0), (qs, w3.at[0], 0), (ks, w3.at[1], 0), (vs, w3.at[2], 0), (os, wo, 0)] + [(us, wu, j * d) for j in range(us.shape[1] // d)]
    g = [Gather(p, a, b, (0, a.shape[0]), (c, d), ssem, rsem, lsem, i) for i, (a, b, c) in enumerate(plan)]
    weights = [pltpu.make_async_copy(w3.at[i], o, osem.at[i]) for i, o in enumerate((wq, wk, wv))]
    results = [pltpu.make_async_copy(y3.at[i], o, osem.at[3 + i]) for i, o in enumerate((q, k, v))]

    def vectors():
        vec[...] = jnp.sum(pk[...].astype(F32).reshape(n, pk.shape[-2], d), axis=0)

    @pl.when(t == 0)
    def _():
        enter(p.peers() + [left, right])

    @pl.when((t > 0) & (t <= 3 * nc))
    def _():
        i = (t - 1) // nc
        c = lanes(lax.rem(t - 1, nc), TC)
        y = dot(x[...], w3[pl.ds(i, 1), ..., c].reshape(d, TC)) + vec[pl.ds(i, 1), c]
        y3[pl.ds(i, 1), :, c] = y.astype(BF16)[None]

    events = []
    for step, i, ph in FIRST_PLAN:
        events.append((step, gather_go, g[i], ph))
        if i == 0 and ph == 0:
            events += [(0, mine.start)] + [(0, c.start) for c in edges]
        if ph == 4 and i == 0:
            events.append((step, vectors))
        if ph == 4 and 1 <= i <= 3:
            events.append((step, weights[i - 1].start))
    events += [(0, mine.wait)] + [(0, c.wait_recv) for c in edges]
    events += [((i + 1) * nc, c.start) for i, c in enumerate(results)]
    last = 3 * nc
    events += [(last, c.sent) for c in g] + [(last, c.wait_send) for c in edges] + [(last, c.wait) for c in weights + results]
    run_at(t, events)


def first_call(n, packed, wq, wk, wv, wo, wu, x):
    rows, d = x.shape
    win = rows + 2 * HALO
    nc = d // TC
    r = wq.shape[0]
    z = grid_of(n) + (2,)
    count = 5 + wu.shape[1] // d
    k = gather_slots(n)
    mat = jax.ShapeDtypeStruct(z + (r, d), BF16)
    out = jax.ShapeDtypeStruct((win, d), BF16)
    res = pl.pallas_call(
        functools.partial(first_kernel, n, nc),
        grid=(3 * nc + 1,),
        in_specs=[ANY] * 7,
        out_specs=[ANY] * 5 + [single(packed.shape)] + [ANY] * 3,
        out_shape=[mat] * 4 + [jax.ShapeDtypeStruct(z + wu.shape, BF16), jax.ShapeDtypeStruct(packed.shape, F32)] + [out] * 3,
        scratch_shapes=[pltpu.VMEM((win, d), BF16), pltpu.VMEM(z + packed.shape, BF16), pltpu.VMEM((3,) + z + (r, d), BF16),
                        pltpu.VMEM((3, win, d), BF16), pltpu.SemaphoreType.DMA((count, k)), pltpu.SemaphoreType.DMA((count, k)),
                        pltpu.SemaphoreType.DMA((count,)), pltpu.SemaphoreType.DMA((2,)), pltpu.SemaphoreType.DMA((2,)),
                        pltpu.SemaphoreType.DMA, pltpu.SemaphoreType.DMA((6,))],
        compiler_params=pltpu.CompilerParams(collective_id=1, has_side_effects=True, vmem_limit_bytes=56 << 20),
        cost_estimate=cost(6 * win * d * d, 2 * (4 * win * d + 3 * d * d)),
        name="first",
    )(packed, wq, wk, wv, wo, wu, x)
    ws = [w.reshape((-1, w.shape[-1])) for w in res[:5]]
    return ws + list(res[5:])


DOWN_PLAN = (
    (0, 1, 0), (2, 1, 1), (2, 0, 0), (3, 1, 2), (3, 2, 0), (3, 0, 1), (4, 2, 1), (4, 3, 0),
    (4, 0, 2), (6, 3, 1), (6, 1, 3), (6, 2, 2), (7, 0, 3), (8, 3, 2), (9, 2, 3), (9, 1, 4),
    (9, 0, 4), (10, 3, 3), (11, 2, 4), (11, 3, 4),
)


def fwd_kernel(n, nu, nc, ctx, wo, x, wu, wds, g, vec, xhat, lowt, ctxt, r1, hidt, dg, out, gs, gd, sums, wd, z, hid, low, wt,
               ssem, rsem, lsem, wsem):
    t = pl.program_id(0)
    rows, d = x.shape
    p = Place(n)
    blocks = len(set(e[1] for e in DOWN_PLAN))
    r = wds.shape[0] // blocks
    ga = [Gather(p, wds, wd, (i * r, r), (0, d), ssem, rsem, lsem, i) for i in range(blocks)]
    fetch = [pltpu.make_async_copy(wd.at[:, :, :, :, :, pl.ds(j * TC, TC)], wt.at[j % 2], wsem.at[j]) for j in range(nc)]
    first = nc + nu

    @pl.when(t == 0)
    def _():
        enter(p.peers())

    run_at(t, [(first + j, fetch[j].wait) for j in range(nc)] + [(first + j, fetch[j + 1].start) for j in range(nc - 1)])

    @pl.when(t < nc)
    def _():
        c = lanes(t, TC)
        z[:, c] = dot(ctx[...], wo[...]) + x[:, c].astype(F32)

    @pl.when(t == nc - 1)
    def _():
        def fin(r):
            n, rr = norm_stats(z[r, :] + vec[OB:OB + 1, :])
            xhat[r, :] = n
            r1[r, :] = jnp.broadcast_to(rr, (RC, r1.shape[1]))
            v = (n * vec[FG:FG + 1, :] + vec[FS:FS + 1, :]).astype(BF16)
            low[r, :] = v
            lowt[:, r] = v.T
            ctxt[:, r] = ctx[r, :].T

        chunks(rows, fin)

    @pl.when((t >= nc) & (t < nc + nu))
    def _():
        for j in range(TF // TC):
            c = slice(j * TC, (j + 1) * TC)
            tile = (t - nc) * (TF // TC) + j
            bias = vec[pl.ds(UB + tile // (d // TC), 1), lanes(lax.rem(tile, d // TC), TC)]
            h, s = gelu_parts(dot(low[...], wu[:, c]) + bias)
            h = h.astype(BF16)
            dg[:, c] = s.astype(BF16)
            hid[:, lanes(tile, TC)] = h
            hidt[c, :] = h.T

    @pl.when(t >= nc + nu)
    def _():
        c = lanes(t - nc - nu, TC)
        z[:, c] = dot(hid[...], wt[pl.ds(lax.rem(t - first, 2), 1)].reshape(hid.shape[1], TC))

    @pl.when(t == 2 * nc + nu - 1)
    def _():
        sums[...] = jnp.zeros_like(sums)

        def fin(r):
            v = (xhat[r, :] * vec[FG:FG + 1, :] + vec[FS:FS + 1, :]) + (z[r, :] + vec[DB:DB + 1, :])
            n, rr = norm_stats(v)
            out[r, :] = (n * vec[SG:SG + 1, :] + vec[SS:SS + 1, :]).astype(BF16)
            gv = g[r, :].astype(F32)
            sums[0:1, :] += colsum(gv * n)
            sums[1:2, :] += colsum(gv)
            grad = norm_back(gv * vec[SG:SG + 1, :], n, rr)
            gs[r, :] = grad
            low_g = grad.astype(BF16)
            gd[r, :] = low_g
            sums[2:3, :] += colsum(low_g.astype(F32))

        chunks(rows, fin)

    run_at(t, [(e[0], gather_go, ga[e[1]], e[2]) for e in DOWN_PLAN] + [(first - 1, c.sent) for c in ga] + [(first - 1, fetch[0].start)])


def fwd_call(n, ctx, wo, x, wu, wd, g, vec):
    rows, d = x.shape
    ff = wu.shape[1]
    nu, nc = ff // TF, d // TC
    z = grid_of(n) + (2,)
    k = gather_slots(n)
    blocks = ff // d
    full = jax.ShapeDtypeStruct(z + wd.shape, BF16)
    *res, down = pl.pallas_call(
        functools.partial(fwd_kernel, n, nu, nc),
        grid=(2 * nc + nu,),
        in_specs=[single(ctx.shape), pl.BlockSpec((d, TC), lambda t: (0, clip(t, 0, nc))), single(x.shape),
                  pl.BlockSpec((d, TF), lambda t: (0, clip(t, nc, nu))), ANY, single(g.shape), single(vec.shape)],
        out_specs=[single((rows, d)), single((d, rows)), single((d, rows)), single((rows, 128)),
                   pl.BlockSpec((TF, rows), lambda t: (clip(t, nc, nu), 0)), pl.BlockSpec((rows, TF), lambda t: (0, clip(t, nc, nu))),
                   single((rows, d)), single((rows, d)), single((rows, d)), single((8, d)), ANY],
        out_shape=[jax.ShapeDtypeStruct((rows, d), F32), jax.ShapeDtypeStruct((d, rows), BF16), jax.ShapeDtypeStruct((d, rows), BF16),
                   jax.ShapeDtypeStruct((rows, 128), F32), jax.ShapeDtypeStruct((ff, rows), BF16),
                   jax.ShapeDtypeStruct((rows, ff), BF16), jax.ShapeDtypeStruct((rows, d), BF16),
                   jax.ShapeDtypeStruct((rows, d), F32), jax.ShapeDtypeStruct((rows, d), BF16), jax.ShapeDtypeStruct((8, d), F32), full],
        scratch_shapes=[pltpu.VMEM((rows, d), F32), pltpu.VMEM((rows, ff), BF16), pltpu.VMEM((rows, d), BF16),
                        pltpu.VMEM((2,) + z + (wd.shape[0], TC), BF16), pltpu.SemaphoreType.DMA((blocks, k)),
                        pltpu.SemaphoreType.DMA((blocks, k)), pltpu.SemaphoreType.DMA((blocks,)), pltpu.SemaphoreType.DMA((nc,))],
        compiler_params=pltpu.CompilerParams(collective_id=2, has_side_effects=True, vmem_limit_bytes=62 << 20),
        cost_estimate=cost(4 * rows * d * ff, 4 * d * ff + 4 * rows * ff + rows * d * 14, 2 * rows * ff),
        name="fwd",
    )(ctx, wo, x, wu, wd, g, vec)
    return res + [down.reshape(ff, d)]


BWD_PLAN = (
    (1, 1, 0, 0), (1, 1, 1, 0), (2, 0, 0, 1), (2, 0, 0, 5), (2, 0, 1, 1), (3, 1, 3, 0),
    (3, 1, 1, 5), (3, 1, 0, 2), (3, 1, 2, 0), (4, 0, 3, 1), (4, 0, 3, 5), (4, 0, 2, 1),
    (5, 1, 5, 0), (5, 1, 1, 2), (5, 1, 4, 0), (6, 0, 0, 3), (6, 0, 2, 5), (6, 0, 5, 1),
    (6, 0, 4, 1), (6, 0, 4, 5), (7, 0, 3, 2), (7, 0, 1, 3), (8, 1, 5, 5), (9, 1, 2, 2),
    (10, 1, 3, 3), (12, 1, 2, 3), (12, 1, 5, 2), (14, 1, 4, 2), (15, 1, 5, 3), (20, 1, 4, 3),
    (21, 1, 1, 4), (22, 1, 2, 4), (23, 1, 3, 4), (23, 1, 5, 4), (23, 1, 0, 4), (23, 1, 4, 4),
)
EARLY = 6


def bwd_kernel(n, nu, nc, nr, gd, lowt, hidt, dg, wd, wu, gs, xhat, r1, vec, wo, ctxt,
               gsf, sums, sumu, gc, dwo, rd, ru, gl, gr, *rest):
    t = pl.program_id(0)
    d, rows = lowt.shape
    per = d // TF
    count = 2 * (nu // per)
    late = rest[:count - EARLY]
    gu, bufd, bufu, ga = rest[count - EARLY:count - EARLY + 4]
    rest = rest[count - EARLY + 4:]
    ssem, rsem, lsem, wsem, hs, hr = rest[-6:]
    p = Place(n)
    r = d // n
    red = []
    for i in range(EARLY):
        j = i // 2
        out = rd.at[pl.ds(j * r, r), :] if i % 2 == 0 else ru.at[:, pl.ds(j * d, d)]
        red.append(Reduce(p, (bufd, bufu)[i % 2], None, rest[8 * i:8 * i + 8], out, ssem, rsem, lsem, i))
    right, left = lax.rem(p.me + 1, n), lax.rem(p.me + n - 1, n)
    edges = [pltpu.make_async_remote_copy(src_ref=gc.at[pl.ds(rows - HALO, HALO), :], dst_ref=gl, send_sem=hs.at[0], recv_sem=hr.at[0],
                                          device_id=(right,), device_id_type=MESH),
             pltpu.make_async_remote_copy(src_ref=gc.at[pl.ds(0, HALO), :], dst_ref=gr, send_sem=hs.at[1], recv_sem=hr.at[1],
                                          device_id=(left,), device_id_type=MESH)]
    last = nu + 3 * nc + nr - 1
    mid = [(e[0], red[e[2]].go, e[3]) for e in BWD_PLAN if e[1] == 0]
    end = [(e[0], red[e[2]].go, e[3]) for e in BWD_PLAN if e[1] == 1]
    for i in range(EARLY, count):
        c = pltpu.make_async_copy((bufd, bufu)[i % 2], late[i - EARLY], wsem.at[i - EARLY])
        end.append((per * (i // 2 + 1) - 1, c.start))
        if per * (i // 2 + 1) < nu:
            mid.append((per * (i // 2 + 1), c.wait))
        else:
            end.append((last, c.wait))
    end += [(nu + 2 * nc + nr - 1, c.start) for c in edges] + [(last, c.wait) for c in edges]
    end += [(last, c.finish) for c in red]

    @pl.when(t == 0)
    def _():
        enter(p.peers() + [left, right])

    @pl.when(t < nu)
    def _():
        for j in range(TF // TC):
            c = slice(j * TC, (j + 1) * TC)
            g = (dot_nt(gd[...], wd[c, :]) * dg[:, c].astype(F32)).astype(BF16)
            gu[:, lanes(t * (TF // TC) + j, TC)] = g
            sumu[:, c] = colsum(g.astype(F32))

    run_at(t, mid)

    @pl.when(t < nu)
    def _():
        half = lax.rem(t, per)
        for j in range(TF // TC):
            c = lanes(half * (TF // TC) + j, TC)
            bufu[..., c] = dot(lowt[...], gu[:, lanes(t * (TF // TC) + j, TC)]).astype(BF16).reshape(bufu.shape[:-1] + (TC,))
            bufd[..., c] = dot(hidt[...].reshape(d, rows), gd[:, c]).astype(BF16).reshape(bufd.shape[:-1] + (TC,))

    @pl.when((t >= nu) & (t < nu + nc))
    def _():
        gsf[:, lanes(t - nu, TC)] = gs[...] + dot_nt(gu[...], wu[...])

    @pl.when(t == nu + nc)
    def _():
        sums[...] = jnp.zeros_like(sums)

    @pl.when((t >= nu + nc) & (t < nu + nc + nr))
    def _():
        at = lanes(t - nu - nc, RC)
        gf = gsf[at, :]
        nn = xhat[...]
        sums[0:1, :] += colsum(gf * nn)
        sums[1:2, :] += colsum(gf)
        grad = norm_back(gf * vec[FG:FG + 1, :], nn, r1[:, 0:1])
        gsf[at, :] = grad
        low_g = grad.astype(BF16)
        ga[at, :] = low_g
        sums[2:3, :] += colsum(low_g.astype(F32))

    first = nu + nc + nr

    @pl.when((t >= first) & (t < first + nc))
    def _():
        gc[:, lanes(t - first, TC)] = dot_nt(ga[...], wo[...]).astype(BF16)

    @pl.when(t >= first + nc)
    def _():
        dwo[...] = dot(ctxt[...], ga[:, lanes(t - first - nc, TC)]).astype(BF16)

    run_at(t, end)


def bwd_call(n, gd, lowt, hidt, dg, wd, wu, gs, xhat, r1, vec, wo, ctxt):
    d, rows = lowt.shape
    ff = wu.shape[1]
    nu, nc, nr = ff // TF, d // TC, rows // RC
    r = d // n
    parts = ff // d
    z = grid_of(n) + (2, r)
    per = d // TF
    chunk = jax.ShapeDtypeStruct(z + (d,), BF16)
    k = reduce_slots(n)
    late = 2 * parts - EARLY
    scratch = [pltpu.VMEM((rows, ff), BF16), pltpu.VMEM(z + (d,), BF16), pltpu.VMEM(z + (d,), BF16), pltpu.VMEM((rows, d), BF16)]
    for i in range(EARLY):
        scratch += reduce_buffers(n, r, d, BF16)
    scratch += [pltpu.SemaphoreType.DMA((EARLY, k)), pltpu.SemaphoreType.DMA((EARLY, k)), pltpu.SemaphoreType.DMA((EARLY, 2)),
                pltpu.SemaphoreType.DMA((late,)), pltpu.SemaphoreType.DMA((2,)), pltpu.SemaphoreType.DMA((2,))]
    edge = jax.ShapeDtypeStruct((HALO, d), BF16)
    first = nu + nc + nr
    return pl.pallas_call(
        functools.partial(bwd_kernel, n, nu, nc, nr),
        grid=(nu + 3 * nc + nr,),
        in_specs=[single(gd.shape), single(lowt.shape),
                  pl.BlockSpec((n, 1, r, rows), lambda t: (0, clip(t, 0, nu) // per, 0, 0)),
                  pl.BlockSpec((rows, TF), lambda t: (0, clip(t, 0, nu))), pl.BlockSpec((TF, d), lambda t: (clip(t, 0, nu), 0)),
                  pl.BlockSpec((TC, ff), lambda t: (clip(t, nu, nc), 0)), pl.BlockSpec((rows, TC), lambda t: (0, clip(t, nu, nc))),
                  pl.BlockSpec((RC, d), lambda t: (clip(t, nu + nc, nr), 0)), pl.BlockSpec((RC, 128), lambda t: (clip(t, nu + nc, nr), 0)),
                  single(vec.shape), pl.BlockSpec((TC, d), lambda t: (clip(t, first, nc), 0)), single(ctxt.shape)],
        out_specs=[single((rows, d)), single((8, d)), pl.BlockSpec((1, TF), lambda t: (0, clip(t, 0, nu))), single((rows, d)),
                   pl.BlockSpec((d, TC), lambda t: (0, clip(t, first + nc, nc)))] + [ANY] * (4 + late),
        out_shape=[jax.ShapeDtypeStruct((rows, d), F32), jax.ShapeDtypeStruct((8, d), F32), jax.ShapeDtypeStruct((1, ff), F32),
                   jax.ShapeDtypeStruct((rows, d), BF16), jax.ShapeDtypeStruct((d, d), BF16),
                   jax.ShapeDtypeStruct(((EARLY + 1) // 2 * r, d), F32), jax.ShapeDtypeStruct((r, EARLY // 2 * d), F32), edge, edge]
        + [chunk] * late,
        scratch_shapes=scratch,
        compiler_params=pltpu.CompilerParams(collective_id=3, has_side_effects=True, vmem_limit_bytes=62 << 20),
        cost_estimate=cost(8 * rows * d * ff, 8 * d * ff + 4 * rows * ff + rows * d * 18),
        name="bwd",
    )(gd, lowt, hidt.reshape(n, parts, r, rows), dg, wd, wu, gs, xhat, r1, vec, wo, ctxt)


IN_PLAN = (
    (0, 6, 0), (0, 1, 0), (2, 6, 1), (2, 2, 0), (2, 6, 5), (3, 1, 1), (3, 1, 5), (4, 6, 2),
    (4, 3, 0), (5, 3, 1), (5, 3, 5), (5, 1, 2), (5, 0, 0), (6, 2, 1), (7, 4, 0), (7, 2, 5),
    (7, 4, 1), (8, 4, 5), (9, 1, 3), (10, 0, 1), (10, 6, 3), (10, 0, 5), (10, 3, 2), (11, 3, 3),
    (11, 5, 0), (11, 2, 2), (12, 0, 2), (12, 5, 1), (12, 6, 4), (12, 5, 5), (12, 2, 3), (12, 4, 2),
    (13, 0, 3), (13, 4, 3), (13, 5, 2), (13, 5, 3), (13, 1, 4), (14, 2, 4), (15, 0, 4), (15, 4, 4),
    (15, 3, 4), (15, 5, 4),
)


def in_bwd_kernel(n, nc, left, x, gsf, dq, dk, dv, wq, wk, wv, *rest):
    t = pl.program_id(0)
    srcs, rest = rest[:left + 2], rest[left + 2:]
    tg, outs, rest = rest[0], rest[1:left + 6], rest[left + 6:]
    xt, bq, bk, bv, owns, rest = rest[0], rest[1], rest[2], rest[3], rest[4:left + 6], rest[left + 6:]
    ssem, rsem, lsem = rest[-3:]
    p = Place(n)
    plan = list(zip(srcs[:-1], owns[:-1])) + [(b, None) for b in (bq, bk, bv)] + [(srcs[-1], owns[-1])]
    red = [Reduce(p, s, o, rest[8 * i:8 * i + 8], outs[i], ssem, rsem, lsem, i) for i, (s, o) in enumerate(plan)]

    @pl.when(t == 0)
    def _():
        enter(p.peers())
        xt[...] = x[...].T

    for i, (a, b) in enumerate(((dq, bq), (dk, bk), (dv, bv))):
        @pl.when((t >= i * nc) & (t < (i + 1) * nc))
        def _():
            c = lanes(t - i * nc, TC)
            b[..., c] = dot(xt[...], a[:, c]).astype(BF16).reshape(b.shape[:-1] + (TC,))

    @pl.when(t >= 3 * nc)
    def _():
        g = gsf[...] + dot_nt(dq[...], wq[...]) + dot_nt(dk[...], wk[...]) + dot_nt(dv[...], wv[...])
        tg[...] = g.astype(BF16)

    run_at(t, [(e[0], red[e[1]].go, e[2]) for e in IN_PLAN] + [(4 * nc - 1, c.finish) for c in red])


def in_bwd_call(n, x, gsf, dq, dk, dv, wq, wk, wv, late, dwo, small):
    rows, d = x.shape
    nc = d // TC
    r = d // n
    z = grid_of(n)
    col = pl.BlockSpec((rows, TC), lambda t: (0, clip(t, 3 * nc, nc)))
    wrow = pl.BlockSpec((TC, d), lambda t: (clip(t, 3 * nc, nc), 0))
    chunk = pltpu.VMEM(z + (2, r, d), BF16)
    own = pltpu.VMEM(z + (r, d), BF16)
    share = jax.ShapeDtypeStruct((r, d), F32)
    sr, sc = small.shape[0] // n, small.shape[1]
    k = reduce_slots(n)
    left = len(late)
    total = left + 5
    scratch = [pltpu.VMEM((d, rows), BF16)] + [chunk] * 3 + [own] * (left + 1) + [pltpu.VMEM(z + (sr, sc), F32)]
    for i in range(total - 1):
        scratch += reduce_buffers(n, r, d, BF16)
    scratch += reduce_buffers(n, sr, sc, F32)
    scratch += [pltpu.SemaphoreType.DMA((total, k)), pltpu.SemaphoreType.DMA((total, k)), pltpu.SemaphoreType.DMA((total, 2))]
    return pl.pallas_call(
        functools.partial(in_bwd_kernel, n, nc, left),
        grid=(4 * nc,),
        in_specs=[single((rows, d)), col] + [single((rows, d))] * 3 + [wrow] * 3 + [ANY] * (left + 2),
        out_specs=[col] + [ANY] * total,
        out_shape=[jax.ShapeDtypeStruct((rows, d), BF16)] + [share] * (left + 4) + [jax.ShapeDtypeStruct((sr, sc), F32)],
        scratch_shapes=scratch,
        compiler_params=pltpu.CompilerParams(collective_id=5, has_side_effects=True, vmem_limit_bytes=62 << 20),
        cost_estimate=cost(12 * rows * d * d, rows * d * 14 + 12 * d * d),
        name="in_bwd",
    )(x, gsf, dq, dk, dv, wq, wk, wv, *late, dwo.reshape(z + (2, r, d)), small.reshape(z + (2, sr, sc)))


def hand_on_kernel(groups, axes, *refs):
    total = sum(groups)
    at = 0
    for g, axis, out in zip(groups, axes, refs[total:]):
        start = 0
        for a in refs[at:at + g]:
            size = a.shape[axis]
            if axis == 0:
                out[start:start + size, :] = a[...]
            else:
                out[:, start:start + size] = a[...]
            start += size
        at += g


def hand_on(parts, axes):
    shapes = []
    for ps, axis in zip(parts, axes):
        shape = list(ps[0].shape)
        shape[axis] = sum(p.shape[axis] for p in ps)
        shapes.append(jax.ShapeDtypeStruct(tuple(shape), ps[0].dtype))
    return pl.pallas_call(
        functools.partial(hand_on_kernel, tuple(len(p) for p in parts), axes),
        out_shape=shapes,
        name="hand_on",
    )(*[a for p in parts for a in p])


def sequence_table(lengths, own, rows):
    ids = jnp.arange(lengths.shape[0], dtype=jnp.int32)
    starts = jnp.sum(jnp.where(ids[None, :] < ids[:, None], lengths[None, :], 0), axis=1)
    blocks = rows // GRAN
    at = own * rows + jnp.arange(blocks, dtype=jnp.int32) * GRAN
    inside = (starts[None, :] <= at[:, None]) & (at[:, None] < (starts + lengths)[None, :])
    first = jnp.sum(jnp.where(inside, starts[None, :], 0), axis=1)
    length = jnp.sum(jnp.where(inside, lengths[None, :], 0), axis=1)
    lead = (first == at) | (jnp.arange(blocks) == 0)
    return jnp.stack([(first - own * rows + HALO) // GRAN, jnp.where(lead, length // GRAN, 0)]).astype(jnp.int32)


def pack(values, n, rows, dtype):
    cols = [v.reshape(n, -1) for v in values]
    flat = jnp.concatenate(cols, axis=1)
    return jnp.pad(flat, ((0, 0), (0, rows * 256 - flat.shape[1]))).astype(dtype).reshape(n * rows, 256)


def unpack(packed, n, part):
    flat = packed.reshape(n, -1)
    vec = flat[:, : 8 * part].reshape(n, 8, part).transpose(1, 0, 2).reshape(8, n * part)
    return vec, flat[:, 8 * part:12 * part].reshape(1, -1)


def local(tokens, cotangent, lengths, dealing, *shards):
    n = lax.axis_size("dp")
    own = lax.axis_index("dp")
    rows, d = tokens.shape
    part = d // n
    qb, vb, ob, ub, db, fg, fs, sg, ss = shards[6:]
    mine = jnp.stack([qb, jnp.zeros_like(qb), vb, ob, db, fg, fs, sg, ss])
    mine = lax.dynamic_update_slice(jnp.zeros((UB, d), BF16), mine, (0, own * part))
    ups = lax.dynamic_update_slice(jnp.zeros((ub.shape[0] * n,), BF16), ub, (own * ub.shape[0],)).reshape(-1, d)
    packed = jnp.concatenate([mine, ups, jnp.zeros((16 - UB - ups.shape[0], d), BF16)])
    wq, wk, wv, wo, wu, vec, q, k, v = first_call(n, packed, *shards[:5], tokens)
    tab = sequence_table(lengths, own, rows)
    ctx, lse = attn_fwd_call(tab, q, k, v, rows)
    xhat, lowt, ctxt, r1, hidt, dg, layer_out, gs, gd, sums2, wd = fwd_call(n, ctx, wo, tokens, wu, shards[5], cotangent, vec)
    gsf, sums1, sumu, gc, dwo, rd, ru, gl, gr, *late = bwd_call(n, gd, lowt, hidt, dg, wd, wu, gs, xhat, r1, vec, wo, ctxt)
    dq, dk, dv, sums0 = attn_bwd_call(tab, q, k, v, lse, gl, gc, gr)
    small = pack([sums0[0], sums0[1], sums1[2], sums2[2], sums1[0], sums1[1], sums2[0], sums2[1], sumu], n, 8, F32)
    tg, *more = in_bwd_call(n, tokens, gsf, dq, dk, dv, wq, wk, wv, late, dwo, small)
    left = len(late)
    go, gq, gk, gv, tiny = more[left:]
    downs = [rd] + [more[i] for i in range(left) if (EARLY + i) % 2 == 0]
    ups = [ru] + [more[i] for i in range(left) if (EARLY + i) % 2 == 1]
    gq, gk, gv, go, gu, gd, tg, layer_out = hand_on([[gq], [gk], [gv], [go], ups, downs, [tg], [layer_out]], (0, 0, 0, 0, 1, 0, 0, 0))
    vecs, ubg = unpack(tiny, 1, part)
    t = [vecs[i] for i in range(8)]
    return (layer_out, tg, gq, gk, gv, go, gu, gd, t[0], t[1], t[2], ubg[0], t[3], t[4], t[5], t[6], t[7])


def solution(mesh):
    mat = P("dp", None)
    vec = P("dp")
    return jax.shard_map(
        local,
        mesh=mesh,
        in_specs=(mat, mat, P(), P()) + (mat,) * 6 + (vec,) * 9,
        out_specs=(mat,) * 8 + (vec,) * 9,
        check_vma=False,
    )
```

```python
import functools

import jax
import jax.numpy as jnp
from jax import lax
from jax.experimental import pallas as pl
from jax.experimental.pallas import tpu as pltpu
from jax.sharding import PartitionSpec as P

HD = 64
GRAN = 128
HALO = 384
EPS = 1e-12
F32 = jnp.float32
BF16 = jnp.bfloat16
NT = (((1,), (1,)), ((), ()))
MESH = pl.DeviceIdType.MESH
ANY = pl.BlockSpec(memory_space=pl.ANY)


def params(limit=56):
    return pltpu.CompilerParams(vmem_limit_bytes=limit << 20)


def whole(shape):
    return pl.BlockSpec(shape, lambda *_: (0,) * len(shape))


def dot(a, b):
    return jnp.dot(a, b, preferred_element_type=F32)


def dot_nt(a, b):
    return lax.dot_general(a, b, NT, preferred_element_type=F32)


def cost(flops, nbytes, trans=0):
    return pl.CostEstimate(flops=flops, bytes_accessed=nbytes, transcendentals=trans)


LANES = 512
TOGETHER = {1: 4, 2: 2, 3: 1, 4: 1}


def sequences(tab, blocks, fn):
    def one(b, c):
        n = tab[1, b]
        s0 = tab[0, b]
        for nn in range(1, 5):
            @pl.when(n == nn)
            def _():
                rows = pl.ds(pl.multiple_of(s0 * GRAN, GRAN), nn * GRAN)
                per = TOGETHER[nn]

                def group(i, c):
                    pairs = [i * per + j for j in range(per)]
                    fn(rows, [(pl.ds(pl.multiple_of(p * 2 * HD, 2 * HD), 2 * HD), 2 * p) for p in pairs])
                    return c

                lax.fori_loop(0, LANES // (2 * HD) // per, group, 0)
        return c

    lax.fori_loop(0, blocks, one, 0)


def masks(shape):
    low = lax.broadcasted_iota(jnp.int32, shape, 1) < HD
    return low, ~low


def eighth(x):
    return x * jnp.asarray(0.125, BF16)


def attn_bwd_kernel(tab, q_ref, k_ref, v_ref, ll, lo, lr, gl, go, gr, dq_o, dk_o, dv_o, sums, lse_ref, g_s, dq_s, dk_s, dv_s):
    rows_own = go.shape[0]
    lse_ref[:, pl.ds(0, HALO)] = ll[...]
    lse_ref[:, pl.ds(HALO, rows_own)] = lo[...]
    lse_ref[:, pl.ds(HALO + rows_own, HALO)] = lr[...]
    g_s[pl.ds(0, HALO), :] = gl[...]
    g_s[pl.ds(HALO, rows_own), :] = go[...]
    g_s[pl.ds(HALO + rows_own, HALO), :] = gr[...]

    def work(rows, pairs):
        mine = masks((rows.size, 2 * HD))
        qs, gs, p, dp = [], [], [], []
        for c, h in pairs:
            q, k, v, g = eighth(q_ref[rows, c]), k_ref[rows, c], v_ref[rows, c], g_s[rows, c]
            zero = jnp.zeros_like(q)
            for j, m in enumerate(mine):
                st = dot_nt(k, jnp.where(m, q, zero))
                p.append(jnp.exp(st - lse_ref[pl.ds(h + j, 1), rows]))
                dp.append(dot_nt(v, jnp.where(m, g, zero)))
            qs.append(q)
            gs.append(g)
        delta = [jnp.sum(a * b, axis=0, keepdims=True) for a, b in zip(p, dp)]
        ds = [(a * (b - d)).astype(BF16) for a, b, d in zip(p, dp, delta)]
        for i, (c, h) in enumerate(pairs):
            kt = eighth(k_ref[rows, c]).T
            dq = [dot(kt[j * HD:(j + 1) * HD, :], ds[2 * i + j]) for j in range(2)]
            dk = [dot(ds[2 * i + j], qs[i]) for j in range(2)]
            dv = [dot(p[2 * i + j].astype(BF16), gs[i]) for j in range(2)]
            dq_s[rows, c] = jnp.concatenate(dq, axis=0).T.astype(BF16)
            dk_s[rows, c] = jnp.where(mine[0], dk[0], dk[1]).astype(BF16)
            dv_s[rows, c] = jnp.where(mine[0], dv[0], dv[1]).astype(BF16)

    sequences(tab, rows_own // GRAN, work)
    own = pl.ds(HALO, rows_own)
    dq_o[...] = dq_s[own, :]
    dk_o[...] = dk_s[own, :]
    dv_o[...] = dv_s[own, :]
    sums[0:1, :] = jnp.sum(dq_o[...].astype(F32), axis=0, keepdims=True)
    sums[1:2, :] = jnp.sum(dv_o[...].astype(F32), axis=0, keepdims=True)


def attn_bwd_call(tab, q, k, v, ll, lse, lr, gl, go, gr):
    win, d = q.shape
    rows = go.shape[0]
    spec = pl.BlockSpec((win, LANES), lambda h, t: (0, h))
    own = pl.BlockSpec((rows, LANES), lambda h, t: (0, h))
    halo = pl.BlockSpec((HALO, LANES), lambda h, t: (0, h))
    out = jax.ShapeDtypeStruct((rows, d), BF16)
    return pl.pallas_call(
        attn_bwd_kernel,
        grid_spec=pltpu.PrefetchScalarGridSpec(
            num_scalar_prefetch=1,
            grid=(d // LANES,),
            in_specs=[spec] * 3 + [pl.BlockSpec((LANES // HD, a.shape[1]), lambda h, t: (h, 0)) for a in (ll, lse, lr)] + [halo, own, halo],
            out_specs=[own] * 3 + [pl.BlockSpec((8, LANES), lambda h, t: (0, h))],
            scratch_shapes=[pltpu.VMEM((LANES // HD, win), F32)] + [pltpu.VMEM((win, LANES), BF16)] * 4,
        ),
        out_shape=[out] * 3 + [jax.ShapeDtypeStruct((8, d), F32)],
        compiler_params=params(),
        cost_estimate=cost(20 * rows * 512 * d, 14 * win * d, rows * 512 * 16),
        name="attn_bwd",
    )(tab, q, k, v, ll, lse, lr, gl, go, gr)


def norm_stats(z):
    cen = z - jnp.mean(z, axis=-1, keepdims=True)
    r = lax.rsqrt(jnp.mean(cen * cen, axis=-1, keepdims=True) + EPS)
    return cen * r, r


def norm_back(e, n, r):
    return r * (e - jnp.mean(e, axis=-1, keepdims=True) - n * jnp.mean(e * n, axis=-1, keepdims=True))


RC = 256
TF = 512
TC = 256


def chunks(rows, fn):
    def step(i, c):
        fn(pl.ds(pl.multiple_of(i * RC, RC), RC))
        return c

    lax.fori_loop(0, rows // RC, step, 0)


def clip(t, first, count):
    return jnp.clip(t - first, 0, count - 1)


def lanes(t, size):
    return pl.ds(pl.multiple_of(t * size, size), size)


def colsum(v):
    return jnp.sum(v, axis=0, keepdims=True)


def gelu_parts(u):
    phi = 0.5 * (1.0 + lax.erf(u * (0.5 ** 0.5)))
    return u * phi, phi + u * (0.3989422804014327 * jnp.exp(-0.5 * u * u))


def single(shape):
    return pl.BlockSpec(shape, lambda *_: (0,) * len(shape), pipeline_mode=pl.Buffered(1))


def grid_of(n):
    chips = n // 2
    return {16: (4, 2, 2), 64: (4, 4, 4)}.get(chips, (chips, 1, 1))


class Place:
    def __init__(self, n):
        self.n = n
        self.size = grid_of(n)
        me = lax.axis_index("dp")
        nz, ny, nx = self.size
        self.me = me
        self.c = lax.rem(me, 2)
        self.x = lax.rem(me // 2, nx)
        self.y = lax.rem(me // (2 * nx), ny)
        self.z = me // (2 * nx * ny)

    def at(self, axis, k):
        nz, ny, nx = self.size
        z, y, x, c = self.z, self.y, self.x, self.c
        if axis == "z":
            z = lax.rem(z + k, nz)
        elif axis == "y":
            y = lax.rem(y + k, ny)
        elif axis == "x":
            x = lax.rem(x + k, nx)
        else:
            c = lax.rem(c + k, 2)
        pos = {"z": z, "y": y, "x": x, "c": c}[axis]
        return ((z * ny + y) * nx + x) * 2 + c, pos

    def steps(self, axis):
        nz, ny, nx = self.size
        return range(1, {"z": nz, "y": ny, "x": nx, "c": 2}[axis])

    def peers(self):
        return [self.at(a, k)[0] for a in "zyxc" for k in self.steps(a)]


def enter(peers):
    sem = pltpu.get_barrier_semaphore()
    for p in peers:
        pl.semaphore_signal(sem, inc=1, device_id=(p,), device_id_type=MESH)
    pl.semaphore_wait(sem, len(peers))


def gather_slots(n):
    nz, ny, nx = grid_of(n)
    return (nz - 1) + 2 * (ny - 1) + 2 * (nx - 1) + 1


class Gather:
    def __init__(self, place, src, dst, rows, cols, ssem, rsem, lsem, index, to=None):
        self.p, self.index = place, index
        self.src, self.dst, self.rows, self.cols = src, dst, rows, cols
        self.ssem, self.rsem, self.lsem = ssem, rsem, lsem
        p = place
        r0, nr = rows
        c0, nc = cols
        rs = pl.ds(r0, nr)
        to = c0 if to is None else to
        mine_cols = pl.ds(c0, nc)
        full = pl.ds(to, nc)
        halves = (pl.ds(to, nc // 2), pl.ds(to + nc // 2, nc // 2))
        self.local = pltpu.make_async_copy(src.at[rs, mine_cols], dst.at[p.z, p.y, p.x, p.c, rs, full], lsem.at[index])
        slot = 0

        def copy(s, d, dev):
            nonlocal slot
            cp = pltpu.make_async_remote_copy(src_ref=s, dst_ref=d, send_sem=ssem.at[index, slot], recv_sem=rsem.at[index, slot],
                                              device_id=(dev,), device_id_type=MESH)
            slot += 1
            return cp

        mine = dst.at[p.z, p.y, p.x, p.c, rs, full]
        self.ph = [[], [], [], []]
        for k in p.steps("z"):
            self.ph[0].append(copy(src.at[rs, mine_cols], mine, p.at("z", k)[0]))
        for h, axis in ((0, "y"), (1, "x")):
            s = dst.at[:, p.y, p.x, p.c, rs, halves[h]]
            for k in p.steps(axis):
                self.ph[1].append(copy(s, s, p.at(axis, k)[0]))
        for h, axis in ((0, "x"), (1, "y")):
            s = dst.at[:, :, p.x, p.c, rs, halves[0]] if h == 0 else dst.at[:, p.y, :, p.c, rs, halves[1]]
            for k in p.steps(axis):
                self.ph[2].append(copy(s, s, p.at(axis, k)[0]))
        s = dst.at[:, :, :, p.c, rs, full]
        self.ph[3].append(copy(s, s, p.at("c", 1)[0]))

    def start(self, i):
        if i == 0:
            self.local.start()
        for cp in self.ph[i]:
            cp.start()

    def wait(self, i):
        if i == 0:
            self.local.wait()
        for cp in self.ph[i]:
            cp.wait_recv()

    def sent(self):
        for ph in self.ph:
            for cp in ph:
                cp.wait_send()


def gather_go(g, ph):
    if ph > 0:
        g.wait(ph - 1)
    if ph < 4:
        g.start(ph)


def reduce_slots(n):
    nz, ny, nx = grid_of(n)
    return (nz - 1) + 2 * (ny - 1) + 2 * (nx - 1) + 1


def reduce_buffers(n, r, cols, dtype):
    nz, ny, nx = grid_of(n)
    h = cols // 2
    return [pltpu.VMEM((nz, ny, nx, r, cols), dtype),
            pltpu.VMEM((max(nx - 1, 1), nz, ny, r, h), dtype), pltpu.VMEM((max(ny - 1, 1), nz, nx, r, h), dtype),
            pltpu.VMEM((max(ny - 1, 1), nz, r, h), dtype), pltpu.VMEM((max(nx - 1, 1), nz, r, h), dtype),
            pltpu.VMEM((max(nz - 1, 1), r, cols), dtype), pltpu.VMEM((nz, r, cols), dtype), pltpu.VMEM((r, cols), F32)]


class Reduce:
    def __init__(self, place, src, own, bufs, out, ssem, rsem, lsem, index):
        self.p, self.src, self.own, self.bufs = place, src, own, bufs
        p = place
        self.h = bufs[1].shape[-1]
        self.ca, self.cb = pl.ds(0, self.h), pl.ds(self.h, self.h)
        if own is not None:
            self.get = pltpu.make_async_copy(src.at[:, :, :, p.c], own, lsem.at[index, 0])
        self.put = pltpu.make_async_copy(bufs[7], out, lsem.at[index, 1])
        slot = 0

        def copy(s, d, dev):
            nonlocal slot
            cp = pltpu.make_async_remote_copy(src_ref=s, dst_ref=d, send_sem=ssem.at[index, slot], recv_sem=rsem.at[index, slot],
                                              device_id=(dev,), device_id_type=MESH)
            slot += 1
            return cp

        self.ph = [[], [], [], []]
        dev, oc = p.at("c", 1)
        self.ph[0].append(copy(src.at[:, :, :, oc], bufs[0], dev))
        for k in p.steps("x"):
            dev, o = p.at("x", k)
            self.ph[1].append(copy(bufs[0].at[:, :, o, :, self.ca], bufs[1].at[k - 1], dev))
        for k in p.steps("y"):
            dev, o = p.at("y", k)
            self.ph[1].append(copy(bufs[0].at[:, o, :, :, self.cb], bufs[2].at[k - 1], dev))
        for k in p.steps("y"):
            dev, o = p.at("y", k)
            self.ph[2].append(copy(bufs[1].at[0, :, o], bufs[3].at[k - 1], dev))
        for k in p.steps("x"):
            dev, o = p.at("x", k)
            self.ph[2].append(copy(bufs[2].at[0, :, o], bufs[4].at[k - 1], dev))
        for k in p.steps("z"):
            dev, o = p.at("z", k)
            self.ph[3].append(copy(bufs[6].at[o], bufs[5].at[k - 1], dev))

    def go(self, i):
        if i == 0:
            self.ph[0][0].start()
            if self.own is not None:
                self.get.start()
            return
        p, bufs = self.p, self.bufs
        nz, ny, nx = p.size
        dt = bufs[0].dtype
        if i == 5:
            for cp in self.ph[1]:
                cp.start()
            return
        for cp in self.ph[i - 1]:
            cp.wait_recv()
        if i == 1:
            self.ph[0][0].wait_send()
            if self.own is not None:
                self.get.wait()

            def add(z, c):
                mine = self.own[z] if self.own is not None else self.src[z, :, :, pl.ds(p.c, 1)][:, :, 0]
                bufs[0][z] = (mine.astype(F32) + bufs[0][z].astype(F32)).astype(dt)
                return c

            lax.fori_loop(0, nz, add, 0)
            return
        elif i == 2:
            def add(z, c):
                a = bufs[0][z, :, pl.ds(p.x, 1), :, self.ca].astype(F32)[:, 0]
                for k in range(nx - 1):
                    a += bufs[1][k, z].astype(F32)
                bufs[1][0, z] = a.astype(dt)
                b = bufs[0][z, pl.ds(p.y, 1), :, :, self.cb].astype(F32)[0]
                for k in range(ny - 1):
                    b += bufs[2][k, z].astype(F32)
                bufs[2][0, z] = b.astype(dt)
                return c

            lax.fori_loop(0, nz, add, 0)
        elif i == 3:
            a = bufs[1][0, :, pl.ds(p.y, 1)].astype(F32)[:, 0]
            for k in range(ny - 1):
                a += bufs[3][k].astype(F32)
            bufs[6][:, :, self.ca] = a.astype(dt)
            b = bufs[2][0, :, pl.ds(p.x, 1)].astype(F32)[:, 0]
            for k in range(nx - 1):
                b += bufs[4][k].astype(F32)
            bufs[6][:, :, self.cb] = b.astype(dt)
        else:
            a = bufs[6][pl.ds(p.z, 1)].astype(F32)[0]
            for k in range(nz - 1):
                a += bufs[5][k].astype(F32)
            bufs[7][...] = a
            self.put.start()
            return
        for cp in self.ph[i]:
            cp.start()

    def finish(self):
        self.put.wait()
        for ph in self.ph[1:]:
            for cp in ph:
                cp.wait_send()


def run_at(t, events):
    for step in sorted({e[0] for e in events}):
        @pl.when(t == step)
        def _():
            for e in events:
                if e[0] == step:
                    e[1](*e[2:])


FIRST_PLAN = (
    (0, 0, 0), (0, 1, 0), (0, 0, 1), (0, 1, 1), (0, 4, 0), (0, 0, 2), (0, 2, 0), (0, 1, 2),
    (0, 4, 1), (0, 0, 3), (0, 1, 3), (0, 3, 0), (0, 2, 1), (0, 4, 2), (0, 1, 4), (0, 0, 4),
    (2, 3, 1), (2, 2, 2), (2, 6, 0), (3, 6, 1), (3, 4, 3), (3, 5, 0), (3, 3, 2), (4, 2, 3),
    (4, 5, 1), (4, 6, 2), (4, 2, 4), (5, 4, 4), (6, 5, 2), (7, 3, 3), (8, 6, 3), (8, 3, 4),
    (10, 5, 3), (12, 6, 4), (12, 5, 4),
)
UPS_FIRST = 2
ZERO_ROW, OB, DB, FG, FS, SG, SS, UB = 1, 3, 4, 5, 6, 7, 8, 9


def first_kernel(n, nc, ps, qs, ks, vs, os, us, xs, wq, wk, wv, wo, wu, vec, q, k, v,
                 x, pk, w3, y3, ssem, rsem, lsem, hs, hr, xsem, osem):
    t = pl.program_id(0)
    p = Place(n)
    rows, d = xs.shape
    r = qs.shape[0]
    right, left = lax.rem(p.me + 1, n), lax.rem(p.me + n - 1, n)
    edges = [pltpu.make_async_remote_copy(src_ref=xs.at[pl.ds(rows - HALO, HALO), :], dst_ref=x.at[pl.ds(0, HALO), :], send_sem=hs.at[0],
                                          recv_sem=hr.at[0], device_id=(right,), device_id_type=MESH),
             pltpu.make_async_remote_copy(src_ref=xs.at[pl.ds(0, HALO), :], dst_ref=x.at[pl.ds(HALO + rows, HALO), :], send_sem=hs.at[1],
                                          recv_sem=hr.at[1], device_id=(left,), device_id_type=MESH)]
    mine = pltpu.make_async_copy(xs, x.at[pl.ds(HALO, rows), :], xsem)
    plan = [(ps, pk, 0), (qs, w3.at[0], 0), (ks, w3.at[1], 0), (vs, w3.at[2], 0), (os, wo, 0)] + [(us, wu, j * d) for j in range(UPS_FIRST)]
    g = [Gather(p, a, b, (0, a.shape[0]), (c, d), ssem, rsem, lsem, i) for i, (a, b, c) in enumerate(plan)]
    weights = [pltpu.make_async_copy(w3.at[i], o, osem.at[i]) for i, o in enumerate((wq, wk, wv))]
    results = [pltpu.make_async_copy(y3.at[i], o, osem.at[3 + i]) for i, o in enumerate((q, k, v))]

    def vectors():
        vec[...] = jnp.sum(pk[...].astype(F32).reshape(n, pk.shape[-2], d), axis=0)

    @pl.when(t == 0)
    def _():
        enter(p.peers() + [left, right])

    @pl.when((t > 0) & (t <= 3 * nc))
    def _():
        i = (t - 1) // nc
        c = lanes(lax.rem(t - 1, nc), TC)
        y = dot(x[...], w3[pl.ds(i, 1), ..., c].reshape(d, TC)) + vec[pl.ds(i, 1), c]
        y3[pl.ds(i, 1), :, c] = y.astype(BF16)[None]

    events = []
    for step, i, ph in FIRST_PLAN:
        events.append((step, gather_go, g[i], ph))
        if i == 0 and ph == 0:
            events += [(0, mine.start)] + [(0, c.start) for c in edges]
        if ph == 4 and i == 0:
            events.append((step, vectors))
        if ph == 4 and 1 <= i <= 3:
            events.append((step, weights[i - 1].start))
    events += [(0, mine.wait)] + [(0, c.wait_recv) for c in edges]
    events += [((i + 1) * nc, c.start) for i, c in enumerate(results)]
    last = 3 * nc
    events += [(last, c.sent) for c in g] + [(last, c.wait_send) for c in edges] + [(last, c.wait) for c in weights + results]
    run_at(t, events)


def first_call(n, packed, wq, wk, wv, wo, wu, x):
    rows, d = x.shape
    win = rows + 2 * HALO
    nc = d // TC
    r = wq.shape[0]
    z = grid_of(n) + (2,)
    count = 5 + UPS_FIRST
    k = gather_slots(n)
    mat = jax.ShapeDtypeStruct(z + (r, d), BF16)
    out = jax.ShapeDtypeStruct((win, d), BF16)
    res = pl.pallas_call(
        functools.partial(first_kernel, n, nc),
        grid=(3 * nc + 1,),
        in_specs=[ANY] * 7,
        out_specs=[ANY] * 5 + [single(packed.shape)] + [ANY] * 3,
        out_shape=[mat] * 4 + [jax.ShapeDtypeStruct(z + (r, UPS_FIRST * d), BF16), jax.ShapeDtypeStruct(packed.shape, F32)] + [out] * 3,
        scratch_shapes=[pltpu.VMEM((win, d), BF16), pltpu.VMEM(z + packed.shape, BF16), pltpu.VMEM((3,) + z + (r, d), BF16),
                        pltpu.VMEM((3, win, d), BF16), pltpu.SemaphoreType.DMA((count, k)), pltpu.SemaphoreType.DMA((count, k)),
                        pltpu.SemaphoreType.DMA((count,)), pltpu.SemaphoreType.DMA((2,)), pltpu.SemaphoreType.DMA((2,)),
                        pltpu.SemaphoreType.DMA, pltpu.SemaphoreType.DMA((6,))],
        compiler_params=pltpu.CompilerParams(collective_id=1, has_side_effects=True, vmem_limit_bytes=56 << 20),
        cost_estimate=cost(6 * win * d * d, 2 * (4 * win * d + 3 * d * d)),
        name="first",
    )(packed, wq, wk, wv, wo, wu, x)
    ws = [w.reshape((-1, w.shape[-1])) for w in res[:5]]
    return ws + list(res[5:])


DOWN_PLAN = (
    (0, 2, 0), (3, 2, 1), (3, 0, 0), (4, 2, 2), (4, 5, 0), (5, 3, 0), (7, 0, 1), (10, 0, 2),
    (12, 1, 0), (12, 5, 1), (15, 3, 1), (16, 4, 0), (17, 1, 1), (17, 2, 3), (17, 0, 3), (18, 3, 2),
    (19, 1, 2), (20, 0, 4), (20, 4, 1), (21, 5, 2), (21, 3, 3), (23, 4, 2), (24, 3, 4), (24, 1, 3),
    (25, 5, 3), (25, 1, 4), (26, 2, 4), (26, 4, 3), (26, 5, 4), (27, 4, 4),
)


AG = 256
MASKED = -1e30


def window(ref, b, c, late):
    x = ref[pl.ds(pl.multiple_of(b * GRAN, GRAN), 4 * GRAN), c]
    for i, at in enumerate(late):
        y = ref[pl.ds(pl.multiple_of((b + i + 1) * GRAN, GRAN), 4 * GRAN), c]
        x = jnp.where(at, y, x)
    return x


def attend(t, tab, q_ref, k_ref, v_ref, ctx, lse):
    subs = ctx.shape[0] // GRAN // 2
    group, sub = t // subs, lax.rem(t, subs)
    units = []
    for j in range(2):
        b = sub * 2 + j
        late = [tab[0, b] == b + i for i in range(1, 4)]
        own = pl.ds(pl.multiple_of(HALO + b * GRAN, GRAN), GRAN)
        inside = lax.broadcasted_iota(jnp.int32, (4 * GRAN, 2 * GRAN), 0) < tab[2, b] * GRAN
        for i in range(AG // (2 * HD)):
            c = slice(i * 2 * HD, (i + 1) * 2 * HD)
            q = eighth(q_ref[own, c])
            zero = jnp.zeros_like(q)
            both = jnp.concatenate([jnp.where(m, q, zero) for m in masks(q.shape)], axis=0)
            k, v = window(k_ref, b, c, late), window(v_ref, b, c, late)
            units.append((b, i, jnp.where(inside, dot_nt(k, both), MASKED), v))
    top = [jnp.max(u[2], axis=0, keepdims=True) for u in units]
    e = [jnp.exp(u[2] - m) for u, m in zip(units, top)]
    total = [jnp.sum(x, axis=0, keepdims=True) for x in e]
    logs = []
    for (b, i, _, v), m, x, s in zip(units, top, e, total):
        y = dot(v.T, x.astype(BF16)) * (1.0 / s)
        logs.append((b, 2 * i, m + jnp.log(s)))
        y = jnp.concatenate([y[:HD, :GRAN], y[HD:, GRAN:]], axis=0)
        rows = pl.ds(pl.multiple_of(b * GRAN, GRAN), GRAN)
        ctx[rows, pl.ds(pl.multiple_of(group * AG + i * 2 * HD, 2 * HD), 2 * HD)] = y.T.astype(BF16)
    for k in range(ctx.shape[1] // AG):
        @pl.when(group == k)
        def _():
            for b, h, log in logs:
                for i in range(2):
                    head = k * (AG // HD) + h + i
                    lse[head:head + 1, pl.ds(pl.multiple_of(b * GRAN, GRAN), GRAN)] = log[:, i * GRAN:(i + 1) * GRAN]


def fwd_kernel(n, na, nu, nc, tab, q_ref, k_ref, v_ref, wo, x, wu, wus, wds, g, vec,
               lse, xhat, lowt, ctxt, r1, hidt, dg, out, gs, gd, sums, wd, wu2, ctx, z, hid, low, wt, w3,
               ssem, rsem, lsem, wsem, usem):
    t = pl.program_id(0) - na
    rows, d = x.shape
    p = Place(n)
    ups = w3.shape[0]
    blocks = len(set(e[1] for e in DOWN_PLAN)) - ups
    r = wds.shape[0] // blocks
    ga = [Gather(p, wus, w3.at[i], (0, r), ((UPS_FIRST + i) * d, d), ssem, rsem, lsem, i, 0) for i in range(ups)]
    ga += [Gather(p, wds, wd, (i * r, r), (0, d), ssem, rsem, lsem, ups + i) for i in range(blocks)]
    keep = [pltpu.make_async_copy(w3.at[i], wu2.at[i], usem.at[i]) for i in range(ups)]
    fetch = [pltpu.make_async_copy(wd.at[:, :, :, :, :, pl.ds(j * TC, TC)], wt.at[j % 2], wsem.at[j]) for j in range(nc)]
    first = nc + nu

    @pl.when(t == -na)
    def _():
        enter(p.peers())

    @pl.when(t < 0)
    def _():
        attend(t + na, tab, q_ref, k_ref, v_ref, ctx, lse)

    run_at(t, [(first + j, fetch[j].wait) for j in range(nc)] + [(first + j, fetch[j + 1].start) for j in range(nc - 1)])

    @pl.when((t >= 0) & (t < nc))
    def _():
        c = lanes(t, TC)
        z[:, c] = dot(ctx[...], wo[...]) + x[:, c].astype(F32)

    @pl.when(t == nc - 1)
    def _():
        def fin(r):
            n, rr = norm_stats(z[r, :] + vec[OB:OB + 1, :])
            xhat[r, :] = n
            r1[r, :] = jnp.broadcast_to(rr, (RC, r1.shape[1]))
            v = (n * vec[FG:FG + 1, :] + vec[FS:FS + 1, :]).astype(BF16)
            low[r, :] = v
            lowt[:, r] = v.T
            ctxt[:, r] = ctx[r, :].T

        chunks(rows, fin)

    def up(weight):
        for j in range(TF // TC):
            c = slice(j * TC, (j + 1) * TC)
            tile = (t - nc) * (TF // TC) + j
            bias = vec[pl.ds(UB + tile // (d // TC), 1), lanes(lax.rem(tile, d // TC), TC)]
            h, s = gelu_parts(dot(low[...], weight(j, tile)) + bias)
            h = h.astype(BF16)
            dg[:, c] = s.astype(BF16)
            hid[:, lanes(tile, TC)] = h
            hidt[c, :] = h.T

    split = nc + UPS_FIRST * (d // TF)

    @pl.when((t >= nc) & (t < split))
    def _():
        up(lambda j, tile: wu[:, j * TC:(j + 1) * TC])

    if ups:
        @pl.when((t >= split) & (t < nc + nu))
        def _():
            up(lambda j, tile: w3[pl.ds(tile // (d // TC) - UPS_FIRST, 1), ..., lanes(lax.rem(tile, d // TC), TC)].reshape(d, TC))

    @pl.when(t >= nc + nu)
    def _():
        c = lanes(t - nc - nu, TC)
        z[:, c] = dot(hid[...], wt[pl.ds(lax.rem(t - first, 2), 1)].reshape(hid.shape[1], TC))

    @pl.when(t == 2 * nc + nu - 1)
    def _():
        sums[...] = jnp.zeros_like(sums)

        def fin(r):
            v = (xhat[r, :] * vec[FG:FG + 1, :] + vec[FS:FS + 1, :]) + (z[r, :] + vec[DB:DB + 1, :])
            n, rr = norm_stats(v)
            out[r, :] = (n * vec[SG:SG + 1, :] + vec[SS:SS + 1, :]).astype(BF16)
            gv = g[r, :].astype(F32)
            sums[0:1, :] += colsum(gv * n)
            sums[1:2, :] += colsum(gv)
            grad = norm_back(gv * vec[SG:SG + 1, :], n, rr)
            gs[r, :] = grad
            low_g = grad.astype(BF16)
            gd[r, :] = low_g
            sums[2:3, :] += colsum(low_g.astype(F32))

        chunks(rows, fin)

    done = {e[1]: e[0] for e in DOWN_PLAN if e[2] == 4}
    run_at(t + na, [(e[0], gather_go, ga[e[1]], e[2]) for e in DOWN_PLAN] + [(done[i], c.start) for i, c in enumerate(keep)]
           + [(na + first - 1, c.sent) for c in ga] + [(na + first - 1, c.wait) for c in keep] + [(na + first - 1, fetch[0].start)])


def fwd_call(n, tab, q, k, v, wo, x, wu, wus, wd, g, vec):
    rows, d = x.shape
    win = q.shape[0]
    ff = wus.shape[1]
    nu, nc = ff // TF, d // TC
    z = grid_of(n) + (2,)
    blocks = ff // d
    ups = blocks - UPS_FIRST
    slots = gather_slots(n)
    count = blocks + ups
    subs = rows // GRAN // 2
    na = d // AG * subs
    split = UPS_FIRST * (d // TF)
    spec = pl.BlockSpec((win, AG), lambda t: (0, clip(t, 0, na) // subs))

    def tile(t):
        return clip(t, na + nc, nu)

    *res, down, up2 = pl.pallas_call(
        functools.partial(fwd_kernel, n, na, nu, nc),
        grid=(na + 2 * nc + nu,),
        in_specs=[pl.BlockSpec(memory_space=pltpu.SMEM), spec, spec, spec, pl.BlockSpec((d, TC), lambda t: (0, clip(t, na, nc))),
                  single(x.shape), pl.BlockSpec((d, TF), lambda t: (0, clip(t, na + nc, split))), ANY, ANY, single(g.shape), single(vec.shape)],
        out_specs=[single((d // HD, rows)), single((rows, d)), single((d, rows)), single((d, rows)), single((rows, 128)),
                   pl.BlockSpec((TF, rows), lambda t: (tile(t), 0)), pl.BlockSpec((rows, TF), lambda t: (0, tile(t))),
                   single((rows, d)), single((rows, d)), single((rows, d)), single((8, d)), ANY, ANY],
        out_shape=[jax.ShapeDtypeStruct((d // HD, rows), F32), jax.ShapeDtypeStruct((rows, d), F32), jax.ShapeDtypeStruct((d, rows), BF16),
                   jax.ShapeDtypeStruct((d, rows), BF16), jax.ShapeDtypeStruct((rows, 128), F32), jax.ShapeDtypeStruct((ff, rows), BF16),
                   jax.ShapeDtypeStruct((rows, ff), BF16), jax.ShapeDtypeStruct((rows, d), BF16),
                   jax.ShapeDtypeStruct((rows, d), F32), jax.ShapeDtypeStruct((rows, d), BF16), jax.ShapeDtypeStruct((8, d), F32),
                   jax.ShapeDtypeStruct(z + wd.shape, BF16), jax.ShapeDtypeStruct((ups,) + z + (wus.shape[0], d), BF16)],
        scratch_shapes=[pltpu.VMEM((rows, d), BF16), pltpu.VMEM((rows, d), F32), pltpu.VMEM((rows, ff), BF16), pltpu.VMEM((rows, d), BF16),
                        pltpu.VMEM((2,) + z + (wd.shape[0], TC), BF16), pltpu.VMEM((ups,) + z + (wus.shape[0], d), BF16),
                        pltpu.SemaphoreType.DMA((count, slots)), pltpu.SemaphoreType.DMA((count, slots)),
                        pltpu.SemaphoreType.DMA((count,)), pltpu.SemaphoreType.DMA((nc,)), pltpu.SemaphoreType.DMA((ups,))],
        compiler_params=pltpu.CompilerParams(collective_id=2, has_side_effects=True, vmem_limit_bytes=62 << 20),
        cost_estimate=cost(4 * rows * d * ff, 4 * d * ff + 4 * rows * ff + rows * d * 14, 2 * rows * ff),
        name="fwd",
    )(tab, q, k, v, wo, x, wu, wus, wd, g, vec)
    return res + [down.reshape(ff, d), up2.reshape(ups, d, d)]


BWD_PLAN = (
    (1, 1, 0, 0), (1, 1, 1, 0), (2, 0, 0, 1), (2, 0, 0, 5), (2, 0, 1, 1), (3, 1, 3, 0),
    (3, 1, 1, 5), (3, 1, 0, 2), (3, 1, 2, 0), (4, 0, 3, 1), (4, 0, 3, 5), (4, 0, 2, 1),
    (5, 1, 5, 0), (5, 1, 1, 2), (5, 1, 4, 0), (6, 0, 0, 3), (6, 0, 2, 5), (6, 0, 5, 1),
    (6, 0, 4, 1), (6, 0, 4, 5), (7, 0, 3, 2), (7, 0, 1, 3), (8, 1, 5, 5), (9, 1, 2, 2),
    (10, 1, 3, 3), (12, 1, 2, 3), (12, 1, 5, 2), (14, 1, 4, 2), (15, 1, 5, 3), (20, 1, 4, 3),
    (21, 1, 1, 4), (22, 1, 2, 4), (23, 1, 3, 4), (23, 1, 5, 4), (23, 1, 0, 4), (23, 1, 4, 4),
)
EARLY = 6


def bwd_kernel(n, nu, nc, nr, gd, lowt, hidt, dg, wd, wu, wu2, gs, xhat, r1, vec, wo, ctxt, lse,
               gsf, sums, sumu, gc, dwo, rd, ru, gl, gr, ll, lr, *rest):
    t = pl.program_id(0)
    d, rows = lowt.shape
    per = d // TF
    count = 2 * (nu // per)
    late = rest[:count - EARLY]
    gu, bufd, bufu, ga = rest[count - EARLY:count - EARLY + 4]
    rest = rest[count - EARLY + 4:]
    ssem, rsem, lsem, wsem, hs, hr = rest[-6:]
    p = Place(n)
    r = d // n
    red = []
    for i in range(EARLY):
        j = i // 2
        out = rd.at[pl.ds(j * r, r), :] if i % 2 == 0 else ru.at[:, pl.ds(j * d, d)]
        red.append(Reduce(p, (bufd, bufu)[i % 2], None, rest[8 * i:8 * i + 8], out, ssem, rsem, lsem, i))
    right, left = lax.rem(p.me + 1, n), lax.rem(p.me + n - 1, n)
    edges = [pltpu.make_async_remote_copy(src_ref=gc.at[pl.ds(rows - HALO, HALO), :], dst_ref=gl, send_sem=hs.at[0], recv_sem=hr.at[0],
                                          device_id=(right,), device_id_type=MESH),
             pltpu.make_async_remote_copy(src_ref=gc.at[pl.ds(0, HALO), :], dst_ref=gr, send_sem=hs.at[1], recv_sem=hr.at[1],
                                          device_id=(left,), device_id_type=MESH),
             pltpu.make_async_remote_copy(src_ref=lse.at[:, pl.ds(rows - HALO, HALO)], dst_ref=ll, send_sem=hs.at[2], recv_sem=hr.at[2],
                                          device_id=(right,), device_id_type=MESH),
             pltpu.make_async_remote_copy(src_ref=lse.at[:, pl.ds(0, HALO)], dst_ref=lr, send_sem=hs.at[3], recv_sem=hr.at[3],
                                          device_id=(left,), device_id_type=MESH)]
    last = nu + 3 * nc + nr - 1
    mid = [(e[0], red[e[2]].go, e[3]) for e in BWD_PLAN if e[1] == 0]
    end = [(e[0], red[e[2]].go, e[3]) for e in BWD_PLAN if e[1] == 1]
    for i in range(EARLY, count):
        c = pltpu.make_async_copy((bufd, bufu)[i % 2], late[i - EARLY], wsem.at[i - EARLY])
        end.append((per * (i // 2 + 1) - 1, c.start))
        if per * (i // 2 + 1) < nu:
            mid.append((per * (i // 2 + 1), c.wait))
        else:
            end.append((last, c.wait))
    end += [(nu + 2 * nc + nr - 1, c.start) for c in edges] + [(last, c.wait) for c in edges]
    end += [(last, c.finish) for c in red]

    @pl.when(t == 0)
    def _():
        enter(p.peers() + [left, right])

    @pl.when(t < nu)
    def _():
        for j in range(TF // TC):
            c = slice(j * TC, (j + 1) * TC)
            g = (dot_nt(gd[...], wd[c, :]) * dg[:, c].astype(F32)).astype(BF16)
            gu[:, lanes(t * (TF // TC) + j, TC)] = g
            sumu[:, c] = colsum(g.astype(F32))

    run_at(t, mid)

    @pl.when(t < nu)
    def _():
        half = lax.rem(t, per)
        for j in range(TF // TC):
            c = lanes(half * (TF // TC) + j, TC)
            bufu[..., c] = dot(lowt[...], gu[:, lanes(t * (TF // TC) + j, TC)]).astype(BF16).reshape(bufu.shape[:-1] + (TC,))
            bufd[..., c] = dot(hidt[...].reshape(d, rows), gd[:, c]).astype(BF16).reshape(bufd.shape[:-1] + (TC,))

    @pl.when((t >= nu) & (t < nu + nc))
    def _():
        v = gs[...] + dot_nt(gu[:, :wu.shape[1]], wu[...])
        for i in range(wu2.shape[0]):
            v += dot_nt(gu[:, wu.shape[1] + i * d:wu.shape[1] + (i + 1) * d], wu2[i])
        gsf[:, lanes(t - nu, TC)] = v

    @pl.when(t == nu + nc)
    def _():
        sums[...] = jnp.zeros_like(sums)

    @pl.when((t >= nu + nc) & (t < nu + nc + nr))
    def _():
        at = lanes(t - nu - nc, RC)
        gf = gsf[at, :]
        nn = xhat[...]
        sums[0:1, :] += colsum(gf * nn)
        sums[1:2, :] += colsum(gf)
        grad = norm_back(gf * vec[FG:FG + 1, :], nn, r1[:, 0:1])
        gsf[at, :] = grad
        low_g = grad.astype(BF16)
        ga[at, :] = low_g
        sums[2:3, :] += colsum(low_g.astype(F32))

    first = nu + nc + nr

    @pl.when((t >= first) & (t < first + nc))
    def _():
        gc[:, lanes(t - first, TC)] = dot_nt(ga[...], wo[...]).astype(BF16)

    @pl.when(t >= first + nc)
    def _():
        dwo[...] = dot(ctxt[...], ga[:, lanes(t - first - nc, TC)]).astype(BF16)

    run_at(t, end)


def bwd_call(n, gd, lowt, hidt, dg, wd, wu, wu2, gs, xhat, r1, vec, wo, ctxt, lse):
    d, rows = lowt.shape
    ff = wd.shape[0]
    nu, nc, nr = ff // TF, d // TC, rows // RC
    r = d // n
    parts = ff // d
    z = grid_of(n) + (2, r)
    per = d // TF
    chunk = jax.ShapeDtypeStruct(z + (d,), BF16)
    k = reduce_slots(n)
    late = 2 * parts - EARLY
    scratch = [pltpu.VMEM((rows, ff), BF16), pltpu.VMEM(z + (d,), BF16), pltpu.VMEM(z + (d,), BF16), pltpu.VMEM((rows, d), BF16)]
    for i in range(EARLY):
        scratch += reduce_buffers(n, r, d, BF16)
    scratch += [pltpu.SemaphoreType.DMA((EARLY, k)), pltpu.SemaphoreType.DMA((EARLY, k)), pltpu.SemaphoreType.DMA((EARLY, 2)),
                pltpu.SemaphoreType.DMA((late,)), pltpu.SemaphoreType.DMA((4,)), pltpu.SemaphoreType.DMA((4,))]
    edge = jax.ShapeDtypeStruct((HALO, d), BF16)
    edge_l = jax.ShapeDtypeStruct((lse.shape[0], HALO), F32)
    first = nu + nc + nr
    return pl.pallas_call(
        functools.partial(bwd_kernel, n, nu, nc, nr),
        grid=(nu + 3 * nc + nr,),
        in_specs=[single(gd.shape), single(lowt.shape),
                  pl.BlockSpec((n, 1, r, rows), lambda t: (0, clip(t, 0, nu) // per, 0, 0)),
                  pl.BlockSpec((rows, TF), lambda t: (0, clip(t, 0, nu))), pl.BlockSpec((TF, d), lambda t: (clip(t, 0, nu), 0)),
                  pl.BlockSpec((TC, wu.shape[1]), lambda t: (clip(t, nu, nc), 0)),
                  pl.BlockSpec((wu2.shape[0], TC, d), lambda t: (0, clip(t, nu, nc), 0)), pl.BlockSpec((rows, TC), lambda t: (0, clip(t, nu, nc))),
                  pl.BlockSpec((RC, d), lambda t: (clip(t, nu + nc, nr), 0)), pl.BlockSpec((RC, 128), lambda t: (clip(t, nu + nc, nr), 0)),
                  single(vec.shape), pl.BlockSpec((TC, d), lambda t: (clip(t, first, nc), 0)), single(ctxt.shape), single(lse.shape)],
        out_specs=[single((rows, d)), single((8, d)), pl.BlockSpec((1, TF), lambda t: (0, clip(t, 0, nu))), single((rows, d)),
                   pl.BlockSpec((d, TC), lambda t: (0, clip(t, first + nc, nc)))] + [ANY] * (6 + late),
        out_shape=[jax.ShapeDtypeStruct((rows, d), F32), jax.ShapeDtypeStruct((8, d), F32), jax.ShapeDtypeStruct((1, ff), F32),
                   jax.ShapeDtypeStruct((rows, d), BF16), jax.ShapeDtypeStruct((d, d), BF16),
                   jax.ShapeDtypeStruct(((EARLY + 1) // 2 * r, d), F32), jax.ShapeDtypeStruct((r, EARLY // 2 * d), F32), edge, edge,
                   edge_l, edge_l] + [chunk] * late,
        scratch_shapes=scratch,
        compiler_params=pltpu.CompilerParams(collective_id=3, has_side_effects=True, vmem_limit_bytes=62 << 20),
        cost_estimate=cost(8 * rows * d * ff, 8 * d * ff + 4 * rows * ff + rows * d * 18),
        name="bwd",
    )(gd, lowt, hidt.reshape(n, parts, r, rows), dg, wd, wu, wu2, gs, xhat, r1, vec, wo, ctxt, lse)


IN_PLAN = (
    (0, 6, 0), (0, 1, 0), (2, 6, 1), (2, 2, 0), (2, 6, 5), (3, 1, 1), (3, 1, 5), (4, 6, 2),
    (4, 3, 0), (5, 3, 1), (5, 3, 5), (5, 1, 2), (5, 0, 0), (6, 2, 1), (7, 4, 0), (7, 2, 5),
    (7, 4, 1), (8, 4, 5), (9, 1, 3), (10, 0, 1), (10, 6, 3), (10, 0, 5), (10, 3, 2), (11, 3, 3),
    (11, 5, 0), (11, 2, 2), (12, 0, 2), (12, 5, 1), (12, 6, 4), (12, 5, 5), (12, 2, 3), (12, 4, 2),
    (13, 0, 3), (13, 4, 3), (13, 5, 2), (13, 5, 3), (13, 1, 4), (14, 2, 4), (15, 0, 4), (15, 4, 4),
    (15, 3, 4), (15, 5, 4),
)


def in_bwd_kernel(n, nc, left, x, gsf, dq, dk, dv, wq, wk, wv, *rest):
    t = pl.program_id(0)
    srcs, rest = rest[:left + 2], rest[left + 2:]
    tg, outs, rest = rest[0], rest[1:left + 6], rest[left + 6:]
    xt, bq, bk, bv, owns, rest = rest[0], rest[1], rest[2], rest[3], rest[4:left + 6], rest[left + 6:]
    ssem, rsem, lsem = rest[-3:]
    p = Place(n)
    plan = list(zip(srcs[:-1], owns[:-1])) + [(b, None) for b in (bq, bk, bv)] + [(srcs[-1], owns[-1])]
    red = [Reduce(p, s, o, rest[8 * i:8 * i + 8], outs[i], ssem, rsem, lsem, i) for i, (s, o) in enumerate(plan)]

    @pl.when(t == 0)
    def _():
        enter(p.peers())
        xt[...] = x[...].T

    for i, (a, b) in enumerate(((dq, bq), (dk, bk), (dv, bv))):
        @pl.when((t >= i * nc) & (t < (i + 1) * nc))
        def _():
            c = lanes(t - i * nc, TC)
            b[..., c] = dot(xt[...], a[:, c]).astype(BF16).reshape(b.shape[:-1] + (TC,))

    @pl.when(t >= 3 * nc)
    def _():
        g = gsf[...] + dot_nt(dq[...], wq[...]) + dot_nt(dk[...], wk[...]) + dot_nt(dv[...], wv[...])
        tg[...] = g.astype(BF16)

    run_at(t, [(e[0], red[e[1]].go, e[2]) for e in IN_PLAN] + [(4 * nc - 1, c.finish) for c in red])


def in_bwd_call(n, x, gsf, dq, dk, dv, wq, wk, wv, late, dwo, small):
    rows, d = x.shape
    nc = d // TC
    r = d // n
    z = grid_of(n)
    col = pl.BlockSpec((rows, TC), lambda t: (0, clip(t, 3 * nc, nc)))
    wrow = pl.BlockSpec((TC, d), lambda t: (clip(t, 3 * nc, nc), 0))
    chunk = pltpu.VMEM(z + (2, r, d), BF16)
    own = pltpu.VMEM(z + (r, d), BF16)
    share = jax.ShapeDtypeStruct((r, d), F32)
    sr, sc = small.shape[0] // n, small.shape[1]
    k = reduce_slots(n)
    left = len(late)
    total = left + 5
    scratch = [pltpu.VMEM((d, rows), BF16)] + [chunk] * 3 + [own] * (left + 1) + [pltpu.VMEM(z + (sr, sc), F32)]
    for i in range(total - 1):
        scratch += reduce_buffers(n, r, d, BF16)
    scratch += reduce_buffers(n, sr, sc, F32)
    scratch += [pltpu.SemaphoreType.DMA((total, k)), pltpu.SemaphoreType.DMA((total, k)), pltpu.SemaphoreType.DMA((total, 2))]
    return pl.pallas_call(
        functools.partial(in_bwd_kernel, n, nc, left),
        grid=(4 * nc,),
        in_specs=[single((rows, d)), col] + [single((rows, d))] * 3 + [wrow] * 3 + [ANY] * (left + 2),
        out_specs=[col] + [ANY] * total,
        out_shape=[jax.ShapeDtypeStruct((rows, d), BF16)] + [share] * (left + 4) + [jax.ShapeDtypeStruct((sr, sc), F32)],
        scratch_shapes=scratch,
        compiler_params=pltpu.CompilerParams(collective_id=5, has_side_effects=True, vmem_limit_bytes=62 << 20),
        cost_estimate=cost(12 * rows * d * d, rows * d * 14 + 12 * d * d),
        name="in_bwd",
    )(x, gsf, dq, dk, dv, wq, wk, wv, *late, dwo.reshape(z + (2, r, d)), small.reshape(z + (2, sr, sc)))


def hand_on_kernel(groups, axes, *refs):
    total = sum(groups)
    at = 0
    for g, axis, out in zip(groups, axes, refs[total:]):
        start = 0
        for a in refs[at:at + g]:
            size = a.shape[axis]
            if axis == 0:
                out[start:start + size, :] = a[...]
            else:
                out[:, start:start + size] = a[...]
            start += size
        at += g


def hand_on(parts, axes):
    shapes = []
    for ps, axis in zip(parts, axes):
        shape = list(ps[0].shape)
        shape[axis] = sum(p.shape[axis] for p in ps)
        shapes.append(jax.ShapeDtypeStruct(tuple(shape), ps[0].dtype))
    return pl.pallas_call(
        functools.partial(hand_on_kernel, tuple(len(p) for p in parts), axes),
        out_shape=shapes,
        name="hand_on",
    )(*[a for p in parts for a in p])


def sequence_table(lengths, own, rows):
    ids = jnp.arange(lengths.shape[0], dtype=jnp.int32)
    starts = jnp.sum(jnp.where(ids[None, :] < ids[:, None], lengths[None, :], 0), axis=1)
    blocks = rows // GRAN
    at = own * rows + jnp.arange(blocks, dtype=jnp.int32) * GRAN
    inside = (starts[None, :] <= at[:, None]) & (at[:, None] < (starts + lengths)[None, :])
    first = jnp.sum(jnp.where(inside, starts[None, :], 0), axis=1)
    length = jnp.sum(jnp.where(inside, lengths[None, :], 0), axis=1)
    lead = (first == at) | (jnp.arange(blocks) == 0)
    return jnp.stack([(first - own * rows + HALO) // GRAN, jnp.where(lead, length // GRAN, 0), length // GRAN]).astype(jnp.int32)


def pack(values, n, rows, dtype):
    cols = [v.reshape(n, -1) for v in values]
    flat = jnp.concatenate(cols, axis=1)
    return jnp.pad(flat, ((0, 0), (0, rows * 256 - flat.shape[1]))).astype(dtype).reshape(n * rows, 256)


def unpack(packed, n, part):
    flat = packed.reshape(n, -1)
    vec = flat[:, : 8 * part].reshape(n, 8, part).transpose(1, 0, 2).reshape(8, n * part)
    return vec, flat[:, 8 * part:12 * part].reshape(1, -1)


def local(tokens, cotangent, lengths, dealing, *shards):
    n = lax.axis_size("dp")
    own = lax.axis_index("dp")
    rows, d = tokens.shape
    part = d // n
    qb, vb, ob, ub, db, fg, fs, sg, ss = shards[6:]
    mine = jnp.stack([qb, jnp.zeros_like(qb), vb, ob, db, fg, fs, sg, ss])
    mine = lax.dynamic_update_slice(jnp.zeros((UB, d), BF16), mine, (0, own * part))
    ups = lax.dynamic_update_slice(jnp.zeros((ub.shape[0] * n,), BF16), ub, (own * ub.shape[0],)).reshape(-1, d)
    packed = jnp.concatenate([mine, ups, jnp.zeros((16 - UB - ups.shape[0], d), BF16)])
    wq, wk, wv, wo, wu, vec, q, k, v = first_call(n, packed, *shards[:5], tokens)
    tab = sequence_table(lengths, own, rows)
    lse, xhat, lowt, ctxt, r1, hidt, dg, layer_out, gs, gd, sums2, wd, wu2 = fwd_call(n, tab, q, k, v, wo, tokens, wu, *shards[4:6], cotangent, vec)
    gsf, sums1, sumu, gc, dwo, rd, ru, gl, gr, ll, lr, *late = bwd_call(n, gd, lowt, hidt, dg, wd, wu, wu2, gs, xhat, r1, vec, wo, ctxt, lse)
    dq, dk, dv, sums0 = attn_bwd_call(tab, q, k, v, ll, lse, lr, gl, gc, gr)
    small = pack([sums0[0], sums0[1], sums1[2], sums2[2], sums1[0], sums1[1], sums2[0], sums2[1], sumu], n, 8, F32)
    tg, *more = in_bwd_call(n, tokens, gsf, dq, dk, dv, wq, wk, wv, late, dwo, small)
    left = len(late)
    go, gq, gk, gv, tiny = more[left:]
    downs = [rd] + [more[i] for i in range(left) if (EARLY + i) % 2 == 0]
    ups = [ru] + [more[i] for i in range(left) if (EARLY + i) % 2 == 1]
    gq, gk, gv, go, gu, gd, tg, layer_out = hand_on([[gq], [gk], [gv], [go], ups, downs, [tg], [layer_out]], (0, 0, 0, 0, 1, 0, 0, 0))
    vecs, ubg = unpack(tiny, 1, part)
    t = [vecs[i] for i in range(8)]
    return (layer_out, tg, gq, gk, gv, go, gu, gd, t[0], t[1], t[2], ubg[0], t[3], t[4], t[5], t[6], t[7])


def solution(mesh):
    mat = P("dp", None)
    vec = P("dp")
    return jax.shard_map(
        local,
        mesh=mesh,
        in_specs=(mat, mat, P(), P()) + (mat,) * 6 + (vec,) * 9,
        out_specs=(mat,) * 8 + (vec,) * 9,
        check_vma=False,
    )
```

```python
import functools

import jax
import jax.numpy as jnp
from jax import lax
from jax.experimental import pallas as pl
from jax.experimental.pallas import tpu as pltpu
from jax.sharding import PartitionSpec as P

HD = 64
GRAN = 128
HALO = 384
EPS = 1e-12
F32 = jnp.float32
BF16 = jnp.bfloat16
NT = (((1,), (1,)), ((), ()))
MESH = pl.DeviceIdType.MESH
ANY = pl.BlockSpec(memory_space=pl.ANY)


def params(limit=56):
    return pltpu.CompilerParams(vmem_limit_bytes=limit << 20)


def whole(shape):
    return pl.BlockSpec(shape, lambda *_: (0,) * len(shape))


def dot(a, b):
    return jnp.dot(a, b, preferred_element_type=F32)


def dot_nt(a, b):
    return lax.dot_general(a, b, NT, preferred_element_type=F32)


def cost(flops, nbytes, trans=0):
    return pl.CostEstimate(flops=flops, bytes_accessed=nbytes, transcendentals=trans)


LANES = 512
TOGETHER = {1: 4, 2: 2, 3: 1, 4: 1}


def sequences(tab, blocks, fn):
    def one(b, c):
        n = tab[1, b]
        s0 = tab[0, b]
        for nn in range(1, 5):
            @pl.when(n == nn)
            def _():
                rows = pl.ds(pl.multiple_of(s0 * GRAN, GRAN), nn * GRAN)
                per = TOGETHER[nn]

                def group(i, c):
                    pairs = [i * per + j for j in range(per)]
                    fn(rows, [(pl.ds(pl.multiple_of(p * 2 * HD, 2 * HD), 2 * HD), 2 * p) for p in pairs])
                    return c

                lax.fori_loop(0, LANES // (2 * HD) // per, group, 0)
        return c

    lax.fori_loop(0, blocks, one, 0)


def masks(shape):
    low = lax.broadcasted_iota(jnp.int32, shape, 1) < HD
    return low, ~low


def eighth(x):
    return x * jnp.asarray(0.125, BF16)


def attn_bwd_kernel(tab, q_ref, k_ref, v_ref, ll, lo, lr, gl, go, gr, dq_o, dk_o, dv_o, sums, lse_ref, g_s, dq_s, dk_s, dv_s):
    rows_own = go.shape[0]
    lse_ref[:, pl.ds(0, HALO)] = ll[...]
    lse_ref[:, pl.ds(HALO, rows_own)] = lo[...]
    lse_ref[:, pl.ds(HALO + rows_own, HALO)] = lr[...]
    g_s[pl.ds(0, HALO), :] = gl[...]
    g_s[pl.ds(HALO, rows_own), :] = go[...]
    g_s[pl.ds(HALO + rows_own, HALO), :] = gr[...]

    def work(rows, pairs):
        mine = masks((rows.size, 2 * HD))
        qs, gs, p, dp = [], [], [], []
        for c, h in pairs:
            q, k, v, g = eighth(q_ref[rows, c]), k_ref[rows, c], v_ref[rows, c], g_s[rows, c]
            zero = jnp.zeros_like(q)
            for j, m in enumerate(mine):
                st = dot_nt(k, jnp.where(m, q, zero))
                p.append(jnp.exp(st - lse_ref[pl.ds(h + j, 1), rows]))
                dp.append(dot_nt(v, jnp.where(m, g, zero)))
            qs.append(q)
            gs.append(g)
        delta = [jnp.sum(a * b, axis=0, keepdims=True) for a, b in zip(p, dp)]
        ds = [(a * (b - d)).astype(BF16) for a, b, d in zip(p, dp, delta)]
        for i, (c, h) in enumerate(pairs):
            kt = eighth(k_ref[rows, c]).T
            dq = [dot(kt[j * HD:(j + 1) * HD, :], ds[2 * i + j]) for j in range(2)]
            dk = [dot(ds[2 * i + j], qs[i]) for j in range(2)]
            dv = [dot(p[2 * i + j].astype(BF16), gs[i]) for j in range(2)]
            dq_s[rows, c] = jnp.concatenate(dq, axis=0).T.astype(BF16)
            dk_s[rows, c] = jnp.where(mine[0], dk[0], dk[1]).astype(BF16)
            dv_s[rows, c] = jnp.where(mine[0], dv[0], dv[1]).astype(BF16)

    sequences(tab, rows_own // GRAN, work)
    own = pl.ds(HALO, rows_own)
    dq_o[...] = dq_s[own, :]
    dk_o[...] = dk_s[own, :]
    dv_o[...] = dv_s[own, :]
    sums[0:1, :] = jnp.sum(dq_o[...].astype(F32), axis=0, keepdims=True)
    sums[1:2, :] = jnp.sum(dv_o[...].astype(F32), axis=0, keepdims=True)


def attn_bwd_call(tab, q, k, v, ll, lse, lr, gl, go, gr):
    win, d = q.shape
    rows = go.shape[0]
    spec = pl.BlockSpec((win, LANES), lambda h, t: (0, h))
    own = pl.BlockSpec((rows, LANES), lambda h, t: (0, h))
    halo = pl.BlockSpec((HALO, LANES), lambda h, t: (0, h))
    out = jax.ShapeDtypeStruct((rows, d), BF16)
    return pl.pallas_call(
        attn_bwd_kernel,
        grid_spec=pltpu.PrefetchScalarGridSpec(
            num_scalar_prefetch=1,
            grid=(d // LANES,),
            in_specs=[spec] * 3 + [pl.BlockSpec((LANES // HD, a.shape[1]), lambda h, t: (h, 0)) for a in (ll, lse, lr)] + [halo, own, halo],
            out_specs=[own] * 3 + [pl.BlockSpec((8, LANES), lambda h, t: (0, h))],
            scratch_shapes=[pltpu.VMEM((LANES // HD, win), F32)] + [pltpu.VMEM((win, LANES), BF16)] * 4,
        ),
        out_shape=[out] * 3 + [jax.ShapeDtypeStruct((8, d), F32)],
        compiler_params=params(),
        cost_estimate=cost(20 * rows * 512 * d, 14 * win * d, rows * 512 * 16),
        name="attn_bwd",
    )(tab, q, k, v, ll, lse, lr, gl, go, gr)


def norm_stats(z):
    cen = z - jnp.mean(z, axis=-1, keepdims=True)
    r = lax.rsqrt(jnp.mean(cen * cen, axis=-1, keepdims=True) + EPS)
    return cen * r, r


def norm_back(e, n, r):
    return r * (e - jnp.mean(e, axis=-1, keepdims=True) - n * jnp.mean(e * n, axis=-1, keepdims=True))


RC = 256
TF = 512
TC = 256


def chunks(rows, fn):
    def step(i, c):
        fn(pl.ds(pl.multiple_of(i * RC, RC), RC))
        return c

    lax.fori_loop(0, rows // RC, step, 0)


def clip(t, first, count):
    return jnp.clip(t - first, 0, count - 1)


def lanes(t, size):
    return pl.ds(pl.multiple_of(t * size, size), size)


def colsum(v):
    return jnp.sum(v, axis=0, keepdims=True)


def gelu_parts(u):
    phi = 0.5 * (1.0 + lax.erf(u * (0.5 ** 0.5)))
    return u * phi, phi + u * (0.3989422804014327 * jnp.exp(-0.5 * u * u))


def single(shape):
    return pl.BlockSpec(shape, lambda *_: (0,) * len(shape), pipeline_mode=pl.Buffered(1))


def grid_of(n):
    chips = n // 2
    return {16: (4, 2, 2), 64: (4, 4, 4)}.get(chips, (chips, 1, 1))


class Place:
    def __init__(self, n):
        self.n = n
        self.size = grid_of(n)
        me = lax.axis_index("dp")
        nz, ny, nx = self.size
        self.me = me
        self.c = lax.rem(me, 2)
        self.x = lax.rem(me // 2, nx)
        self.y = lax.rem(me // (2 * nx), ny)
        self.z = me // (2 * nx * ny)

    def at(self, axis, k):
        nz, ny, nx = self.size
        z, y, x, c = self.z, self.y, self.x, self.c
        if axis == "z":
            z = lax.rem(z + k, nz)
        elif axis == "y":
            y = lax.rem(y + k, ny)
        elif axis == "x":
            x = lax.rem(x + k, nx)
        else:
            c = lax.rem(c + k, 2)
        pos = {"z": z, "y": y, "x": x, "c": c}[axis]
        return ((z * ny + y) * nx + x) * 2 + c, pos

    def steps(self, axis):
        nz, ny, nx = self.size
        return range(1, {"z": nz, "y": ny, "x": nx, "c": 2}[axis])

    def peers(self):
        return [self.at(a, k)[0] for a in "zyxc" for k in self.steps(a)]


def enter(peers):
    sem = pltpu.get_barrier_semaphore()
    for p in peers:
        pl.semaphore_signal(sem, inc=1, device_id=(p,), device_id_type=MESH)
    pl.semaphore_wait(sem, len(peers))


def gather_slots(n):
    nz, ny, nx = grid_of(n)
    return (nz - 1) + 2 * (ny - 1) + 2 * (nx - 1) + 1


class Gather:
    def __init__(self, place, src, dst, rows, cols, ssem, rsem, lsem, index, to=None):
        self.p, self.index = place, index
        self.src, self.dst, self.rows, self.cols = src, dst, rows, cols
        self.ssem, self.rsem, self.lsem = ssem, rsem, lsem
        p = place
        r0, nr = rows
        c0, nc = cols
        rs = pl.ds(r0, nr)
        to = c0 if to is None else to
        mine_cols = pl.ds(c0, nc)
        full = pl.ds(to, nc)
        halves = (pl.ds(to, nc // 2), pl.ds(to + nc // 2, nc // 2))
        self.local = pltpu.make_async_copy(src.at[rs, mine_cols], dst.at[p.z, p.y, p.x, p.c, rs, full], lsem.at[index])
        slot = 0

        def copy(s, d, dev):
            nonlocal slot
            cp = pltpu.make_async_remote_copy(src_ref=s, dst_ref=d, send_sem=ssem.at[index, slot], recv_sem=rsem.at[index, slot],
                                              device_id=(dev,), device_id_type=MESH)
            slot += 1
            return cp

        mine = dst.at[p.z, p.y, p.x, p.c, rs, full]
        self.ph = [[], [], [], []]
        for k in p.steps("z"):
            self.ph[0].append(copy(src.at[rs, mine_cols], mine, p.at("z", k)[0]))
        for h, axis in ((0, "y"), (1, "x")):
            s = dst.at[:, p.y, p.x, p.c, rs, halves[h]]
            for k in p.steps(axis):
                self.ph[1].append(copy(s, s, p.at(axis, k)[0]))
        for h, axis in ((0, "x"), (1, "y")):
            s = dst.at[:, :, p.x, p.c, rs, halves[0]] if h == 0 else dst.at[:, p.y, :, p.c, rs, halves[1]]
            for k in p.steps(axis):
                self.ph[2].append(copy(s, s, p.at(axis, k)[0]))
        s = dst.at[:, :, :, p.c, rs, full]
        self.ph[3].append(copy(s, s, p.at("c", 1)[0]))

    def start(self, i):
        if i == 0:
            self.local.start()
        for cp in self.ph[i]:
            cp.start()

    def wait(self, i):
        if i == 0:
            self.local.wait()
        for cp in self.ph[i]:
            cp.wait_recv()

    def sent(self):
        for ph in self.ph:
            for cp in ph:
                cp.wait_send()


def gather_go(g, ph):
    if ph > 0:
        g.wait(ph - 1)
    if ph < 4:
        g.start(ph)


def reduce_slots(n):
    nz, ny, nx = grid_of(n)
    return (nz - 1) + 2 * (ny - 1) + 2 * (nx - 1) + 1


def reduce_buffers(n, r, cols, dtype):
    nz, ny, nx = grid_of(n)
    h = cols // 2
    return [pltpu.VMEM((nz, ny, nx, r, cols), dtype),
            pltpu.VMEM((max(nx - 1, 1), nz, ny, r, h), dtype), pltpu.VMEM((max(ny - 1, 1), nz, nx, r, h), dtype),
            pltpu.VMEM((max(ny - 1, 1), nz, r, h), dtype), pltpu.VMEM((max(nx - 1, 1), nz, r, h), dtype),
            pltpu.VMEM((max(nz - 1, 1), r, cols), dtype), pltpu.VMEM((nz, r, cols), dtype), pltpu.VMEM((r, cols), F32)]


class Reduce:
    def __init__(self, place, src, own, bufs, out, ssem, rsem, lsem, index):
        self.p, self.src, self.own, self.bufs = place, src, own, bufs
        p = place
        self.h = bufs[1].shape[-1]
        self.ca, self.cb = pl.ds(0, self.h), pl.ds(self.h, self.h)
        if own is not None:
            self.get = pltpu.make_async_copy(src.at[:, :, :, p.c], own, lsem.at[index, 0])
        self.put = pltpu.make_async_copy(bufs[7], out, lsem.at[index, 1])
        slot = 0

        def copy(s, d, dev):
            nonlocal slot
            cp = pltpu.make_async_remote_copy(src_ref=s, dst_ref=d, send_sem=ssem.at[index, slot], recv_sem=rsem.at[index, slot],
                                              device_id=(dev,), device_id_type=MESH)
            slot += 1
            return cp

        self.ph = [[], [], [], []]
        dev, oc = p.at("c", 1)
        self.ph[0].append(copy(src.at[:, :, :, oc], bufs[0], dev))
        for k in p.steps("x"):
            dev, o = p.at("x", k)
            self.ph[1].append(copy(bufs[0].at[:, :, o, :, self.ca], bufs[1].at[k - 1], dev))
        for k in p.steps("y"):
            dev, o = p.at("y", k)
            self.ph[1].append(copy(bufs[0].at[:, o, :, :, self.cb], bufs[2].at[k - 1], dev))
        for k in p.steps("y"):
            dev, o = p.at("y", k)
            self.ph[2].append(copy(bufs[1].at[0, :, o], bufs[3].at[k - 1], dev))
        for k in p.steps("x"):
            dev, o = p.at("x", k)
            self.ph[2].append(copy(bufs[2].at[0, :, o], bufs[4].at[k - 1], dev))
        for k in p.steps("z"):
            dev, o = p.at("z", k)
            self.ph[3].append(copy(bufs[6].at[o], bufs[5].at[k - 1], dev))

    def go(self, i):
        if i == 0:
            self.ph[0][0].start()
            if self.own is not None:
                self.get.start()
            return
        p, bufs = self.p, self.bufs
        nz, ny, nx = p.size
        if i == 5:
            for cp in self.ph[1]:
                cp.start()
            return
        for cp in self.ph[i - 1]:
            cp.wait_recv()
        if i == 1:
            self.ph[0][0].wait_send()
            if self.own is not None:
                self.get.wait()

            def add(z, c):
                mine = self.own[z] if self.own is not None else self.src[z, :, :, pl.ds(p.c, 1)][:, :, 0]
                bufs[0][z] = mine + bufs[0][z]
                return c

            lax.fori_loop(0, nz, add, 0)
            return
        elif i == 2:
            def add(z, c):
                a = bufs[0][z, :, pl.ds(p.x, 1), :, self.ca][:, 0]
                for k in range(nx - 1):
                    a += bufs[1][k, z]
                bufs[1][0, z] = a
                b = bufs[0][z, pl.ds(p.y, 1), :, :, self.cb][0]
                for k in range(ny - 1):
                    b += bufs[2][k, z]
                bufs[2][0, z] = b
                return c

            lax.fori_loop(0, nz, add, 0)
        elif i == 3:
            a = bufs[1][0, :, pl.ds(p.y, 1)][:, 0]
            for k in range(ny - 1):
                a += bufs[3][k]
            bufs[6][:, :, self.ca] = a
            b = bufs[2][0, :, pl.ds(p.x, 1)][:, 0]
            for k in range(nx - 1):
                b += bufs[4][k]
            bufs[6][:, :, self.cb] = b
        else:
            a = bufs[6][pl.ds(p.z, 1)].astype(F32)[0]
            for k in range(nz - 1):
                a += bufs[5][k].astype(F32)
            bufs[7][...] = a
            self.put.start()
            return
        for cp in self.ph[i]:
            cp.start()

    def finish(self):
        self.put.wait()
        for ph in self.ph[1:]:
            for cp in ph:
                cp.wait_send()


def run_at(t, events):
    for step in sorted({e[0] for e in events}):
        @pl.when(t == step)
        def _():
            for e in events:
                if e[0] == step:
                    e[1](*e[2:])


FIRST_PLAN = (
    (0, 0, 0), (0, 1, 0), (0, 0, 1), (0, 1, 1), (0, 4, 0), (0, 0, 2), (0, 2, 0), (0, 1, 2),
    (0, 4, 1), (0, 0, 3), (0, 1, 3), (0, 3, 0), (0, 2, 1), (0, 4, 2), (0, 1, 4), (0, 0, 4),
    (2, 3, 1), (2, 2, 2), (2, 6, 0), (3, 6, 1), (3, 4, 3), (3, 5, 0), (3, 3, 2), (4, 2, 3),
    (4, 5, 1), (4, 6, 2), (4, 2, 4), (5, 4, 4), (6, 5, 2), (7, 3, 3), (8, 6, 3), (8, 3, 4),
    (10, 5, 3), (12, 6, 4), (12, 5, 4),
)
UPS_FIRST = 2
ZERO_ROW, OB, DB, FG, FS, SG, SS, UB = 1, 3, 4, 5, 6, 7, 8, 9


def first_kernel(n, nc, ps, qs, ks, vs, os, us, xs, wq, wk, wv, wo, wu, vec, q, k, v,
                 x, pk, w3, y3, ssem, rsem, lsem, hs, hr, xsem, osem):
    t = pl.program_id(0)
    p = Place(n)
    rows, d = xs.shape
    r = qs.shape[0]
    right, left = lax.rem(p.me + 1, n), lax.rem(p.me + n - 1, n)
    edges = [pltpu.make_async_remote_copy(src_ref=xs.at[pl.ds(rows - HALO, HALO), :], dst_ref=x.at[pl.ds(0, HALO), :], send_sem=hs.at[0],
                                          recv_sem=hr.at[0], device_id=(right,), device_id_type=MESH),
             pltpu.make_async_remote_copy(src_ref=xs.at[pl.ds(0, HALO), :], dst_ref=x.at[pl.ds(HALO + rows, HALO), :], send_sem=hs.at[1],
                                          recv_sem=hr.at[1], device_id=(left,), device_id_type=MESH)]
    mine = pltpu.make_async_copy(xs, x.at[pl.ds(HALO, rows), :], xsem)
    plan = [(ps, pk, 0), (qs, w3.at[0], 0), (ks, w3.at[1], 0), (vs, w3.at[2], 0), (os, wo, 0)] + [(us, wu, j * d) for j in range(UPS_FIRST)]
    g = [Gather(p, a, b, (0, a.shape[0]), (c, d), ssem, rsem, lsem, i) for i, (a, b, c) in enumerate(plan)]
    weights = [pltpu.make_async_copy(w3.at[i], o, osem.at[i]) for i, o in enumerate((wq, wk, wv))]
    results = [pltpu.make_async_copy(y3.at[i], o, osem.at[3 + i]) for i, o in enumerate((q, k, v))]

    def vectors():
        vec[...] = jnp.sum(pk[...].astype(F32).reshape(n, pk.shape[-2], d), axis=0)

    @pl.when(t == 0)
    def _():
        enter(p.peers() + [left, right])

    @pl.when((t > 0) & (t <= 3 * nc))
    def _():
        i = (t - 1) // nc
        c = lanes(lax.rem(t - 1, nc), TC)
        y = dot(x[...], w3[pl.ds(i, 1), ..., c].reshape(d, TC)) + vec[pl.ds(i, 1), c]
        y3[pl.ds(i, 1), :, c] = y.astype(BF16)[None]

    events = []
    for step, i, ph in FIRST_PLAN:
        events.append((step, gather_go, g[i], ph))
        if i == 0 and ph == 0:
            events += [(0, mine.start)] + [(0, c.start) for c in edges]
        if ph == 4 and i == 0:
            events.append((step, vectors))
        if ph == 4 and 1 <= i <= 3:
            events.append((step, weights[i - 1].start))
    events += [(0, mine.wait)] + [(0, c.wait_recv) for c in edges]
    events += [((i + 1) * nc, c.start) for i, c in enumerate(results)]
    last = 3 * nc
    events += [(last, c.sent) for c in g] + [(last, c.wait_send) for c in edges] + [(last, c.wait) for c in weights + results]
    run_at(t, events)


def first_call(n, packed, wq, wk, wv, wo, wu, x):
    rows, d = x.shape
    win = rows + 2 * HALO
    nc = d // TC
    r = wq.shape[0]
    z = grid_of(n) + (2,)
    count = 5 + UPS_FIRST
    k = gather_slots(n)
    mat = jax.ShapeDtypeStruct(z + (r, d), BF16)
    out = jax.ShapeDtypeStruct((win, d), BF16)
    res = pl.pallas_call(
        functools.partial(first_kernel, n, nc),
        grid=(3 * nc + 1,),
        in_specs=[ANY] * 7,
        out_specs=[ANY] * 5 + [single(packed.shape)] + [ANY] * 3,
        out_shape=[mat] * 4 + [jax.ShapeDtypeStruct(z + (r, UPS_FIRST * d), BF16), jax.ShapeDtypeStruct(packed.shape, F32)] + [out] * 3,
        scratch_shapes=[pltpu.VMEM((win, d), BF16), pltpu.VMEM(z + packed.shape, BF16), pltpu.VMEM((3,) + z + (r, d), BF16),
                        pltpu.VMEM((3, win, d), BF16), pltpu.SemaphoreType.DMA((count, k)), pltpu.SemaphoreType.DMA((count, k)),
                        pltpu.SemaphoreType.DMA((count,)), pltpu.SemaphoreType.DMA((2,)), pltpu.SemaphoreType.DMA((2,)),
                        pltpu.SemaphoreType.DMA, pltpu.SemaphoreType.DMA((6,))],
        compiler_params=pltpu.CompilerParams(collective_id=1, has_side_effects=True, vmem_limit_bytes=56 << 20),
        cost_estimate=cost(6 * win * d * d, 2 * (4 * win * d + 3 * d * d)),
        name="first",
    )(packed, wq, wk, wv, wo, wu, x)
    ws = [w.reshape((-1, w.shape[-1])) for w in res[:5]]
    return ws + list(res[5:])


DOWN_PLAN = (
    (0, 2, 0), (3, 2, 1), (3, 0, 0), (4, 2, 2), (4, 5, 0), (5, 3, 0), (7, 0, 1), (10, 0, 2),
    (12, 1, 0), (12, 5, 1), (15, 3, 1), (16, 4, 0), (17, 1, 1), (17, 2, 3), (17, 0, 3), (18, 3, 2),
    (19, 1, 2), (20, 0, 4), (20, 4, 1), (21, 5, 2), (21, 3, 3), (23, 4, 2), (24, 3, 4), (24, 1, 3),
    (25, 5, 3), (25, 1, 4), (26, 2, 4), (26, 4, 3), (26, 5, 4), (27, 4, 4),
)


AG = 256
MASKED = -1e30


def window(ref, b, c, late):
    x = ref[pl.ds(pl.multiple_of(b * GRAN, GRAN), 4 * GRAN), c]
    for i, at in enumerate(late):
        y = ref[pl.ds(pl.multiple_of((b + i + 1) * GRAN, GRAN), 4 * GRAN), c]
        x = jnp.where(at, y, x)
    return x


def attend(t, tab, q_ref, k_ref, v_ref, ctx, lse):
    subs = ctx.shape[0] // GRAN // 2
    group, sub = t // subs, lax.rem(t, subs)
    units = []
    for j in range(2):
        b = sub * 2 + j
        late = [tab[0, b] == b + i for i in range(1, 4)]
        own = pl.ds(pl.multiple_of(HALO + b * GRAN, GRAN), GRAN)
        inside = lax.broadcasted_iota(jnp.int32, (4 * GRAN, 2 * GRAN), 0) < tab[2, b] * GRAN
        for i in range(AG // (2 * HD)):
            c = slice(i * 2 * HD, (i + 1) * 2 * HD)
            q = eighth(q_ref[own, c])
            zero = jnp.zeros_like(q)
            both = jnp.concatenate([jnp.where(m, q, zero) for m in masks(q.shape)], axis=0)
            k, v = window(k_ref, b, c, late), window(v_ref, b, c, late)
            units.append((b, i, jnp.where(inside, dot_nt(k, both), MASKED), v))
    top = [jnp.max(u[2], axis=0, keepdims=True) for u in units]
    e = [jnp.exp(u[2] - m) for u, m in zip(units, top)]
    total = [jnp.sum(x, axis=0, keepdims=True) for x in e]
    logs = []
    for (b, i, _, v), m, x, s in zip(units, top, e, total):
        y = dot(v.T, x.astype(BF16)) * (1.0 / s)
        logs.append((b, 2 * i, m + jnp.log(s)))
        y = jnp.concatenate([y[:HD, :GRAN], y[HD:, GRAN:]], axis=0)
        rows = pl.ds(pl.multiple_of(b * GRAN, GRAN), GRAN)
        ctx[rows, pl.ds(pl.multiple_of(group * AG + i * 2 * HD, 2 * HD), 2 * HD)] = y.T.astype(BF16)
    for k in range(ctx.shape[1] // AG):
        @pl.when(group == k)
        def _():
            for b, h, log in logs:
                for i in range(2):
                    head = k * (AG // HD) + h + i
                    lse[head:head + 1, pl.ds(pl.multiple_of(b * GRAN, GRAN), GRAN)] = log[:, i * GRAN:(i + 1) * GRAN]


def fwd_kernel(n, na, nu, nc, tab, q_ref, k_ref, v_ref, wo, x, wu, wus, wds, g, vec,
               lse, xhat, lowt, ctxt, r1, hidt, dg, out, gs, gd, sums, wd, wu2, ctx, z, hid, low, wt, w3,
               ssem, rsem, lsem, wsem, usem):
    t = pl.program_id(0) - na
    rows, d = x.shape
    p = Place(n)
    ups = w3.shape[0]
    blocks = len(set(e[1] for e in DOWN_PLAN)) - ups
    r = wds.shape[0] // blocks
    ga = [Gather(p, wus, w3.at[i], (0, r), ((UPS_FIRST + i) * d, d), ssem, rsem, lsem, i, 0) for i in range(ups)]
    ga += [Gather(p, wds, wd, (i * r, r), (0, d), ssem, rsem, lsem, ups + i) for i in range(blocks)]
    keep = [pltpu.make_async_copy(w3.at[i], wu2.at[i], usem.at[i]) for i in range(ups)]
    fetch = [pltpu.make_async_copy(wd.at[:, :, :, :, :, pl.ds(j * TC, TC)], wt.at[j % 2], wsem.at[j]) for j in range(nc)]
    first = nc + nu

    @pl.when(t == -na)
    def _():
        enter(p.peers())

    @pl.when(t < 0)
    def _():
        attend(t + na, tab, q_ref, k_ref, v_ref, ctx, lse)

    run_at(t, [(first + j, fetch[j].wait) for j in range(nc)] + [(first + j, fetch[j + 1].start) for j in range(nc - 1)])

    @pl.when((t >= 0) & (t < nc))
    def _():
        c = lanes(t, TC)
        z[:, c] = dot(ctx[...], wo[...]) + x[:, c].astype(F32)

    @pl.when(t == nc - 1)
    def _():
        def fin(r):
            n, rr = norm_stats(z[r, :] + vec[OB:OB + 1, :])
            xhat[r, :] = n
            r1[r, :] = jnp.broadcast_to(rr, (RC, r1.shape[1]))
            v = (n * vec[FG:FG + 1, :] + vec[FS:FS + 1, :]).astype(BF16)
            low[r, :] = v
            lowt[:, r] = v.T
            ctxt[:, r] = ctx[r, :].T

        chunks(rows, fin)

    def up(weight):
        for j in range(TF // TC):
            c = slice(j * TC, (j + 1) * TC)
            tile = (t - nc) * (TF // TC) + j
            bias = vec[pl.ds(UB + tile // (d // TC), 1), lanes(lax.rem(tile, d // TC), TC)]
            h, s = gelu_parts(dot(low[...], weight(j, tile)) + bias)
            h = h.astype(BF16)
            dg[:, c] = s.astype(BF16)
            hid[:, lanes(tile, TC)] = h
            hidt[c, :] = h.T

    split = nc + UPS_FIRST * (d // TF)

    @pl.when((t >= nc) & (t < split))
    def _():
        up(lambda j, tile: wu[:, j * TC:(j + 1) * TC])

    if ups:
        @pl.when((t >= split) & (t < nc + nu))
        def _():
            up(lambda j, tile: w3[pl.ds(tile // (d // TC) - UPS_FIRST, 1), ..., lanes(lax.rem(tile, d // TC), TC)].reshape(d, TC))

    @pl.when(t >= nc + nu)
    def _():
        c = lanes(t - nc - nu, TC)
        z[:, c] = dot(hid[...], wt[pl.ds(lax.rem(t - first, 2), 1)].reshape(hid.shape[1], TC))

    @pl.when(t == 2 * nc + nu - 1)
    def _():
        sums[...] = jnp.zeros_like(sums)

        def fin(r):
            v = (xhat[r, :] * vec[FG:FG + 1, :] + vec[FS:FS + 1, :]) + (z[r, :] + vec[DB:DB + 1, :])
            n, rr = norm_stats(v)
            out[r, :] = (n * vec[SG:SG + 1, :] + vec[SS:SS + 1, :]).astype(BF16)
            gv = g[r, :].astype(F32)
            sums[0:1, :] += colsum(gv * n)
            sums[1:2, :] += colsum(gv)
            grad = norm_back(gv * vec[SG:SG + 1, :], n, rr)
            gs[r, :] = grad
            low_g = grad.astype(BF16)
            gd[r, :] = low_g
            sums[2:3, :] += colsum(low_g.astype(F32))

        chunks(rows, fin)

    done = {e[1]: e[0] for e in DOWN_PLAN if e[2] == 4}
    run_at(t + na, [(e[0], gather_go, ga[e[1]], e[2]) for e in DOWN_PLAN] + [(done[i], c.start) for i, c in enumerate(keep)]
           + [(na + first - 1, c.sent) for c in ga] + [(na + first - 1, c.wait) for c in keep] + [(na + first - 1, fetch[0].start)])


def fwd_call(n, tab, q, k, v, wo, x, wu, wus, wd, g, vec):
    rows, d = x.shape
    win = q.shape[0]
    ff = wus.shape[1]
    nu, nc = ff // TF, d // TC
    z = grid_of(n) + (2,)
    blocks = ff // d
    ups = blocks - UPS_FIRST
    slots = gather_slots(n)
    count = blocks + ups
    subs = rows // GRAN // 2
    na = d // AG * subs
    split = UPS_FIRST * (d // TF)
    spec = pl.BlockSpec((win, AG), lambda t: (0, clip(t, 0, na) // subs))

    def tile(t):
        return clip(t, na + nc, nu)

    *res, down, up2 = pl.pallas_call(
        functools.partial(fwd_kernel, n, na, nu, nc),
        grid=(na + 2 * nc + nu,),
        in_specs=[pl.BlockSpec(memory_space=pltpu.SMEM), spec, spec, spec, pl.BlockSpec((d, TC), lambda t: (0, clip(t, na, nc))),
                  single(x.shape), pl.BlockSpec((d, TF), lambda t: (0, clip(t, na + nc, split))), ANY, ANY, single(g.shape), single(vec.shape)],
        out_specs=[single((d // HD, rows)), single((rows, d)), single((d, rows)), single((d, rows)), single((rows, 128)),
                   pl.BlockSpec((TF, rows), lambda t: (tile(t), 0)), pl.BlockSpec((rows, TF), lambda t: (0, tile(t))),
                   single((rows, d)), single((rows, d)), single((rows, d)), single((8, d)), ANY, ANY],
        out_shape=[jax.ShapeDtypeStruct((d // HD, rows), F32), jax.ShapeDtypeStruct((rows, d), F32), jax.ShapeDtypeStruct((d, rows), BF16),
                   jax.ShapeDtypeStruct((d, rows), BF16), jax.ShapeDtypeStruct((rows, 128), F32), jax.ShapeDtypeStruct((ff, rows), BF16),
                   jax.ShapeDtypeStruct((rows, ff), BF16), jax.ShapeDtypeStruct((rows, d), BF16),
                   jax.ShapeDtypeStruct((rows, d), F32), jax.ShapeDtypeStruct((rows, d), BF16), jax.ShapeDtypeStruct((8, d), F32),
                   jax.ShapeDtypeStruct(z + wd.shape, BF16), jax.ShapeDtypeStruct((ups,) + z + (wus.shape[0], d), BF16)],
        scratch_shapes=[pltpu.VMEM((rows, d), BF16), pltpu.VMEM((rows, d), F32), pltpu.VMEM((rows, ff), BF16), pltpu.VMEM((rows, d), BF16),
                        pltpu.VMEM((2,) + z + (wd.shape[0], TC), BF16), pltpu.VMEM((ups,) + z + (wus.shape[0], d), BF16),
                        pltpu.SemaphoreType.DMA((count, slots)), pltpu.SemaphoreType.DMA((count, slots)),
                        pltpu.SemaphoreType.DMA((count,)), pltpu.SemaphoreType.DMA((nc,)), pltpu.SemaphoreType.DMA((ups,))],
        compiler_params=pltpu.CompilerParams(collective_id=2, has_side_effects=True, vmem_limit_bytes=62 << 20),
        cost_estimate=cost(4 * rows * d * ff, 4 * d * ff + 4 * rows * ff + rows * d * 14, 2 * rows * ff),
        name="fwd",
    )(tab, q, k, v, wo, x, wu, wus, wd, g, vec)
    return res + [down.reshape(ff, d), up2.reshape(ups, d, d)]


BWD_PLAN = (
    (0, 0, 0), (1, 1, 0), (1, 0, 1), (2, 0, 5), (2, 2, 0), (2, 1, 1), (2, 1, 5), (3, 3, 0),
    (3, 2, 1), (4, 2, 5), (5, 4, 0), (5, 3, 1), (6, 3, 5), (7, 5, 0), (7, 2, 2), (7, 4, 1),
    (8, 3, 2), (8, 1, 2), (8, 5, 1), (8, 4, 5), (9, 6, 0), (9, 2, 3), (10, 6, 1), (10, 3, 3),
    (10, 0, 2), (10, 6, 5), (11, 1, 3), (12, 5, 5), (13, 4, 2), (13, 0, 3), (14, 6, 2), (17, 4, 3),
    (17, 2, 4), (17, 1, 4), (17, 5, 2), (19, 6, 3), (24, 5, 3), (24, 3, 4), (26, 0, 4), (27, 4, 4),
    (27, 6, 4), (27, 5, 4),
)
EARLY = 7


def bwd_kernel(n, nu, nc, nr, gd, lowt, hidt, dg, wd, wu, wu2, gs, xhat, r1, vec, wo, ctxt, lse,
               gsf, sums, sumu, gc, dwo, rd, ru, gl, gr, ll, lr, *rest):
    d, rows = lowt.shape
    per = d // TF
    nd = nu // per
    t = pl.program_id(0) - nd
    late = rest[:2 * nd - EARLY]
    gu, buf0, buf1, ga = rest[2 * nd - EARLY:2 * nd - EARLY + 4]
    rest = rest[2 * nd - EARLY + 4:]
    ssem, rsem, lsem, wsem, hs, hr = rest[-6:]
    p = Place(n)
    r = d // n
    bufs = (buf0, buf1)
    red = []
    for i in range(EARLY):
        out = rd.at[pl.ds(i * r, r), :] if i < nd else ru.at[:, pl.ds((i - nd) * d, d)]
        red.append(Reduce(p, bufs[i % 2], None, rest[8 * i:8 * i + 8], out, ssem, rsem, lsem, i))
    right, left = lax.rem(p.me + 1, n), lax.rem(p.me + n - 1, n)
    edges = [pltpu.make_async_remote_copy(src_ref=gc.at[pl.ds(rows - HALO, HALO), :], dst_ref=gl, send_sem=hs.at[0], recv_sem=hr.at[0],
                                          device_id=(right,), device_id_type=MESH),
             pltpu.make_async_remote_copy(src_ref=gc.at[pl.ds(0, HALO), :], dst_ref=gr, send_sem=hs.at[1], recv_sem=hr.at[1],
                                          device_id=(left,), device_id_type=MESH),
             pltpu.make_async_remote_copy(src_ref=lse.at[:, pl.ds(rows - HALO, HALO)], dst_ref=ll, send_sem=hs.at[2], recv_sem=hr.at[2],
                                          device_id=(right,), device_id_type=MESH),
             pltpu.make_async_remote_copy(src_ref=lse.at[:, pl.ds(0, HALO)], dst_ref=lr, send_sem=hs.at[3], recv_sem=hr.at[3],
                                          device_id=(left,), device_id_type=MESH)]
    last = nu + 3 * nc + nr - 1
    end = [(e[0] - nd, red[e[1]].go, e[2]) for e in BWD_PLAN]
    for i in range(EARLY, 2 * nd):
        c = pltpu.make_async_copy(bufs[i % 2], late[i - EARLY], wsem.at[i - EARLY])
        end += [(per * (i - nd + 1) - 1, c.start), (last, c.wait)]
    end += [(nu + 2 * nc + nr - 1, c.start) for c in edges] + [(last, c.wait) for c in edges]
    end += [(last, c.finish) for c in red]

    @pl.when(t == -nd)
    def _():
        enter(p.peers() + [left, right])

    for k, buf in enumerate(bufs):
        @pl.when((t < 0) & (lax.rem(t + nd, 2) == k))
        def _():
            for j in range(d // TC):
                c = slice(j * TC, (j + 1) * TC)
                buf[..., c] = dot(hidt[...].reshape(d, rows), gd[:, c]).astype(BF16).reshape(buf.shape[:-1] + (TC,))

    @pl.when((t >= 0) & (t < nu))
    def _():
        for j in range(TF // TC):
            c = slice(j * TC, (j + 1) * TC)
            g = (dot_nt(gd[...], wd[c, :]) * dg[:, c].astype(F32)).astype(BF16)
            gu[:, lanes(t * (TF // TC) + j, TC)] = g
            sumu[:, c] = colsum(g.astype(F32))

    for k, buf in enumerate(bufs):
        @pl.when((t >= 0) & (t < nu) & (lax.rem(t // per, 2) == k))
        def _():
            for j in range(TF // TC):
                c = lanes(lax.rem(t, per) * (TF // TC) + j, TC)
                buf[..., c] = dot(lowt[...], gu[:, lanes(t * (TF // TC) + j, TC)]).astype(BF16).reshape(buf.shape[:-1] + (TC,))

    @pl.when((t >= nu) & (t < nu + nc))
    def _():
        v = gs[...] + dot_nt(gu[:, :wu.shape[1]], wu[...])
        for i in range(wu2.shape[0]):
            v += dot_nt(gu[:, wu.shape[1] + i * d:wu.shape[1] + (i + 1) * d], wu2[i])
        gsf[:, lanes(t - nu, TC)] = v

    @pl.when(t == nu + nc)
    def _():
        sums[...] = jnp.zeros_like(sums)

    @pl.when((t >= nu + nc) & (t < nu + nc + nr))
    def _():
        at = lanes(t - nu - nc, RC)
        gf = gsf[at, :]
        nn = xhat[...]
        sums[0:1, :] += colsum(gf * nn)
        sums[1:2, :] += colsum(gf)
        grad = norm_back(gf * vec[FG:FG + 1, :], nn, r1[:, 0:1])
        gsf[at, :] = grad
        low_g = grad.astype(BF16)
        ga[at, :] = low_g
        sums[2:3, :] += colsum(low_g.astype(F32))

    first = nu + nc + nr

    @pl.when((t >= first) & (t < first + nc))
    def _():
        gc[:, lanes(t - first, TC)] = dot_nt(ga[...], wo[...]).astype(BF16)

    @pl.when(t >= first + nc)
    def _():
        dwo[...] = dot(ctxt[...], ga[...]).astype(BF16)

    run_at(t, end)


def bwd_call(n, gd, lowt, hidt, dg, wd, wu, wu2, gs, xhat, r1, vec, wo, ctxt, lse):
    d, rows = lowt.shape
    ff = wd.shape[0]
    nu, nc, nr = ff // TF, d // TC, rows // RC
    r = d // n
    parts = ff // d
    z = grid_of(n) + (2, r)
    chunk = jax.ShapeDtypeStruct(z + (d,), BF16)
    k = reduce_slots(n)
    late = 2 * parts - EARLY
    nd = parts
    scratch = [pltpu.VMEM((rows, ff), BF16), pltpu.VMEM(z + (d,), BF16), pltpu.VMEM(z + (d,), BF16), pltpu.VMEM((rows, d), BF16)]
    for i in range(EARLY):
        scratch += reduce_buffers(n, r, d, BF16)
    scratch += [pltpu.SemaphoreType.DMA((EARLY, k)), pltpu.SemaphoreType.DMA((EARLY, k)), pltpu.SemaphoreType.DMA((EARLY, 2)),
                pltpu.SemaphoreType.DMA((late,)), pltpu.SemaphoreType.DMA((4,)), pltpu.SemaphoreType.DMA((4,))]
    edge = jax.ShapeDtypeStruct((HALO, d), BF16)
    edge_l = jax.ShapeDtypeStruct((lse.shape[0], HALO), F32)
    first = nd + nu + nc + nr
    return pl.pallas_call(
        functools.partial(bwd_kernel, n, nu, nc, nr),
        grid=(nd + nu + 3 * nc + nr,),
        in_specs=[single(gd.shape), single(lowt.shape),
                  pl.BlockSpec((n, 1, r, rows), lambda t: (0, clip(t, 0, nd), 0, 0)),
                  pl.BlockSpec((rows, TF), lambda t: (0, clip(t, nd, nu))), pl.BlockSpec((TF, d), lambda t: (clip(t, nd, nu), 0)),
                  pl.BlockSpec((TC, wu.shape[1]), lambda t: (clip(t, nd + nu, nc), 0)),
                  pl.BlockSpec((wu2.shape[0], TC, d), lambda t: (0, clip(t, nd + nu, nc), 0)), pl.BlockSpec((rows, TC), lambda t: (0, clip(t, nd + nu, nc))),
                  pl.BlockSpec((RC, d), lambda t: (clip(t, nd + nu + nc, nr), 0)), pl.BlockSpec((RC, 128), lambda t: (clip(t, nd + nu + nc, nr), 0)),
                  single(vec.shape), pl.BlockSpec((TC, d), lambda t: (clip(t, first, nc), 0)), pl.BlockSpec((TC, rows), lambda t: (clip(t, first + nc, nc), 0)), single(lse.shape)],
        out_specs=[single((rows, d)), single((8, d)), pl.BlockSpec((1, TF), lambda t: (0, clip(t, nd, nu))), single((rows, d)),
                   pl.BlockSpec((TC, d), lambda t: (clip(t, first + nc, nc), 0))] + [ANY] * (6 + late),
        out_shape=[jax.ShapeDtypeStruct((rows, d), F32), jax.ShapeDtypeStruct((8, d), F32), jax.ShapeDtypeStruct((1, ff), F32),
                   jax.ShapeDtypeStruct((rows, d), BF16), jax.ShapeDtypeStruct((d, d), BF16),
                   jax.ShapeDtypeStruct((nd * r, d), F32), jax.ShapeDtypeStruct((r, (EARLY - nd) * d), F32), edge, edge,
                   edge_l, edge_l] + [chunk] * late,
        scratch_shapes=scratch,
        compiler_params=pltpu.CompilerParams(collective_id=3, has_side_effects=True, vmem_limit_bytes=62 << 20),
        cost_estimate=cost(8 * rows * d * ff, 8 * d * ff + 4 * rows * ff + rows * d * 18),
        name="bwd",
    )(gd, lowt, hidt.reshape(n, parts, r, rows), dg, wd, wu, wu2, gs, xhat, r1, vec, wo, ctxt, lse)


IN_PLAN = (
    (0, 1, 0), (2, 1, 1), (2, 1, 5), (2, 0, 0), (3, 2, 0), (5, 0, 1), (5, 0, 5), (7, 3, 0),
    (8, 1, 2), (8, 3, 1), (8, 3, 5), (8, 5, 0), (8, 0, 2), (8, 5, 1), (9, 5, 5), (9, 2, 1),
    (10, 1, 3), (11, 4, 0), (11, 2, 5), (11, 4, 1), (11, 0, 3), (12, 3, 2), (12, 2, 2), (13, 4, 5),
    (13, 3, 3), (13, 2, 3), (13, 1, 4), (14, 5, 2), (14, 4, 2), (15, 0, 4), (15, 3, 4), (15, 5, 3),
    (15, 4, 3), (15, 2, 4), (15, 5, 4), (15, 4, 4),
)


def in_bwd_kernel(n, nc, left, x, gsf, dq, dk, dv, wq, wk, wv, *rest):
    t = pl.program_id(0)
    srcs, rest = rest[:left + 2], rest[left + 2:]
    tg, outs, rest = rest[0], rest[1:left + 6], rest[left + 6:]
    xt, bq, bk, bv, owns, rest = rest[0], rest[1], rest[2], rest[3], rest[4:left + 6], rest[left + 6:]
    ssem, rsem, lsem = rest[-3:]
    p = Place(n)
    plan = list(zip(srcs[:-1], owns[:-1])) + [(b, None) for b in (bq, bk, bv)] + [(srcs[-1], owns[-1])]
    red = [Reduce(p, s, o, rest[8 * i:8 * i + 8], outs[i], ssem, rsem, lsem, i) for i, (s, o) in enumerate(plan)]

    @pl.when(t == 0)
    def _():
        enter(p.peers())
        xt[...] = x[...].T

    for i, (a, b) in enumerate(((dq, bq), (dk, bk), (dv, bv))):
        @pl.when((t >= i * nc) & (t < (i + 1) * nc))
        def _():
            c = lanes(t - i * nc, TC)
            b[..., c] = dot(xt[...], a[:, c]).astype(BF16).reshape(b.shape[:-1] + (TC,))

    @pl.when(t >= 3 * nc)
    def _():
        g = gsf[...] + dot_nt(dq[...], wq[...]) + dot_nt(dk[...], wk[...]) + dot_nt(dv[...], wv[...])
        tg[...] = g.astype(BF16)

    run_at(t, [(e[0], red[e[1]].go, e[2]) for e in IN_PLAN] + [(4 * nc - 1, c.finish) for c in red])


def in_bwd_call(n, x, gsf, dq, dk, dv, wq, wk, wv, late, dwo, small):
    rows, d = x.shape
    nc = d // TC
    r = d // n
    z = grid_of(n)
    col = pl.BlockSpec((rows, TC), lambda t: (0, clip(t, 3 * nc, nc)))
    wrow = pl.BlockSpec((TC, d), lambda t: (clip(t, 3 * nc, nc), 0))
    chunk = pltpu.VMEM(z + (2, r, d), BF16)
    own = pltpu.VMEM(z + (r, d), BF16)
    share = jax.ShapeDtypeStruct((r, d), F32)
    sr, sc = small.shape[0] // n, small.shape[1]
    k = reduce_slots(n)
    left = len(late)
    total = left + 5
    scratch = [pltpu.VMEM((d, rows), BF16)] + [chunk] * 3 + [own] * (left + 1) + [pltpu.VMEM(z + (sr, sc), F32)]
    for i in range(total - 1):
        scratch += reduce_buffers(n, r, d, BF16)
    scratch += reduce_buffers(n, sr, sc, F32)
    scratch += [pltpu.SemaphoreType.DMA((total, k)), pltpu.SemaphoreType.DMA((total, k)), pltpu.SemaphoreType.DMA((total, 2))]
    return pl.pallas_call(
        functools.partial(in_bwd_kernel, n, nc, left),
        grid=(4 * nc,),
        in_specs=[single((rows, d)), col] + [single((rows, d))] * 3 + [wrow] * 3 + [ANY] * (left + 2),
        out_specs=[col] + [ANY] * total,
        out_shape=[jax.ShapeDtypeStruct((rows, d), BF16)] + [share] * (left + 4) + [jax.ShapeDtypeStruct((sr, sc), F32)],
        scratch_shapes=scratch,
        compiler_params=pltpu.CompilerParams(collective_id=5, has_side_effects=True, vmem_limit_bytes=62 << 20),
        cost_estimate=cost(12 * rows * d * d, rows * d * 14 + 12 * d * d),
        name="in_bwd",
    )(x, gsf, dq, dk, dv, wq, wk, wv, *late, dwo.reshape(z + (2, r, d)), small.reshape(z + (2, sr, sc)))


def hand_on_kernel(groups, axes, *refs):
    total = sum(groups)
    at = 0
    for g, axis, out in zip(groups, axes, refs[total:]):
        start = 0
        for a in refs[at:at + g]:
            size = a.shape[axis]
            if axis == 0:
                out[start:start + size, :] = a[...]
            else:
                out[:, start:start + size] = a[...]
            start += size
        at += g


def hand_on(parts, axes):
    shapes = []
    for ps, axis in zip(parts, axes):
        shape = list(ps[0].shape)
        shape[axis] = sum(p.shape[axis] for p in ps)
        shapes.append(jax.ShapeDtypeStruct(tuple(shape), ps[0].dtype))
    return pl.pallas_call(
        functools.partial(hand_on_kernel, tuple(len(p) for p in parts), axes),
        out_shape=shapes,
        name="hand_on",
    )(*[a for p in parts for a in p])


def sequence_table(lengths, own, rows):
    ids = jnp.arange(lengths.shape[0], dtype=jnp.int32)
    starts = jnp.sum(jnp.where(ids[None, :] < ids[:, None], lengths[None, :], 0), axis=1)
    blocks = rows // GRAN
    at = own * rows + jnp.arange(blocks, dtype=jnp.int32) * GRAN
    inside = (starts[None, :] <= at[:, None]) & (at[:, None] < (starts + lengths)[None, :])
    first = jnp.sum(jnp.where(inside, starts[None, :], 0), axis=1)
    length = jnp.sum(jnp.where(inside, lengths[None, :], 0), axis=1)
    lead = (first == at) | (jnp.arange(blocks) == 0)
    return jnp.stack([(first - own * rows + HALO) // GRAN, jnp.where(lead, length // GRAN, 0), length // GRAN]).astype(jnp.int32)


def pack(values, n, rows, dtype):
    cols = [v.reshape(n, -1) for v in values]
    flat = jnp.concatenate(cols, axis=1)
    return jnp.pad(flat, ((0, 0), (0, rows * 256 - flat.shape[1]))).astype(dtype).reshape(n * rows, 256)


def unpack(packed, n, part):
    flat = packed.reshape(n, -1)
    vec = flat[:, : 8 * part].reshape(n, 8, part).transpose(1, 0, 2).reshape(8, n * part)
    return vec, flat[:, 8 * part:12 * part].reshape(1, -1)


def local(tokens, cotangent, lengths, dealing, *shards):
    n = lax.axis_size("dp")
    own = lax.axis_index("dp")
    rows, d = tokens.shape
    part = d // n
    qb, vb, ob, ub, db, fg, fs, sg, ss = shards[6:]
    mine = jnp.stack([qb, jnp.zeros_like(qb), vb, ob, db, fg, fs, sg, ss])
    mine = lax.dynamic_update_slice(jnp.zeros((UB, d), BF16), mine, (0, own * part))
    ups = lax.dynamic_update_slice(jnp.zeros((ub.shape[0] * n,), BF16), ub, (own * ub.shape[0],)).reshape(-1, d)
    packed = jnp.concatenate([mine, ups, jnp.zeros((16 - UB - ups.shape[0], d), BF16)])
    wq, wk, wv, wo, wu, vec, q, k, v = first_call(n, packed, *shards[:5], tokens)
    tab = sequence_table(lengths, own, rows)
    lse, xhat, lowt, ctxt, r1, hidt, dg, layer_out, gs, gd, sums2, wd, wu2 = fwd_call(n, tab, q, k, v, wo, tokens, wu, *shards[4:6], cotangent, vec)
    gsf, sums1, sumu, gc, dwo, rd, ru, gl, gr, ll, lr, *late = bwd_call(n, gd, lowt, hidt, dg, wd, wu, wu2, gs, xhat, r1, vec, wo, ctxt, lse)
    dq, dk, dv, sums0 = attn_bwd_call(tab, q, k, v, ll, lse, lr, gl, gc, gr)
    small = pack([sums0[0], sums0[1], sums1[2], sums2[2], sums1[0], sums1[1], sums2[0], sums2[1], sumu], n, 8, F32)
    tg, *more = in_bwd_call(n, tokens, gsf, dq, dk, dv, wq, wk, wv, late, dwo, small)
    left = len(late)
    go, gq, gk, gv, tiny = more[left:]
    gq, gk, gv, go, gu, gd, tg, layer_out = hand_on([[gq], [gk], [gv], [go], [ru] + more[:left], [rd], [tg], [layer_out]], (0, 0, 0, 0, 1, 0, 0, 0))
    vecs, ubg = unpack(tiny, 1, part)
    t = [vecs[i] for i in range(8)]
    return (layer_out, tg, gq, gk, gv, go, gu, gd, t[0], t[1], t[2], ubg[0], t[3], t[4], t[5], t[6], t[7])


def solution(mesh):
    mat = P("dp", None)
    vec = P("dp")
    return jax.shard_map(
        local,
        mesh=mesh,
        in_specs=(mat, mat, P(), P()) + (mat,) * 6 + (vec,) * 9,
        out_specs=(mat,) * 8 + (vec,) * 9,
        check_vma=False,
    )
```

```python
import functools

import jax
import jax.numpy as jnp
from jax import lax
from jax.experimental import pallas as pl
from jax.experimental.pallas import tpu as pltpu
from jax.sharding import PartitionSpec as P

HD = 64
GRAN = 128
HALO = 384
EPS = 1e-12
F32 = jnp.float32
BF16 = jnp.bfloat16
NT = (((1,), (1,)), ((), ()))
MESH = pl.DeviceIdType.MESH
ANY = pl.BlockSpec(memory_space=pl.ANY)


def params(limit=56):
    return pltpu.CompilerParams(vmem_limit_bytes=limit << 20)


def whole(shape):
    return pl.BlockSpec(shape, lambda *_: (0,) * len(shape))


def dot(a, b):
    return jnp.dot(a, b, preferred_element_type=F32)


def dot_nt(a, b):
    return lax.dot_general(a, b, NT, preferred_element_type=F32)


def cost(flops, nbytes, trans=0):
    return pl.CostEstimate(flops=flops, bytes_accessed=nbytes, transcendentals=trans)


LANES = 512
TOGETHER = {1: 4, 2: 2, 3: 1, 4: 1}


def sequences(tab, blocks, fn):
    def one(b, c):
        n = tab[1, b]
        s0 = tab[0, b]
        for nn in range(1, 5):
            @pl.when(n == nn)
            def _():
                rows = pl.ds(pl.multiple_of(s0 * GRAN, GRAN), nn * GRAN)
                per = TOGETHER[nn]

                def group(i, c):
                    pairs = [i * per + j for j in range(per)]
                    fn(rows, [(pl.ds(pl.multiple_of(p * 2 * HD, 2 * HD), 2 * HD), 2 * p) for p in pairs])
                    return c

                lax.fori_loop(0, LANES // (2 * HD) // per, group, 0)
        return c

    lax.fori_loop(0, blocks, one, 0)


def masks(shape):
    low = lax.broadcasted_iota(jnp.int32, shape, 1) < HD
    return low, ~low


def eighth(x):
    return x * jnp.asarray(0.125, BF16)


def attn_bwd_kernel(tab, q_ref, k_ref, v_ref, ll, lo, lr, gl, go, gr, dq_o, dk_o, dv_o, sums, lse_ref, g_s, dq_s, dk_s, dv_s):
    rows_own = go.shape[0]
    lse_ref[:, pl.ds(0, HALO)] = ll[...]
    lse_ref[:, pl.ds(HALO, rows_own)] = lo[...]
    lse_ref[:, pl.ds(HALO + rows_own, HALO)] = lr[...]
    g_s[pl.ds(0, HALO), :] = gl[...]
    g_s[pl.ds(HALO, rows_own), :] = go[...]
    g_s[pl.ds(HALO + rows_own, HALO), :] = gr[...]

    def work(rows, pairs):
        mine = masks((rows.size, 2 * HD))
        qs, gs, p, dp = [], [], [], []
        for c, h in pairs:
            q, k, v, g = eighth(q_ref[rows, c]), k_ref[rows, c], v_ref[rows, c], g_s[rows, c]
            zero = jnp.zeros_like(q)
            for j, m in enumerate(mine):
                st = dot_nt(k, jnp.where(m, q, zero))
                p.append(jnp.exp(st - lse_ref[pl.ds(h + j, 1), rows]))
                dp.append(dot_nt(v, jnp.where(m, g, zero)))
            qs.append(q)
            gs.append(g)
        delta = [jnp.sum(a * b, axis=0, keepdims=True) for a, b in zip(p, dp)]
        ds = [(a * (b - d)).astype(BF16) for a, b, d in zip(p, dp, delta)]
        for i, (c, h) in enumerate(pairs):
            kt = eighth(k_ref[rows, c]).T
            dq = [dot(kt[j * HD:(j + 1) * HD, :], ds[2 * i + j]) for j in range(2)]
            dk = [dot(ds[2 * i + j], qs[i]) for j in range(2)]
            dv = [dot(p[2 * i + j].astype(BF16), gs[i]) for j in range(2)]
            dq_s[rows, c] = jnp.concatenate(dq, axis=0).T.astype(BF16)
            dk_s[rows, c] = jnp.where(mine[0], dk[0], dk[1]).astype(BF16)
            dv_s[rows, c] = jnp.where(mine[0], dv[0], dv[1]).astype(BF16)

    sequences(tab, rows_own // GRAN, work)
    own = pl.ds(HALO, rows_own)
    dq_o[...] = dq_s[own, :]
    dk_o[...] = dk_s[own, :]
    dv_o[...] = dv_s[own, :]
    sums[0:1, :] = jnp.sum(dq_o[...].astype(F32), axis=0, keepdims=True)
    sums[1:2, :] = jnp.sum(dv_o[...].astype(F32), axis=0, keepdims=True)


def attn_bwd_call(tab, q, k, v, ll, lse, lr, gl, go, gr):
    win, d = q.shape
    rows = go.shape[0]
    spec = pl.BlockSpec((win, LANES), lambda h, t: (0, h))
    own = pl.BlockSpec((rows, LANES), lambda h, t: (0, h))
    halo = pl.BlockSpec((HALO, LANES), lambda h, t: (0, h))
    out = jax.ShapeDtypeStruct((rows, d), BF16)
    return pl.pallas_call(
        attn_bwd_kernel,
        grid_spec=pltpu.PrefetchScalarGridSpec(
            num_scalar_prefetch=1,
            grid=(d // LANES,),
            in_specs=[spec] * 3 + [pl.BlockSpec((LANES // HD, a.shape[1]), lambda h, t: (h, 0)) for a in (ll, lse, lr)] + [halo, own, halo],
            out_specs=[own] * 3 + [pl.BlockSpec((8, LANES), lambda h, t: (0, h))],
            scratch_shapes=[pltpu.VMEM((LANES // HD, win), F32)] + [pltpu.VMEM((win, LANES), BF16)] * 4,
        ),
        out_shape=[out] * 3 + [jax.ShapeDtypeStruct((8, d), F32)],
        compiler_params=params(),
        cost_estimate=cost(20 * rows * 512 * d, 14 * win * d, rows * 512 * 16),
        name="attn_bwd",
    )(tab, q, k, v, ll, lse, lr, gl, go, gr)


def norm_stats(z):
    cen = z - jnp.mean(z, axis=-1, keepdims=True)
    r = lax.rsqrt(jnp.mean(cen * cen, axis=-1, keepdims=True) + EPS)
    return cen * r, r


def norm_back(e, n, r):
    return r * (e - jnp.mean(e, axis=-1, keepdims=True) - n * jnp.mean(e * n, axis=-1, keepdims=True))


RC = 256
TF = 512
TC = 256


def chunks(rows, fn):
    def step(i, c):
        fn(pl.ds(pl.multiple_of(i * RC, RC), RC))
        return c

    lax.fori_loop(0, rows // RC, step, 0)


def clip(t, first, count):
    return jnp.clip(t - first, 0, count - 1)


def lanes(t, size):
    return pl.ds(pl.multiple_of(t * size, size), size)


def colsum(v):
    return jnp.sum(v, axis=0, keepdims=True)


def gelu_parts(u):
    phi = 0.5 * (1.0 + lax.erf(u * (0.5 ** 0.5)))
    return u * phi, phi + u * (0.3989422804014327 * jnp.exp(-0.5 * u * u))


def single(shape):
    return pl.BlockSpec(shape, lambda *_: (0,) * len(shape), pipeline_mode=pl.Buffered(1))


def grid_of(n):
    chips = n // 2
    return {16: (4, 2, 2), 64: (4, 4, 4)}.get(chips, (chips, 1, 1))


class Place:
    def __init__(self, n):
        self.n = n
        self.size = grid_of(n)
        me = lax.axis_index("dp")
        nz, ny, nx = self.size
        self.me = me
        self.c = lax.rem(me, 2)
        self.x = lax.rem(me // 2, nx)
        self.y = lax.rem(me // (2 * nx), ny)
        self.z = me // (2 * nx * ny)

    def at(self, axis, k):
        nz, ny, nx = self.size
        z, y, x, c = self.z, self.y, self.x, self.c
        if axis == "z":
            z = lax.rem(z + k, nz)
        elif axis == "y":
            y = lax.rem(y + k, ny)
        elif axis == "x":
            x = lax.rem(x + k, nx)
        else:
            c = lax.rem(c + k, 2)
        pos = {"z": z, "y": y, "x": x, "c": c}[axis]
        return ((z * ny + y) * nx + x) * 2 + c, pos

    def steps(self, axis):
        nz, ny, nx = self.size
        return range(1, {"z": nz, "y": ny, "x": nx, "c": 2}[axis])

    def peers(self):
        return [self.at(a, k)[0] for a in "zyxc" for k in self.steps(a)]


def enter(peers):
    sem = pltpu.get_barrier_semaphore()
    for p in peers:
        pl.semaphore_signal(sem, inc=1, device_id=(p,), device_id_type=MESH)
    pl.semaphore_wait(sem, len(peers))


def gather_slots(n):
    nz, ny, nx = grid_of(n)
    return (nz - 1) + 2 * (ny - 1) + 2 * (nx - 1) + 1


class Gather:
    def __init__(self, place, src, dst, rows, cols, ssem, rsem, lsem, index, to=None):
        self.p, self.index = place, index
        self.src, self.dst, self.rows, self.cols = src, dst, rows, cols
        self.ssem, self.rsem, self.lsem = ssem, rsem, lsem
        p = place
        r0, nr = rows
        c0, nc = cols
        rs = pl.ds(r0, nr)
        to = c0 if to is None else to
        mine_cols = pl.ds(c0, nc)
        full = pl.ds(to, nc)
        halves = (pl.ds(to, nc // 2), pl.ds(to + nc // 2, nc // 2))
        self.local = pltpu.make_async_copy(src.at[rs, mine_cols], dst.at[p.z, p.y, p.x, p.c, rs, full], lsem.at[index])
        slot = 0

        def copy(s, d, dev):
            nonlocal slot
            cp = pltpu.make_async_remote_copy(src_ref=s, dst_ref=d, send_sem=ssem.at[index, slot], recv_sem=rsem.at[index, slot],
                                              device_id=(dev,), device_id_type=MESH)
            slot += 1
            return cp

        mine = dst.at[p.z, p.y, p.x, p.c, rs, full]
        self.ph = [[], [], [], []]
        for k in p.steps("z"):
            self.ph[0].append(copy(src.at[rs, mine_cols], mine, p.at("z", k)[0]))
        for h, axis in ((0, "y"), (1, "x")):
            s = dst.at[:, p.y, p.x, p.c, rs, halves[h]]
            for k in p.steps(axis):
                self.ph[1].append(copy(s, s, p.at(axis, k)[0]))
        for h, axis in ((0, "x"), (1, "y")):
            s = dst.at[:, :, p.x, p.c, rs, halves[0]] if h == 0 else dst.at[:, p.y, :, p.c, rs, halves[1]]
            for k in p.steps(axis):
                self.ph[2].append(copy(s, s, p.at(axis, k)[0]))
        s = dst.at[:, :, :, p.c, rs, full]
        self.ph[3].append(copy(s, s, p.at("c", 1)[0]))

    def start(self, i):
        if i == 0:
            self.local.start()
        for cp in self.ph[i]:
            cp.start()

    def wait(self, i):
        if i == 0:
            self.local.wait()
        for cp in self.ph[i]:
            cp.wait_recv()

    def sent(self):
        for ph in self.ph:
            for cp in ph:
                cp.wait_send()


def gather_go(g, ph):
    if ph > 0:
        g.wait(ph - 1)
    if ph < 4:
        g.start(ph)


def reduce_slots(n):
    nz, ny, nx = grid_of(n)
    return (nz - 1) + 2 * (ny - 1) + 2 * (nx - 1) + 1


def reduce_buffers(n, r, cols, dtype):
    nz, ny, nx = grid_of(n)
    h = cols // 2
    return [pltpu.VMEM((nz, ny, nx, r, cols), dtype),
            pltpu.VMEM((max(nx - 1, 1), nz, ny, r, h), dtype), pltpu.VMEM((max(ny - 1, 1), nz, nx, r, h), dtype),
            pltpu.VMEM((max(ny - 1, 1), nz, r, h), dtype), pltpu.VMEM((max(nx - 1, 1), nz, r, h), dtype),
            pltpu.VMEM((max(nz - 1, 1), r, cols), dtype), pltpu.VMEM((nz, r, cols), dtype), pltpu.VMEM((r, cols), F32)]


class Reduce:
    def __init__(self, place, src, own, bufs, out, ssem, rsem, lsem, index):
        self.p, self.src, self.own, self.bufs = place, src, own, bufs
        p = place
        self.h = bufs[1].shape[-1]
        self.ca, self.cb = pl.ds(0, self.h), pl.ds(self.h, self.h)
        if own is not None:
            self.get = pltpu.make_async_copy(src.at[:, :, :, p.c], own, lsem.at[index, 0])
        self.put = pltpu.make_async_copy(bufs[7], out, lsem.at[index, 1])
        slot = 0

        def copy(s, d, dev):
            nonlocal slot
            cp = pltpu.make_async_remote_copy(src_ref=s, dst_ref=d, send_sem=ssem.at[index, slot], recv_sem=rsem.at[index, slot],
                                              device_id=(dev,), device_id_type=MESH)
            slot += 1
            return cp

        self.ph = [[], [], [], []]
        dev, oc = p.at("c", 1)
        self.ph[0].append(copy(src.at[:, :, :, oc], bufs[0], dev))
        for k in p.steps("x"):
            dev, o = p.at("x", k)
            self.ph[1].append(copy(bufs[0].at[:, :, o, :, self.ca], bufs[1].at[k - 1], dev))
        for k in p.steps("y"):
            dev, o = p.at("y", k)
            self.ph[1].append(copy(bufs[0].at[:, o, :, :, self.cb], bufs[2].at[k - 1], dev))
        for k in p.steps("y"):
            dev, o = p.at("y", k)
            self.ph[2].append(copy(bufs[1].at[0, :, o], bufs[3].at[k - 1], dev))
        for k in p.steps("x"):
            dev, o = p.at("x", k)
            self.ph[2].append(copy(bufs[2].at[0, :, o], bufs[4].at[k - 1], dev))
        for k in p.steps("z"):
            dev, o = p.at("z", k)
            self.ph[3].append(copy(bufs[6].at[o], bufs[5].at[k - 1], dev))

    def go(self, i):
        if i == 0:
            self.ph[0][0].start()
            if self.own is not None:
                self.get.start()
            return
        p, bufs = self.p, self.bufs
        nz, ny, nx = p.size
        if i == 5:
            for cp in self.ph[1]:
                cp.start()
            return
        for cp in self.ph[i - 1]:
            cp.wait_recv()
        if i == 1:
            self.ph[0][0].wait_send()
            if self.own is not None:
                self.get.wait()

            def add(z, c):
                mine = self.own[z] if self.own is not None else self.src[z, :, :, pl.ds(p.c, 1)][:, :, 0]
                bufs[0][z] = mine + bufs[0][z]
                return c

            lax.fori_loop(0, nz, add, 0)
            return
        elif i == 2:
            def add(z, c):
                a = bufs[0][z, :, pl.ds(p.x, 1), :, self.ca][:, 0]
                for k in range(nx - 1):
                    a += bufs[1][k, z]
                bufs[1][0, z] = a
                b = bufs[0][z, pl.ds(p.y, 1), :, :, self.cb][0]
                for k in range(ny - 1):
                    b += bufs[2][k, z]
                bufs[2][0, z] = b
                return c

            lax.fori_loop(0, nz, add, 0)
        elif i == 3:
            a = bufs[1][0, :, pl.ds(p.y, 1)][:, 0]
            for k in range(ny - 1):
                a += bufs[3][k]
            bufs[6][:, :, self.ca] = a
            b = bufs[2][0, :, pl.ds(p.x, 1)][:, 0]
            for k in range(nx - 1):
                b += bufs[4][k]
            bufs[6][:, :, self.cb] = b
        else:
            a = bufs[6][pl.ds(p.z, 1)].astype(F32)[0]
            for k in range(nz - 1):
                a += bufs[5][k].astype(F32)
            bufs[7][...] = a
            self.put.start()
            return
        for cp in self.ph[i]:
            cp.start()

    def finish(self):
        self.put.wait()
        for ph in self.ph[1:]:
            for cp in ph:
                cp.wait_send()


def run_at(t, events):
    for step in sorted({e[0] for e in events}):
        @pl.when(t == step)
        def _():
            for e in events:
                if e[0] == step:
                    e[1](*e[2:])


FIRST_PLAN = (
    (0, 0, 0), (0, 1, 0), (0, 0, 1), (0, 1, 1), (0, 4, 0), (0, 0, 2), (0, 2, 0), (0, 1, 2),
    (0, 4, 1), (0, 0, 3), (0, 1, 3), (0, 3, 0), (0, 2, 1), (0, 4, 2), (0, 1, 4), (0, 0, 4),
    (2, 3, 1), (2, 2, 2), (2, 6, 0), (3, 6, 1), (3, 4, 3), (3, 5, 0), (3, 3, 2), (4, 2, 3),
    (4, 5, 1), (4, 6, 2), (4, 2, 4), (5, 4, 4), (6, 5, 2), (7, 3, 3), (8, 6, 3), (8, 3, 4),
    (10, 5, 3), (12, 6, 4), (12, 5, 4),
)
UPS_FIRST = 2
ZERO_ROW, OB, DB, FG, FS, SG, SS, UB = 1, 3, 4, 5, 6, 7, 8, 9


def first_kernel(n, nc, ps, qs, ks, vs, os, us, xs, wq, wk, wv, wo, wu, vec, q, k, v,
                 x, pk, w3, y3, ssem, rsem, lsem, hs, hr, xsem, osem):
    t = pl.program_id(0)
    p = Place(n)
    rows, d = xs.shape
    r = qs.shape[0]
    right, left = lax.rem(p.me + 1, n), lax.rem(p.me + n - 1, n)
    edges = [pltpu.make_async_remote_copy(src_ref=xs.at[pl.ds(rows - HALO, HALO), :], dst_ref=x.at[pl.ds(0, HALO), :], send_sem=hs.at[0],
                                          recv_sem=hr.at[0], device_id=(right,), device_id_type=MESH),
             pltpu.make_async_remote_copy(src_ref=xs.at[pl.ds(0, HALO), :], dst_ref=x.at[pl.ds(HALO + rows, HALO), :], send_sem=hs.at[1],
                                          recv_sem=hr.at[1], device_id=(left,), device_id_type=MESH)]
    mine = pltpu.make_async_copy(xs, x.at[pl.ds(HALO, rows), :], xsem)
    plan = [(ps, pk, 0), (qs, w3.at[0], 0), (ks, w3.at[1], 0), (vs, w3.at[2], 0), (os, wo, 0)] + [(us, wu, j * d) for j in range(UPS_FIRST)]
    g = [Gather(p, a, b, (0, a.shape[0]), (c, d), ssem, rsem, lsem, i) for i, (a, b, c) in enumerate(plan)]
    weights = [pltpu.make_async_copy(w3.at[i], o, osem.at[i]) for i, o in enumerate((wq, wk, wv))]
    results = [pltpu.make_async_copy(y3.at[i], o, osem.at[3 + i]) for i, o in enumerate((q, k, v))]

    def vectors():
        vec[...] = jnp.sum(pk[...].astype(F32).reshape(n, pk.shape[-2], d), axis=0)

    @pl.when(t == 0)
    def _():
        enter(p.peers() + [left, right])

    @pl.when((t > 0) & (t <= 3 * nc))
    def _():
        i = (t - 1) // nc
        c = lanes(lax.rem(t - 1, nc), TC)
        y = dot(x[...], w3[pl.ds(i, 1), ..., c].reshape(d, TC)) + vec[pl.ds(i, 1), c]
        y3[pl.ds(i, 1), :, c] = y.astype(BF16)[None]

    events = []
    for step, i, ph in FIRST_PLAN:
        events.append((step, gather_go, g[i], ph))
        if i == 0 and ph == 0:
            events += [(0, mine.start)] + [(0, c.start) for c in edges]
        if ph == 4 and i == 0:
            events.append((step, vectors))
        if ph == 4 and 1 <= i <= 3:
            events.append((step, weights[i - 1].start))
    events += [(0, mine.wait)] + [(0, c.wait_recv) for c in edges]
    events += [((i + 1) * nc, c.start) for i, c in enumerate(results)]
    last = 3 * nc
    events += [(last, c.sent) for c in g] + [(last, c.wait_send) for c in edges] + [(last, c.wait) for c in weights + results]
    run_at(t, events)


def first_call(n, packed, wq, wk, wv, wo, wu, x):
    rows, d = x.shape
    win = rows + 2 * HALO
    nc = d // TC
    r = wq.shape[0]
    z = grid_of(n) + (2,)
    count = 5 + UPS_FIRST
    k = gather_slots(n)
    mat = jax.ShapeDtypeStruct(z + (r, d), BF16)
    out = jax.ShapeDtypeStruct((win, d), BF16)
    res = pl.pallas_call(
        functools.partial(first_kernel, n, nc),
        grid=(3 * nc + 1,),
        in_specs=[ANY] * 7,
        out_specs=[ANY] * 5 + [single(packed.shape)] + [ANY] * 3,
        out_shape=[mat] * 4 + [jax.ShapeDtypeStruct(z + (r, UPS_FIRST * d), BF16), jax.ShapeDtypeStruct(packed.shape, F32)] + [out] * 3,
        scratch_shapes=[pltpu.VMEM((win, d), BF16), pltpu.VMEM(z + packed.shape, BF16), pltpu.VMEM((3,) + z + (r, d), BF16),
                        pltpu.VMEM((3, win, d), BF16), pltpu.SemaphoreType.DMA((count, k)), pltpu.SemaphoreType.DMA((count, k)),
                        pltpu.SemaphoreType.DMA((count,)), pltpu.SemaphoreType.DMA((2,)), pltpu.SemaphoreType.DMA((2,)),
                        pltpu.SemaphoreType.DMA, pltpu.SemaphoreType.DMA((6,))],
        compiler_params=pltpu.CompilerParams(collective_id=1, has_side_effects=True, vmem_limit_bytes=56 << 20),
        cost_estimate=cost(6 * win * d * d, 2 * (4 * win * d + 3 * d * d)),
        name="first",
    )(packed, wq, wk, wv, wo, wu, x)
    ws = [w.reshape((-1, w.shape[-1])) for w in res[:5]]
    return ws + list(res[5:])


DOWN_PLAN = (
    (0, 2, 0), (3, 2, 1), (3, 0, 0), (4, 2, 2), (4, 5, 0), (5, 3, 0), (7, 0, 1), (10, 0, 2),
    (12, 1, 0), (12, 5, 1), (15, 3, 1), (16, 4, 0), (17, 1, 1), (17, 2, 3), (17, 0, 3), (18, 3, 2),
    (19, 1, 2), (20, 0, 4), (20, 4, 1), (21, 5, 2), (21, 3, 3), (23, 4, 2), (24, 3, 4), (24, 1, 3),
    (25, 5, 3), (25, 1, 4), (26, 2, 4), (26, 4, 3), (26, 5, 4), (27, 4, 4),
)


AG = 256
MASKED = -1e30


def window(ref, b, c, late):
    x = ref[pl.ds(pl.multiple_of(b * GRAN, GRAN), 4 * GRAN), c]
    for i, at in enumerate(late):
        y = ref[pl.ds(pl.multiple_of((b + i + 1) * GRAN, GRAN), 4 * GRAN), c]
        x = jnp.where(at, y, x)
    return x


def attend(t, tab, q_ref, k_ref, v_ref, ctx, lse):
    subs = ctx.shape[0] // GRAN // 2
    group, sub = t // subs, lax.rem(t, subs)
    units = []
    for j in range(2):
        b = sub * 2 + j
        late = [tab[0, b] == b + i for i in range(1, 4)]
        own = pl.ds(pl.multiple_of(HALO + b * GRAN, GRAN), GRAN)
        inside = lax.broadcasted_iota(jnp.int32, (4 * GRAN, 2 * GRAN), 0) < tab[2, b] * GRAN
        for i in range(AG // (2 * HD)):
            c = slice(i * 2 * HD, (i + 1) * 2 * HD)
            q = eighth(q_ref[own, c])
            zero = jnp.zeros_like(q)
            both = jnp.concatenate([jnp.where(m, q, zero) for m in masks(q.shape)], axis=0)
            k, v = window(k_ref, b, c, late), window(v_ref, b, c, late)
            units.append((b, i, jnp.where(inside, dot_nt(k, both), MASKED), v))
    top = [jnp.max(u[2], axis=0, keepdims=True) for u in units]
    e = [jnp.exp(u[2] - m) for u, m in zip(units, top)]
    total = [jnp.sum(x, axis=0, keepdims=True) for x in e]
    logs = []
    for (b, i, _, v), m, x, s in zip(units, top, e, total):
        y = dot(v.T, x.astype(BF16)) * (1.0 / s)
        logs.append((b, 2 * i, m + jnp.log(s)))
        y = jnp.concatenate([y[:HD, :GRAN], y[HD:, GRAN:]], axis=0)
        rows = pl.ds(pl.multiple_of(b * GRAN, GRAN), GRAN)
        ctx[rows, pl.ds(pl.multiple_of(group * AG + i * 2 * HD, 2 * HD), 2 * HD)] = y.T.astype(BF16)
    for k in range(ctx.shape[1] // AG):
        @pl.when(group == k)
        def _():
            for b, h, log in logs:
                for i in range(2):
                    head = k * (AG // HD) + h + i
                    lse[head:head + 1, pl.ds(pl.multiple_of(b * GRAN, GRAN), GRAN)] = log[:, i * GRAN:(i + 1) * GRAN]


def fwd_kernel(n, na, nu, nc, tab, q_ref, k_ref, v_ref, wo, x, wu, wus, wds, g, vec,
               lse, xhat, lowt, ctxt, r1, hidt, dg, out, gs, gd, sums, wd, wu2, ctx, z, hid, low, wt, w3,
               ssem, rsem, lsem, wsem, usem):
    t = pl.program_id(0) - na
    rows, d = x.shape
    p = Place(n)
    ups = w3.shape[0]
    blocks = len(set(e[1] for e in DOWN_PLAN)) - ups
    r = wds.shape[0] // blocks
    ga = [Gather(p, wus, w3.at[i], (0, r), ((UPS_FIRST + i) * d, d), ssem, rsem, lsem, i, 0) for i in range(ups)]
    ga += [Gather(p, wds, wd, (i * r, r), (0, d), ssem, rsem, lsem, ups + i) for i in range(blocks)]
    keep = [pltpu.make_async_copy(w3.at[i], wu2.at[i], usem.at[i]) for i in range(ups)]
    fetch = [pltpu.make_async_copy(wd.at[:, :, :, :, :, pl.ds(j * TC, TC)], wt.at[j % 2], wsem.at[j]) for j in range(nc)]
    first = nc + nu

    @pl.when(t == -na)
    def _():
        enter(p.peers())

    @pl.when(t < 0)
    def _():
        attend(t + na, tab, q_ref, k_ref, v_ref, ctx, lse)

    run_at(t, [(first + j, fetch[j].wait) for j in range(nc)] + [(first + j, fetch[j + 1].start) for j in range(nc - 1)])

    @pl.when((t >= 0) & (t < nc))
    def _():
        c = lanes(t, TC)
        z[:, c] = dot(ctx[...], wo[...]) + x[:, c].astype(F32)

    @pl.when(t == nc - 1)
    def _():
        def fin(r):
            n, rr = norm_stats(z[r, :] + vec[OB:OB + 1, :])
            xhat[r, :] = n
            r1[r, :] = jnp.broadcast_to(rr, (RC, r1.shape[1]))
            v = (n * vec[FG:FG + 1, :] + vec[FS:FS + 1, :]).astype(BF16)
            low[r, :] = v
            lowt[:, r] = v.T
            ctxt[:, r] = ctx[r, :].T

        chunks(rows, fin)

    def up(weight):
        for j in range(TF // TC):
            c = slice(j * TC, (j + 1) * TC)
            tile = (t - nc) * (TF // TC) + j
            bias = vec[pl.ds(UB + tile // (d // TC), 1), lanes(lax.rem(tile, d // TC), TC)]
            h, s = gelu_parts(dot(low[...], weight(j, tile)) + bias)
            h = h.astype(BF16)
            dg[:, c] = s.astype(BF16)
            hid[:, lanes(tile, TC)] = h
            hidt[c, :] = h.T

    split = nc + UPS_FIRST * (d // TF)

    @pl.when((t >= nc) & (t < split))
    def _():
        up(lambda j, tile: wu[:, j * TC:(j + 1) * TC])

    if ups:
        @pl.when((t >= split) & (t < nc + nu))
        def _():
            up(lambda j, tile: w3[pl.ds(tile // (d // TC) - UPS_FIRST, 1), ..., lanes(lax.rem(tile, d // TC), TC)].reshape(d, TC))

    @pl.when(t >= nc + nu)
    def _():
        c = lanes(t - nc - nu, TC)
        z[:, c] = dot(hid[...], wt[pl.ds(lax.rem(t - first, 2), 1)].reshape(hid.shape[1], TC))

    @pl.when(t == 2 * nc + nu - 1)
    def _():
        sums[...] = jnp.zeros_like(sums)

        def fin(r):
            v = (xhat[r, :] * vec[FG:FG + 1, :] + vec[FS:FS + 1, :]) + (z[r, :] + vec[DB:DB + 1, :])
            n, rr = norm_stats(v)
            out[r, :] = (n * vec[SG:SG + 1, :] + vec[SS:SS + 1, :]).astype(BF16)
            gv = g[r, :].astype(F32)
            sums[0:1, :] += colsum(gv * n)
            sums[1:2, :] += colsum(gv)
            grad = norm_back(gv * vec[SG:SG + 1, :], n, rr)
            gs[r, :] = grad
            low_g = grad.astype(BF16)
            gd[r, :] = low_g
            sums[2:3, :] += colsum(low_g.astype(F32))

        chunks(rows, fin)

    done = {e[1]: e[0] for e in DOWN_PLAN if e[2] == 4}
    run_at(t + na, [(e[0], gather_go, ga[e[1]], e[2]) for e in DOWN_PLAN] + [(done[i], c.start) for i, c in enumerate(keep)]
           + [(na + first - 1, c.sent) for c in ga] + [(na + first - 1, c.wait) for c in keep] + [(na + first - 1, fetch[0].start)])


def fwd_call(n, tab, q, k, v, wo, x, wu, wus, wd, g, vec):
    rows, d = x.shape
    win = q.shape[0]
    ff = wus.shape[1]
    nu, nc = ff // TF, d // TC
    z = grid_of(n) + (2,)
    blocks = ff // d
    ups = blocks - UPS_FIRST
    slots = gather_slots(n)
    count = blocks + ups
    subs = rows // GRAN // 2
    na = d // AG * subs
    split = UPS_FIRST * (d // TF)
    spec = pl.BlockSpec((win, AG), lambda t: (0, clip(t, 0, na) // subs))

    def tile(t):
        return clip(t, na + nc, nu)

    *res, down, up2 = pl.pallas_call(
        functools.partial(fwd_kernel, n, na, nu, nc),
        grid=(na + 2 * nc + nu,),
        in_specs=[pl.BlockSpec(memory_space=pltpu.SMEM), spec, spec, spec, pl.BlockSpec((d, TC), lambda t: (0, clip(t, na, nc))),
                  single(x.shape), pl.BlockSpec((d, TF), lambda t: (0, clip(t, na + nc, split))), ANY, ANY, single(g.shape), single(vec.shape)],
        out_specs=[single((d // HD, rows)), single((rows, d)), single((d, rows)), single((d, rows)), single((rows, 128)),
                   pl.BlockSpec((TF, rows), lambda t: (tile(t), 0)), pl.BlockSpec((rows, TF), lambda t: (0, tile(t))),
                   single((rows, d)), single((rows, d)), single((rows, d)), single((8, d)), ANY, ANY],
        out_shape=[jax.ShapeDtypeStruct((d // HD, rows), F32), jax.ShapeDtypeStruct((rows, d), F32), jax.ShapeDtypeStruct((d, rows), BF16),
                   jax.ShapeDtypeStruct((d, rows), BF16), jax.ShapeDtypeStruct((rows, 128), F32), jax.ShapeDtypeStruct((ff, rows), BF16),
                   jax.ShapeDtypeStruct((rows, ff), BF16), jax.ShapeDtypeStruct((rows, d), BF16),
                   jax.ShapeDtypeStruct((rows, d), F32), jax.ShapeDtypeStruct((rows, d), BF16), jax.ShapeDtypeStruct((8, d), F32),
                   jax.ShapeDtypeStruct(z + wd.shape, BF16), jax.ShapeDtypeStruct((ups,) + z + (wus.shape[0], d), BF16)],
        scratch_shapes=[pltpu.VMEM((rows, d), BF16), pltpu.VMEM((rows, d), F32), pltpu.VMEM((rows, ff), BF16), pltpu.VMEM((rows, d), BF16),
                        pltpu.VMEM((2,) + z + (wd.shape[0], TC), BF16), pltpu.VMEM((ups,) + z + (wus.shape[0], d), BF16),
                        pltpu.SemaphoreType.DMA((count, slots)), pltpu.SemaphoreType.DMA((count, slots)),
                        pltpu.SemaphoreType.DMA((count,)), pltpu.SemaphoreType.DMA((nc,)), pltpu.SemaphoreType.DMA((ups,))],
        compiler_params=pltpu.CompilerParams(collective_id=2, has_side_effects=True, vmem_limit_bytes=62 << 20),
        cost_estimate=cost(4 * rows * d * ff, 4 * d * ff + 4 * rows * ff + rows * d * 14, 2 * rows * ff),
        name="fwd",
    )(tab, q, k, v, wo, x, wu, wus, wd, g, vec)
    return res + [down.reshape(ff, d), up2.reshape(ups, d, d)]


BWD_PLAN = (
    (0, 0, 0), (1, 1, 0), (1, 0, 1), (1, 0, 5), (2, 2, 0), (2, 1, 1), (3, 3, 0), (3, 1, 5),
    (3, 2, 1), (5, 4, 0), (5, 2, 5), (5, 3, 1), (6, 3, 5), (6, 1, 2), (7, 5, 0), (7, 0, 2),
    (7, 4, 1), (8, 5, 1), (8, 2, 2), (8, 4, 5), (9, 6, 0), (10, 5, 5), (10, 2, 3), (11, 4, 2),
    (11, 0, 3), (11, 3, 2), (12, 6, 1), (12, 5, 2), (12, 1, 3), (13, 4, 3), (14, 3, 3), (14, 6, 5),
    (19, 5, 3), (20, 6, 2), (25, 3, 4), (25, 6, 3), (26, 2, 4), (26, 5, 4), (26, 4, 4), (27, 1, 4),
    (27, 0, 4), (27, 6, 4),
)
EARLY = 7


def bwd_kernel(n, nu, nc, nr, gd, lowt, hidt, dg, wd, wu, wu2, gs, xhat, r1, vec, wo, ctxt, lse,
               gsf, sums, sumu, gc, dwo, rd, ru, gl, gr, ll, lr, *rest):
    d, rows = lowt.shape
    per = d // TF
    nd = nu // per
    t = pl.program_id(0) - nd
    late = rest[:2 * nd - EARLY]
    gu, buf0, buf1, ga = rest[2 * nd - EARLY:2 * nd - EARLY + 4]
    rest = rest[2 * nd - EARLY + 4:]
    ssem, rsem, lsem, wsem, hs, hr = rest[-6:]
    p = Place(n)
    r = d // n
    bufs = (buf0, buf1)
    red = []
    for i in range(EARLY):
        out = rd.at[pl.ds(i * r, r), :] if i < nd else ru.at[:, pl.ds((i - nd) * d, d)]
        red.append(Reduce(p, bufs[i % 2], None, rest[8 * i:8 * i + 8], out, ssem, rsem, lsem, i))
    right, left = lax.rem(p.me + 1, n), lax.rem(p.me + n - 1, n)
    edges = [pltpu.make_async_remote_copy(src_ref=gc.at[pl.ds(rows - HALO, HALO), :], dst_ref=gl, send_sem=hs.at[0], recv_sem=hr.at[0],
                                          device_id=(right,), device_id_type=MESH),
             pltpu.make_async_remote_copy(src_ref=gc.at[pl.ds(0, HALO), :], dst_ref=gr, send_sem=hs.at[1], recv_sem=hr.at[1],
                                          device_id=(left,), device_id_type=MESH),
             pltpu.make_async_remote_copy(src_ref=lse.at[:, pl.ds(rows - HALO, HALO)], dst_ref=ll, send_sem=hs.at[2], recv_sem=hr.at[2],
                                          device_id=(right,), device_id_type=MESH),
             pltpu.make_async_remote_copy(src_ref=lse.at[:, pl.ds(0, HALO)], dst_ref=lr, send_sem=hs.at[3], recv_sem=hr.at[3],
                                          device_id=(left,), device_id_type=MESH)]
    last = nu + 3 * nc + nr - 1
    end = [(e[0] - nd, red[e[1]].go, e[2]) for e in BWD_PLAN]
    for i in range(EARLY, 2 * nd):
        c = pltpu.make_async_copy(bufs[i % 2], late[i - EARLY], wsem.at[i - EARLY])
        end += [(per * (i - nd + 1) - 1, c.start), (last, c.wait)]
    end += [(nu + 2 * nc + nr - 1, c.start) for c in edges] + [(last, c.wait) for c in edges]
    end += [(last, c.finish) for c in red]

    @pl.when(t == -nd)
    def _():
        enter(p.peers() + [left, right])

    for k, buf in enumerate(bufs):
        @pl.when((t < 0) & (lax.rem(t + nd, 2) == k))
        def _():
            for j in range(d // TC):
                c = slice(j * TC, (j + 1) * TC)
                buf[..., c] = dot(hidt[...].reshape(d, rows), gd[:, c]).astype(BF16).reshape(buf.shape[:-1] + (TC,))

    @pl.when((t >= 0) & (t < nu))
    def _():
        for j in range(TF // TC):
            c = slice(j * TC, (j + 1) * TC)
            g = (dot_nt(gd[...], wd[c, :]) * dg[:, c].astype(F32)).astype(BF16)
            gu[:, lanes(t * (TF // TC) + j, TC)] = g
            sumu[:, c] = colsum(g.astype(F32))

    for k, buf in enumerate(bufs):
        @pl.when((t >= 0) & (t < nu) & (lax.rem(t // per, 2) == k))
        def _():
            for j in range(TF // TC):
                c = lanes(lax.rem(t, per) * (TF // TC) + j, TC)
                buf[..., c] = dot(lowt[...], gu[:, lanes(t * (TF // TC) + j, TC)]).astype(BF16).reshape(buf.shape[:-1] + (TC,))

    @pl.when((t >= nu) & (t < nu + nc))
    def _():
        v = gs[...] + dot_nt(gu[:, :wu.shape[1]], wu[...])
        for i in range(wu2.shape[0]):
            v += dot_nt(gu[:, wu.shape[1] + i * d:wu.shape[1] + (i + 1) * d], wu2[i])
        gsf[:, lanes(t - nu, TC)] = v

    @pl.when(t == nu + nc)
    def _():
        sums[...] = jnp.zeros_like(sums)

    @pl.when((t >= nu + nc) & (t < nu + nc + nr))
    def _():
        at = lanes(t - nu - nc, RC)
        gf = gsf[at, :]
        nn = xhat[...]
        sums[0:1, :] += colsum(gf * nn)
        sums[1:2, :] += colsum(gf)
        grad = norm_back(gf * vec[FG:FG + 1, :], nn, r1[:, 0:1])
        gsf[at, :] = grad
        low_g = grad.astype(BF16)
        ga[at, :] = low_g
        sums[2:3, :] += colsum(low_g.astype(F32))

    first = nu + nc + nr

    @pl.when((t >= first) & (t < first + nc))
    def _():
        gc[:, lanes(t - first, TC)] = dot_nt(ga[...], wo[...]).astype(BF16)

    @pl.when(t >= first + nc)
    def _():
        dwo[...] = dot(ctxt[...], ga[...]).astype(BF16)

    run_at(t, end)


def bwd_call(n, gd, lowt, hidt, dg, wd, wu, wu2, gs, xhat, r1, vec, wo, ctxt, lse):
    d, rows = lowt.shape
    ff = wd.shape[0]
    nu, nc, nr = ff // TF, d // TC, rows // RC
    r = d // n
    parts = ff // d
    z = grid_of(n) + (2, r)
    chunk = jax.ShapeDtypeStruct(z + (d,), BF16)
    k = reduce_slots(n)
    late = 2 * parts - EARLY
    nd = parts
    scratch = [pltpu.VMEM((rows, ff), BF16), pltpu.VMEM(z + (d,), BF16), pltpu.VMEM(z + (d,), BF16), pltpu.VMEM((rows, d), BF16)]
    for i in range(EARLY):
        scratch += reduce_buffers(n, r, d, BF16)
    scratch += [pltpu.SemaphoreType.DMA((EARLY, k)), pltpu.SemaphoreType.DMA((EARLY, k)), pltpu.SemaphoreType.DMA((EARLY, 2)),
                pltpu.SemaphoreType.DMA((late,)), pltpu.SemaphoreType.DMA((4,)), pltpu.SemaphoreType.DMA((4,))]
    edge = jax.ShapeDtypeStruct((HALO, d), BF16)
    edge_l = jax.ShapeDtypeStruct((lse.shape[0], HALO), F32)
    first = nd + nu + nc + nr
    return pl.pallas_call(
        functools.partial(bwd_kernel, n, nu, nc, nr),
        grid=(nd + nu + 3 * nc + nr,),
        in_specs=[single(gd.shape), single(lowt.shape),
                  pl.BlockSpec((n, 1, r, rows), lambda t: (0, clip(t, 0, nd), 0, 0)),
                  pl.BlockSpec((rows, TF), lambda t: (0, clip(t, nd, nu))), pl.BlockSpec((TF, d), lambda t: (clip(t, nd, nu), 0)),
                  pl.BlockSpec((TC, wu.shape[1]), lambda t: (clip(t, nd + nu, nc), 0)),
                  pl.BlockSpec((wu2.shape[0], TC, d), lambda t: (0, clip(t, nd + nu, nc), 0)), pl.BlockSpec((rows, TC), lambda t: (0, clip(t, nd + nu, nc))),
                  pl.BlockSpec((RC, d), lambda t: (clip(t, nd + nu + nc, nr), 0)), pl.BlockSpec((RC, 128), lambda t: (clip(t, nd + nu + nc, nr), 0)),
                  single(vec.shape), pl.BlockSpec((TC, d), lambda t: (clip(t, first, nc), 0)), pl.BlockSpec((TC, rows), lambda t: (clip(t, first + nc, nc), 0)), single(lse.shape)],
        out_specs=[single((rows, d)), single((8, d)), pl.BlockSpec((1, TF), lambda t: (0, clip(t, nd, nu))), single((rows, d)),
                   pl.BlockSpec((TC, d), lambda t: (clip(t, first + nc, nc), 0))] + [ANY] * (6 + late),
        out_shape=[jax.ShapeDtypeStruct((rows, d), F32), jax.ShapeDtypeStruct((8, d), F32), jax.ShapeDtypeStruct((1, ff), F32),
                   jax.ShapeDtypeStruct((rows, d), BF16), jax.ShapeDtypeStruct((d, d), BF16),
                   jax.ShapeDtypeStruct((nd * r, d), F32), jax.ShapeDtypeStruct((r, (EARLY - nd) * d), F32), edge, edge,
                   edge_l, edge_l] + [chunk] * late,
        scratch_shapes=scratch,
        compiler_params=pltpu.CompilerParams(collective_id=3, has_side_effects=True, vmem_limit_bytes=62 << 20),
        cost_estimate=cost(8 * rows * d * ff, 8 * d * ff + 4 * rows * ff + rows * d * 18),
        name="bwd",
    )(gd, lowt, hidt.reshape(n, parts, r, rows), dg, wd, wu, wu2, gs, xhat, r1, vec, wo, ctxt, lse)


IN_PLAN = (
    (0, 1, 0), (2, 1, 1), (2, 1, 5), (2, 0, 0), (3, 2, 0), (5, 0, 1), (5, 0, 5), (7, 3, 0),
    (8, 1, 2), (8, 3, 1), (8, 3, 5), (8, 5, 0), (8, 0, 2), (8, 5, 1), (9, 5, 5), (9, 2, 1),
    (10, 1, 3), (11, 4, 0), (11, 2, 5), (11, 4, 1), (11, 0, 3), (12, 3, 2), (12, 2, 2), (13, 4, 5),
    (13, 3, 3), (13, 2, 3), (13, 1, 4), (14, 5, 2), (14, 4, 2), (15, 0, 4), (15, 3, 4), (15, 5, 3),
    (15, 4, 3), (15, 2, 4), (15, 5, 4), (15, 4, 4),
)


def in_bwd_kernel(n, nc, left, x, gsf, dq, dk, dv, wq, wk, wv, *rest):
    t = pl.program_id(0)
    srcs, rest = rest[:left + 2], rest[left + 2:]
    tg, outs, rest = rest[0], rest[1:left + 6], rest[left + 6:]
    xt, bq, bk, bv, owns, rest = rest[0], rest[1], rest[2], rest[3], rest[4:left + 6], rest[left + 6:]
    ssem, rsem, lsem = rest[-3:]
    p = Place(n)
    plan = list(zip(srcs[:-1], owns[:-1])) + [(b, None) for b in (bq, bk, bv)] + [(srcs[-1], owns[-1])]
    red = [Reduce(p, s, o, rest[8 * i:8 * i + 8], outs[i], ssem, rsem, lsem, i) for i, (s, o) in enumerate(plan)]

    @pl.when(t == 0)
    def _():
        enter(p.peers())
        xt[...] = x[...].T

    for i, (a, b) in enumerate(((dq, bq), (dk, bk), (dv, bv))):
        @pl.when((t >= i * nc) & (t < (i + 1) * nc))
        def _():
            c = lanes(t - i * nc, TC)
            b[..., c] = dot(xt[...], a[:, c]).astype(BF16).reshape(b.shape[:-1] + (TC,))

    @pl.when(t >= 3 * nc)
    def _():
        g = gsf[...] + dot_nt(dq[...], wq[...]) + dot_nt(dk[...], wk[...]) + dot_nt(dv[...], wv[...])
        tg[...] = g.astype(BF16)

    run_at(t, [(e[0], red[e[1]].go, e[2]) for e in IN_PLAN] + [(4 * nc - 1, c.finish) for c in red])


def in_bwd_call(n, x, gsf, dq, dk, dv, wq, wk, wv, late, dwo, small):
    rows, d = x.shape
    nc = d // TC
    r = d // n
    z = grid_of(n)
    col = pl.BlockSpec((rows, TC), lambda t: (0, clip(t, 3 * nc, nc)))
    wrow = pl.BlockSpec((TC, d), lambda t: (clip(t, 3 * nc, nc), 0))
    chunk = pltpu.VMEM(z + (2, r, d), BF16)
    own = pltpu.VMEM(z + (r, d), BF16)
    share = jax.ShapeDtypeStruct((r, d), F32)
    sr, sc = small.shape[0] // n, small.shape[1]
    k = reduce_slots(n)
    left = len(late)
    total = left + 5
    scratch = [pltpu.VMEM((d, rows), BF16)] + [chunk] * 3 + [own] * (left + 1) + [pltpu.VMEM(z + (sr, sc), F32)]
    for i in range(total - 1):
        scratch += reduce_buffers(n, r, d, BF16)
    scratch += reduce_buffers(n, sr, sc, F32)
    scratch += [pltpu.SemaphoreType.DMA((total, k)), pltpu.SemaphoreType.DMA((total, k)), pltpu.SemaphoreType.DMA((total, 2))]
    return pl.pallas_call(
        functools.partial(in_bwd_kernel, n, nc, left),
        grid=(4 * nc,),
        in_specs=[single((rows, d)), col] + [single((rows, d))] * 3 + [wrow] * 3 + [ANY] * (left + 2),
        out_specs=[col] + [ANY] * total,
        out_shape=[jax.ShapeDtypeStruct((rows, d), BF16)] + [share] * (left + 4) + [jax.ShapeDtypeStruct((sr, sc), F32)],
        scratch_shapes=scratch,
        compiler_params=pltpu.CompilerParams(collective_id=5, has_side_effects=True, vmem_limit_bytes=62 << 20),
        cost_estimate=cost(12 * rows * d * d, rows * d * 14 + 12 * d * d),
        name="in_bwd",
    )(x, gsf, dq, dk, dv, wq, wk, wv, *late, dwo.reshape(z + (2, r, d)), small.reshape(z + (2, sr, sc)))


def hand_on_kernel(groups, axes, *refs):
    total = sum(groups)
    at = 0
    for g, axis, out in zip(groups, axes, refs[total:]):
        start = 0
        for a in refs[at:at + g]:
            size = a.shape[axis]
            if axis == 0:
                out[start:start + size, :] = a[...]
            else:
                out[:, start:start + size] = a[...]
            start += size
        at += g


def hand_on(parts, axes):
    shapes = []
    for ps, axis in zip(parts, axes):
        shape = list(ps[0].shape)
        shape[axis] = sum(p.shape[axis] for p in ps)
        shapes.append(jax.ShapeDtypeStruct(tuple(shape), ps[0].dtype))
    return pl.pallas_call(
        functools.partial(hand_on_kernel, tuple(len(p) for p in parts), axes),
        out_shape=shapes,
        name="hand_on",
    )(*[a for p in parts for a in p])


def sequence_table(lengths, own, rows):
    ids = jnp.arange(lengths.shape[0], dtype=jnp.int32)
    starts = jnp.sum(jnp.where(ids[None, :] < ids[:, None], lengths[None, :], 0), axis=1)
    blocks = rows // GRAN
    at = own * rows + jnp.arange(blocks, dtype=jnp.int32) * GRAN
    inside = (starts[None, :] <= at[:, None]) & (at[:, None] < (starts + lengths)[None, :])
    first = jnp.sum(jnp.where(inside, starts[None, :], 0), axis=1)
    length = jnp.sum(jnp.where(inside, lengths[None, :], 0), axis=1)
    lead = (first == at) | (jnp.arange(blocks) == 0)
    return jnp.stack([(first - own * rows + HALO) // GRAN, jnp.where(lead, length // GRAN, 0), length // GRAN]).astype(jnp.int32)


def pack(values, n, rows, dtype):
    cols = [v.reshape(n, -1) for v in values]
    flat = jnp.concatenate(cols, axis=1)
    return jnp.pad(flat, ((0, 0), (0, rows * 256 - flat.shape[1]))).astype(dtype).reshape(n * rows, 256)


def unpack(packed, n, part):
    flat = packed.reshape(n, -1)
    vec = flat[:, : 8 * part].reshape(n, 8, part).transpose(1, 0, 2).reshape(8, n * part)
    return vec, flat[:, 8 * part:12 * part].reshape(1, -1)


def local(tokens, cotangent, lengths, dealing, *shards):
    n = lax.axis_size("dp")
    own = lax.axis_index("dp")
    rows, d = tokens.shape
    part = d // n
    qb, vb, ob, ub, db, fg, fs, sg, ss = shards[6:]
    mine = jnp.stack([qb, jnp.zeros_like(qb), vb, ob, db, fg, fs, sg, ss])
    mine = lax.dynamic_update_slice(jnp.zeros((UB, d), BF16), mine, (0, own * part))
    ups = lax.dynamic_update_slice(jnp.zeros((ub.shape[0] * n,), BF16), ub, (own * ub.shape[0],)).reshape(-1, d)
    packed = jnp.concatenate([mine, ups, jnp.zeros((16 - UB - ups.shape[0], d), BF16)])
    wq, wk, wv, wo, wu, vec, q, k, v = first_call(n, packed, *shards[:5], tokens)
    tab = sequence_table(lengths, own, rows)
    lse, xhat, lowt, ctxt, r1, hidt, dg, layer_out, gs, gd, sums2, wd, wu2 = fwd_call(n, tab, q, k, v, wo, tokens, wu, *shards[4:6], cotangent, vec)
    gsf, sums1, sumu, gc, dwo, rd, ru, gl, gr, ll, lr, *late = bwd_call(n, gd, lowt, hidt, dg, wd, wu, wu2, gs, xhat, r1, vec, wo, ctxt, lse)
    dq, dk, dv, sums0 = attn_bwd_call(tab, q, k, v, ll, lse, lr, gl, gc, gr)
    small = pack([sums0[0], sums0[1], sums1[2], sums2[2], sums1[0], sums1[1], sums2[0], sums2[1], sumu], n, 8, F32)
    tg, *more = in_bwd_call(n, tokens, gsf, dq, dk, dv, wq, wk, wv, late, dwo, small)
    left = len(late)
    go, gq, gk, gv, tiny = more[left:]
    gq, gk, gv, go, gu, gd, tg, layer_out = hand_on([[gq], [gk], [gv], [go], [ru] + more[:left], [rd], [tg], [layer_out]], (0, 0, 0, 0, 1, 0, 0, 0))
    vecs, ubg = unpack(tiny, 1, part)
    t = [vecs[i] for i in range(8)]
    return (layer_out, tg, gq, gk, gv, go, gu, gd, t[0], t[1], t[2], ubg[0], t[3], t[4], t[5], t[6], t[7])


def solution(mesh):
    mat = P("dp", None)
    vec = P("dp")
    return jax.shard_map(
        local,
        mesh=mesh,
        in_specs=(mat, mat, P(), P()) + (mat,) * 6 + (vec,) * 9,
        out_specs=(mat,) * 8 + (vec,) * 9,
        check_vma=False,
    )
```
